128 devices in a mesh: gx: 4 (over z), gy: 32 (over y, x, core).
Axes of the slice: x: 4, y: 4, z: 4, core: 2. Of those that a mesh axis runs over, the one named last changes fastest.
Arguments:
- velocity: float32 [3, 16, 1024, 1024], P(None, 'gx', 'gy'), may hold values from -6 to 6
- section: float32 [3, 16, 1024, 1024], P(None, 'gx', 'gy'), may hold values from -8 to 8
- diffusion: float32 [1024], replicated, may hold values from 1000 to 10000
- rhs_near: float32 [1024], P('gy'), may hold values from 0.6 to 1.2
- rhs_far: float32 [1024], P('gy'), may hold values from -0.2 to -0.05
- part_vel: float32 [3, 1048576], P(None, ('gx', 'gy')), may hold values from -6 to 6
- part_rate: float32 [1048576], P(('gx', 'gy')), may hold values from 0.5 to 5
- counts: int32 [128, 128], P(('gx', 'gy')), may hold values from 0 to 64, as said below
- cell_slot: int32 [128, 8192], P(('gx', 'gy')), may hold values from 0 to 131071
Outputs:
- velocity_new: float32 [3, 16, 1024, 1024], P(None, 'gx', 'gy')
- section_new: float32 [3, 16, 1024, 1024], P(None, 'gx', 'gy')
- part_new: float32 [3, 1048576], P(None, ('gx', 'gy'))
The draws below stay inside these ranges and needn't reach their ends.
Inputs may be any that keep to these rules, and one draw needn't show every extreme that they name: counts[d, s] is the number of live slots, from the front, of the block that device s sends to device d; in every draw one receiving device gets 64 live slots from every sender.
All inputs are finite; a program needn't handle non-finite values.
Results may differ from the reference program's by a relative error of at most 0.0003.
The reference program's roundings to bfloat16 on the way (of `velocity_bf` and `push`) count: a program that leaves them out, or rounds other values in their place, can miss the bound.
Values sent between devices are 32-bit elements; how exact they have to be, the bound alone decides.
No kernel may reach another device: no remote copies, remote signals or barrier semaphores. Data moves between devices by JAX's collectives and lax.ppermute only.
A program may use at most 128 MiB of HBM per device.

```python
import math
import jax
import jax.numpy as jnp

CX = 4
NY = 1024
CZ = 1024
SLOTS = 64
NX = 16
CY = 32
N_GX = 4
N_GY = 32
DEVICES = 128


def draw_counts(key, part):
    key_level, key_dense, key_raw, key_star = jax.random.split(key, 4)
    level_cap = jax.random.randint(key_level, (DEVICES,), 0, SLOTS + 1)
    dense_flag = jax.random.randint(key_dense, (DEVICES,), 0, 2)
    raw_count = jax.random.randint(key_raw, (DEVICES, DEVICES), 0, SLOTS + 1)
    capped = jnp.minimum(raw_count, (level_cap * dense_flag)[:, None])
    star_row = jax.random.randint(key_star, (), 0, DEVICES)
    row_ids = jnp.arange(DEVICES)[:, None]
    return jnp.where(row_ids == star_row, SLOTS, capped).astype(jnp.int32)


def draw_diffusion(key, part):
    key_amp, key_phase, key_rough = jax.random.split(jax.random.fold_in(key, 11), 3)
    rows = (jnp.arange(NY, dtype=jnp.float32) + 0.5) / NY
    amps = jax.random.uniform(key_amp, (3,), jnp.float32, -1.0, 1.0)
    phases = jax.random.uniform(key_phase, (3,), jnp.float32, 0.0, 6.2831853)
    orders = jnp.arange(1, 4, dtype=jnp.float32)
    waves = jnp.sin(jnp.pi * orders[:, None] * rows[None, :] + phases[:, None])
    smooth = (amps[0] * waves[0] + amps[1] * waves[1] + amps[2] * waves[2]) / 3.0
    rough = jax.random.uniform(key_rough, (NY,), jnp.float32, -1.0, 1.0)
    exponent = 3.5 + 0.35 * smooth + 0.15 * rough
    return jnp.exp(exponent * 2.302585093).astype(jnp.float32)


def draw_section(key, part):
    key_rough, key_level = jax.random.split(jax.random.fold_in(key, 23))
    rows = (jnp.arange(NY, dtype=jnp.float32) + 0.5) / NY
    profile = jnp.sin(jnp.pi * rows)[None, None, :, None]
    rough = jnp.clip(jax.random.normal(key_rough, (3, NX, NY, CZ), jnp.float32), -5.0, 5.0)
    level = jnp.clip(jax.random.normal(key_level, (3, NX, 1, CZ), jnp.float32), -2.5, 2.5)
    return (rough + level * profile).astype(jnp.float32)


def touch_ends(entries, rng, least, largest):
    index_at = [jax.random.randint(jax.random.fold_in(rng, axis), (), 0, length) for axis, length in enumerate(entries.shape)]
    longest = entries.shape.index(max(entries.shape))
    beside = index_at[:longest] + [(index_at[longest] + 1) % entries.shape[longest]] + index_at[longest + 1:]
    return entries.at[tuple(index_at)].set(least).at[tuple(beside)].set(largest)


def block_levels(own_key, dims, shards, least, high):
    loudness, own = 1.0, jax.random.fold_in(own_key, 6)
    for position, parts in shards:
        draws = jnp.exp(jax.random.uniform(jax.random.fold_in(own, position), (parts,), jnp.float32, least / len(shards), high / len(shards)))
        loudness = loudness * jnp.repeat(draws, dims[position] // parts).reshape([-1 if axis == position else 1 for axis in range(len(dims))])
    return loudness


def gaussian(key, extent, width, most, cuts=(), held_as=jnp.bfloat16):
    array = jax.random.normal(key, extent, jnp.float32) * width
    if len(cuts) > 0:
        array = block_levels(key, extent, cuts, -0.22, 0.18) * array
    return jnp.clip(array, min=-most, max=most).astype(held_as)


def setup_inputs(seed: int = 0) -> dict:
    key_list = jax.random.split(jax.random.key(seed), 10)
    return {
        "velocity": gaussian(key_list[0], (3, NX, NY, CZ), 1.0, 6.0, ((1, 4), (2, 32)), jnp.float32),
        "section": draw_section(jax.random.fold_in(key_list[9], 71), 0),
        "diffusion": draw_diffusion(jax.random.fold_in(key_list[9], 71), 0),
        "rhs_near": jnp.clip(0.6 + 0.6 * jax.random.uniform(key_list[3], (NY,), jnp.float32) ** block_levels(key_list[3], (NY,), ((0, 32),), -0.2, 0.2), 0.6, 1.2),
        "rhs_far": jnp.clip(-0.2 + 0.15 * jax.random.uniform(key_list[4], (NY,), jnp.float32) ** block_levels(key_list[4], (NY,), ((0, 32),), -0.2, 0.2), -0.2, -0.05),
        "part_vel": gaussian(key_list[5], (3, DEVICES * DEVICES * SLOTS), 1.0, 6.0, ((1, 128),), jnp.float32),
        "part_rate": jnp.clip(jnp.exp(math.log(5.0) - 2.3025851 * jax.random.uniform(key_list[6], (DEVICES * DEVICES * SLOTS,), jnp.float32) ** block_levels(key_list[6], (DEVICES * DEVICES * SLOTS,), ((0, 128),), -0.2, 0.2)), 0.5, 5.0),
        "counts": draw_counts(jax.random.fold_in(key_list[9], 71), 0),
        "cell_slot": touch_ends(jax.random.randint(key_list[8], (DEVICES, DEVICES * SLOTS), 0, CX * CY * CZ), jax.random.fold_in(key_list[8], 1), 0, (CX * CY * CZ) - 1).astype(jnp.int32),
    }


def reference(velocity, section, diffusion, rhs_near, rhs_far, part_vel, part_rate, counts, cell_slot):
    devices_all = N_GX * N_GY
    velocity_bf = velocity.astype(jnp.bfloat16)
    moved_vel = part_vel.reshape(3, devices_all, devices_all, SLOTS).transpose(0, 2, 1, 3).reshape(3, -1)
    moved_rate = part_rate.reshape(devices_all, devices_all, SLOTS).transpose(1, 0, 2).reshape(-1)
    slot_ids = jnp.arange(devices_all * devices_all * SLOTS, dtype=jnp.int32)
    target = slot_ids // (devices_all * SLOTS)
    source = slot_ids // SLOTS % devices_all
    within = slot_ids % SLOTS
    live = within < counts[target, source]
    cell_ids = cell_slot.reshape(-1)
    global_x = target // N_GY * CX + cell_ids // (CY * CZ)
    global_y = target % N_GY * CY + cell_ids // CZ % CY
    global_z = cell_ids % CZ
    fluid_at = velocity_bf[:, global_x, global_y, global_z].astype(jnp.float32)
    relative = fluid_at - moved_vel
    part_new = jnp.where(live[None], moved_vel + 0.2 * moved_rate[None] * relative, 0.0)
    push = jnp.where(live[None], -moved_rate[None] * relative, 0.0).astype(jnp.bfloat16)
    deposit = jnp.zeros_like(velocity).at[:, global_x, global_y, global_z].add(push.astype(velocity.dtype))

    def central(field, axis_id):
        return (8.0 * (jnp.roll(field, -1, axis_id) - jnp.roll(field, 1, axis_id)) - (jnp.roll(field, -2, axis_id) - jnp.roll(field, 2, axis_id))) / 12.0
    ddx = central(velocity, 1)
    ddz = central(velocity, 3)
    padded = jnp.pad(velocity, ((0, 0), (0, 0), (2, 2), (0, 0)))
    ddy = rhs_near[None, None, :, None] * (padded[:, :, 3:NY + 3] - padded[:, :, 1:NY + 1]) + rhs_far[None, None, :, None] * (padded[:, :, 4:] - padded[:, :, :NY])
    rhs = -(velocity[0:1] * ddx + velocity[1:2] * ddy + velocity[2:3] * ddz) + deposit
    section_new = -5.0 / 9.0 * section + 0.2 * rhs
    main_diag = 1.0 + 2.5 * diffusion
    near_coef = -4.0 / 3.0 * diffusion
    far_coef = diffusion / 12.0
    system = jnp.diag(main_diag) + jnp.diag(near_coef[1:], -1) + jnp.diag(near_coef[:-1], 1) + jnp.diag(far_coef[2:], -2) + jnp.diag(far_coef[:-2], 2)
    lines = jnp.moveaxis(15.0 / 16.0 * section_new, 2, 0).reshape(NY, -1)
    solved = jnp.linalg.solve(system, lines)
    increment = jnp.moveaxis(solved.reshape(NY, 3, NX, CZ), 0, 2)
    velocity_new = velocity + increment
    return (velocity_new, section_new, part_new)
```

```python
import jax
import jax.numpy as jnp
from jax import lax
from jax.experimental import pallas as pl
from jax.experimental.pallas import tpu as pltpu
from jax.sharding import PartitionSpec as P

TIME_STEP = 0.2
SECTION_KEEP = -5.0 / 9.0
SECTION_GAIN = 15.0 / 16.0
MAIN = 2.5
NEAR = -4.0 / 3.0
FAR = 1.0 / 12.0
SLABS = 32
ROWS = 32
CX = 4
CZ = 1024
PLANES = CX * ROWS
SLOTS = 64
PEERS = 128
TOTAL = PEERS * SLOTS
CHUNK = 1024
HIGH = lax.Precision.HIGHEST
F32 = jnp.float32
BF16 = jnp.bfloat16


def params(mib=60):
    return pltpu.CompilerParams(vmem_limit_bytes=mib * 1024 * 1024)


VMEM = pl.BlockSpec(memory_space=pltpu.MemorySpace.VMEM)
SMEM = pl.BlockSpec(memory_space=pltpu.MemorySpace.SMEM)
ANY = pl.BlockSpec(memory_space=pl.ANY)


def shaped(*shape):
    return jax.ShapeDtypeStruct(shape, F32)


def mm(a, b):
    return tuple(
        tuple(a[i][0] * b[0][j] + a[i][1] * b[1][j] for j in range(2)) for i in range(2)
    )


def add(a, b, sign=1.0):
    return tuple(tuple(a[i][j] + sign * b[i][j] for j in range(2)) for i in range(2))


def neg(a):
    return tuple(tuple(-e for e in row) for row in a)


def each(a, fn):
    return tuple(tuple(fn(e) for e in row) for row in a)


def inverse_of_one_minus(a):
    p, q, r, s = 1.0 - a[0][0], -a[0][1], -a[1][0], 1.0 - a[1][1]
    scale = 1.0 / (p * s - q * r)
    return ((s * scale, -q * scale), (-r * scale, p * scale))


def factor_kernel(place_ref, rate_ref, scale_ref, tip_ref, fix_ref, solve_ref, green_ref, wide_ref, coef_ref):
    slab = place_ref[0]
    lane8 = lax.broadcasted_iota(jnp.int32, (8, 128), 1)
    sub8 = lax.broadcasted_iota(jnp.int32, (8, 128), 0)
    lane32 = lax.broadcasted_iota(jnp.int32, (ROWS, 128), 1)
    inv_rate = 1.0 / rate_ref[...]
    wide_ref[0:ROWS] = inv_rate + MAIN
    recip, low1, low2 = [], [], []
    zero = jnp.zeros((8, 128), F32)
    for k in range(ROWS):
        main = jnp.broadcast_to(wide_ref[k : k + 1, :], (8, 128))
        if k == 0:
            low1.append(zero)
            low2.append(zero)
            recip.append(1.0 / main)
            continue
        edge = NEAR - FAR * low1[k - 1]
        one = edge * recip[k - 1]
        two = FAR * recip[k - 2] if k > 1 else zero
        low1.append(one)
        low2.append(two)
        recip.append(1.0 / (main - edge * one - FAR * two))
    ends = (0, 1, ROWS - 2, ROWS - 1)
    half = []
    for k in range(ROWS):
        unit = (sub8 == ends.index(k)).astype(F32) if k in ends else zero
        value = unit
        if k > 0:
            value = value - low1[k] * half[k - 1]
        if k > 1:
            value = value - low2[k] * half[k - 2]
        half.append(value)
    full = [None] * ROWS
    for k in reversed(range(ROWS)):
        value = half[k] * recip[k]
        if k < ROWS - 1:
            value = value - low1[k + 1] * full[k + 1]
        if k < ROWS - 2:
            value = value - low2[k + 2] * full[k + 2]
        full[k] = value

    def entry(k, i):
        return jnp.broadcast_to(full[k][i : i + 1, :], (8, 128))

    not_first = ((lane8 > 0) & (lane8 < SLABS)).astype(F32)
    not_last = (lane8 < SLABS - 1).astype(F32)

    def lower(k):
        s0, s1 = entry(k, 0), entry(k, 1)
        return (FAR * s0 * not_first, (NEAR * s0 + FAR * s1) * not_first)

    def upper(k):
        s2, s3 = entry(k, 2), entry(k, 3)
        return ((FAR * s2 + NEAR * s3) * not_last, FAR * s3 * not_last)

    low_a = (lower(ends[0]), lower(ends[1]))
    low_c = (lower(ends[2]), lower(ends[3]))
    up_b = (upper(ends[0]), upper(ends[1]))
    up_e = (upper(ends[2]), upper(ends[3]))
    a, b, c, e = low_a, up_b, low_c, up_e
    for hop in (1, 2, 4, 8, 16):
        ax, bx, cx, ex = (each(m, lambda v: pltpu.roll(v, hop, 1)) for m in (a, b, c, e))
        w = inverse_of_one_minus(mm(a, ex))
        wa_c = mm(w, mm(a, cx))
        wb = mm(w, b)
        cy_ex = mm(c, ex)
        new_e = add(e, mm(cy_ex, wb))
        new_c = neg(add(mm(c, cx), mm(cy_ex, wa_c)))
        new_a = add(ax, mm(bx, wa_c))
        new_b = neg(mm(bx, wb))
        joined = lane8 >= hop

        def pick(new, old):
            return tuple(
                tuple(jnp.where(joined, new[i][j], old[i][j]) for j in range(2)) for i in range(2)
            )

        a, b, c, e = pick(new_a, a), pick(new_b, b), pick(new_c, c), pick(new_e, e)
    q = e
    q_prev = each(q, lambda v: jnp.where(lane8 > 0, pltpu.roll(v, 1, 1), 0.0))
    z = inverse_of_one_minus(mm(low_a, q_prev))
    gain = mm(mm(low_c, q_prev), z)
    carry = add(low_c, mm(gain, low_a))
    z_low = mm(z, low_a)
    z_up = mm(z, up_b)
    for group, mats in enumerate(((carry, gain), (z, z_low), (z_up, q))):
        block = jnp.zeros((8, 128), F32)
        for n, m in enumerate(mats):
            for i in range(2):
                for j in range(2):
                    block = jnp.where(sub8 == 4 * n + 2 * i + j, m[i][j], block)
        for s in range(SLABS):
            coef_ref[s, 8 * group : 8 * group + 8, :] = jnp.broadcast_to(block[:, s : s + 1], (8, 128))

    def coef(s, n):
        def one(i, j):
            at = 4 * n + 2 * i + j
            return jnp.broadcast_to(coef_ref[s, at : at + 1, :], (8, 128))

        return tuple(tuple(one(i, j) for j in range(2)) for i in range(2))

    def at_lane(n):
        return lane8 == n

    forward = []
    prev = None
    for s in range(SLABS):
        m, g = coef(s, 0), coef(s, 1)
        now = []
        for i in range(2):
            value = jnp.where(at_lane(4 * s), g[i][0], 0.0)
            value = jnp.where(at_lane(4 * s + 1), g[i][1], value)
            value = jnp.where(at_lane(4 * s + 2 + i), 1.0, value)
            if prev is not None:
                value = value - m[i][0] * prev[0] - m[i][1] * prev[1]
            now.append(value)
        forward.append(now)
        prev = now
    for row in (0, 1, 4 * SLABS - 2, 4 * SLABS - 1):
        green_ref[row : row + 1, :] = jnp.zeros((1, 128), F32)
    after = None
    for s in reversed(range(SLABS)):
        zc, zl, zu, qc = coef(s, 2), coef(s, 3), coef(s, 4), coef(s, 5)
        now = []
        for i in range(2):
            value = jnp.where(at_lane(4 * s), zc[i][0], 0.0)
            value = jnp.where(at_lane(4 * s + 1), zc[i][1], value)
            if s > 0:
                value = value - zl[i][0] * forward[s - 1][0] - zl[i][1] * forward[s - 1][1]
            if after is not None:
                value = value - zu[i][0] * after[0] - zu[i][1] * after[1]
            now.append(value)
        if s < SLABS - 1:
            for i in range(2):
                high = forward[s][i] - qc[i][0] * after[0] - qc[i][1] * after[1]
                green_ref[4 * (s + 1) + i : 4 * (s + 1) + i + 1, :] = high[0:1]
        if s > 0:
            for i in range(2):
                green_ref[4 * (s - 1) + 2 + i : 4 * (s - 1) + 3 + i, :] = now[i][0:1]
        after = now

    for k in range(ROWS):
        wide_ref[k : k + 1, :] = low1[k][0:1]
        wide_ref[ROWS + k : ROWS + k + 1, :] = low2[k][0:1]
        wide_ref[2 * ROWS + k : 2 * ROWS + k + 1, :] = recip[k][0:1]
    own = lane32 == slab

    def own_column(v):
        return jnp.broadcast_to(jnp.sum(jnp.where(own, v, 0.0), axis=1, keepdims=True), (ROWS, 128))

    for part in range(3):
        wide_ref[part * ROWS : (part + 1) * ROWS, :] = own_column(
            wide_ref[part * ROWS : (part + 1) * ROWS, :]
        )
    scale_ref[...] = SECTION_GAIN * own_column(inv_rate)

    def wide(part, k):
        return jnp.broadcast_to(wide_ref[part * ROWS + k : part * ROWS + k + 1, :], (8, 128))

    half = []
    for k in range(ROWS):
        value = (lane8 == k).astype(F32)
        if k > 0:
            value = value - wide(0, k) * half[k - 1]
        if k > 1:
            value = value - wide(1, k) * half[k - 2]
        half.append(value)
    full = [None] * ROWS
    for k in reversed(range(ROWS)):
        value = half[k] * wide(2, k)
        if k < ROWS - 1:
            value = value - wide(0, k + 1) * full[k + 1]
        if k < ROWS - 2:
            value = value - wide(1, k + 2) * full[k + 2]
        full[k] = value
        solve_ref[k : k + 1, :] = value[0:1]
    solve = solve_ref[...]
    cols = [jnp.broadcast_to(solve[:, n : n + 1], (ROWS, 128)) for n in ends]
    for n in range(4):
        tip_ref[n] = cols[n]
    has_low = jnp.where(slab > 0, 1.0, 0.0)
    has_high = jnp.where(slab < SLABS - 1, 1.0, 0.0)
    fix_ref[0] = FAR * cols[0] * has_low
    fix_ref[1] = (NEAR * cols[0] + FAR * cols[1]) * has_low
    fix_ref[2] = (FAR * cols[2] + NEAR * cols[3]) * has_high
    fix_ref[3] = FAR * cols[3] * has_high


def factors(place, rate):
    return pl.pallas_call(
        factor_kernel,
        out_shape=(
            shaped(ROWS, 128),
            shaped(4, ROWS, 128),
            shaped(4, ROWS, 128),
            shaped(ROWS, 128),
            shaped(128, 128),
        ),
        in_specs=[SMEM, VMEM],
        out_specs=(VMEM,) * 5,
        scratch_shapes=[pltpu.VMEM((3 * ROWS, 128), F32), pltpu.VMEM((SLABS, 24, 128), F32)],
        name="factors",
    )(place, rate)


def pack_kernel(vel_ref, rate_ref, out_ref):
    left = lax.broadcasted_iota(jnp.int32, (1, 128), 1) < SLOTS
    for r in range(PEERS // 2):
        part = [vel_ref[i : i + 1, 128 * r : 128 * r + 128] for i in range(3)]
        part.append(rate_ref[0:1, 128 * r : 128 * r + 128])
        for n in range(2):
            one, two = part[2 * n], part[2 * n + 1]
            out_ref[2 * r, n : n + 1, :] = jnp.where(left, one, pltpu.roll(two, SLOTS, 1))
            out_ref[2 * r + 1, n : n + 1, :] = jnp.where(left, pltpu.roll(one, SLOTS, 1), two)


def packed(part_vel, part_rate):
    return pl.pallas_call(
        pack_kernel,
        out_shape=shaped(PEERS, 2, 128),
        in_specs=[VMEM, VMEM],
        out_specs=VMEM,
        name="pack",
    )(part_vel, part_rate)


def halves(cells):
    plane = cells >> 10
    span = cells & (CZ - 1)
    return plane, span >> 7, span & 127


def span_table(high, low):
    width = high.shape[1]
    inner = lax.broadcasted_iota(jnp.int32, (128, width), 0) == low
    inner = inner.astype(F32).astype(BF16)
    rows = []
    for t in range(8):
        flag = (high == t).astype(F32).astype(BF16)
        rows.append(inner * flag)
    return jnp.concatenate(rows, axis=0)


def gather_kernel(vel_ref, cell_ref, out_ref, bf_ref):
    @pl.when(pl.program_id(0) == 0)
    def _():
        bf_ref[...] = vel_ref[...].astype(BF16)

    plane, high, low = halves(cell_ref[...])
    table = span_table(high, low)
    at = jnp.dot(bf_ref[...], table, preferred_element_type=F32)
    mask = lax.broadcasted_iota(jnp.int32, (PLANES, CHUNK), 0) == plane
    for n in range(3):
        out_ref[n : n + 1, :] = jnp.sum(
            jnp.where(mask, at[n * PLANES : (n + 1) * PLANES], 0.0), axis=0, keepdims=True
        )


def gathered(velocity, cells):
    return pl.pallas_call(
        gather_kernel,
        grid=(TOTAL // CHUNK,),
        out_shape=shaped(3, TOTAL),
        in_specs=[
            pl.BlockSpec((3 * PLANES, CZ), lambda i: (0, 0)),
            pl.BlockSpec((1, CHUNK), lambda i: (0, i)),
        ],
        out_specs=pl.BlockSpec((3, CHUNK), lambda i: (0, i)),
        scratch_shapes=[pltpu.VMEM((3 * PLANES, CZ), BF16)],
        compiler_params=params(),
        name="gather",
    )(velocity.reshape(3 * PLANES, CZ), cells)


def deposit_kernel(moved_ref, count_ref, cell_ref, fluid_ref, part_ref, sum_ref, got_ref):
    step = pl.program_id(0)
    senders = CHUNK // SLOTS
    left = lax.broadcasted_iota(jnp.int32, (1, 128), 1) < SLOTS
    lane = lax.broadcasted_iota(jnp.int32, (1, 128), 1)
    for r in range(senders // 2):
        for n in range(2):
            one = moved_ref[2 * r, n : n + 1, :]
            two = moved_ref[2 * r + 1, n : n + 1, :]
            got_ref[2 * n : 2 * n + 1, 128 * r : 128 * r + 128] = jnp.where(
                left, one, pltpu.roll(two, SLOTS, 1)
            )
            got_ref[2 * n + 1 : 2 * n + 2, 128 * r : 128 * r + 128] = jnp.where(
                left, pltpu.roll(one, SLOTS, 1), two
            )
        first = step * senders + 2 * r
        limit = jnp.where(left, count_ref[0, first], count_ref[0, first + 1])
        got_ref[4:5, 128 * r : 128 * r + 128] = ((lane & (SLOTS - 1)) < limit).astype(F32)
    live = got_ref[4:5, :] > 0.5
    rate = got_ref[3:4, :]
    plane, high, low = halves(cell_ref[...])
    table = span_table(high, low)
    mask = (lax.broadcasted_iota(jnp.int32, (PLANES, CHUNK), 0) == plane).astype(F32).astype(BF16)
    spread = []
    for n in range(3):
        old = got_ref[n : n + 1, :]
        relative = fluid_ref[n : n + 1, :] - old
        part_ref[n : n + 1, :] = jnp.where(live, old + TIME_STEP * rate * relative, 0.0)
        push = jnp.where(live, -rate * relative, 0.0).astype(BF16)
        spread.append(mask * push)
    spread = jnp.concatenate(spread, axis=0)
    new = lax.dot_general(
        spread, table, (((1,), (1,)), ((), ())), preferred_element_type=F32
    )

    @pl.when(step == 0)
    def _():
        sum_ref[...] = new

    @pl.when(step > 0)
    def _():
        sum_ref[...] += new


def deposited(moved, counts, cells, fluid):
    senders = CHUNK // SLOTS
    return pl.pallas_call(
        deposit_kernel,
        grid=(TOTAL // CHUNK,),
        out_shape=(shaped(3, TOTAL), shaped(3 * PLANES, CZ)),
        in_specs=[
            pl.BlockSpec((senders, 2, 128), lambda i: (i, 0, 0)),
            SMEM,
            pl.BlockSpec((1, CHUNK), lambda i: (0, i)),
            pl.BlockSpec((3, CHUNK), lambda i: (0, i)),
        ],
        out_specs=(
            pl.BlockSpec((3, CHUNK), lambda i: (0, i)),
            pl.BlockSpec((3 * PLANES, CZ), lambda i: (0, 0)),
        ),
        scratch_shapes=[pltpu.VMEM((8, CHUNK), F32)],
        compiler_params=params(),
        name="deposit",
    )(moved, counts, cells, fluid)


def column_of(row, length):
    wide = jnp.broadcast_to(row, (length, length))
    here = lax.broadcasted_iota(jnp.int32, (length, length), 0) == lax.broadcasted_iota(
        jnp.int32, (length, length), 1
    )
    return jnp.broadcast_to(
        jnp.sum(jnp.where(here, wide, 0.0), axis=1, keepdims=True), (length, 128)
    )


def rhs_kernel(
    vel_hbm, below_hbm, above_hbm, before_ref, behind_ref, section_ref, deposit_ref,
    near_ref, far_ref, scale_ref, tip_ref, out_ref, tips_ref, pad_ref, coef_ref, sems,
):
    copies = [
        pltpu.make_async_copy(vel_hbm, pad_ref.at[:, :, 8 : 8 + ROWS, :], sems.at[0]),
        pltpu.make_async_copy(below_hbm, pad_ref.at[:, :, 6:8, :], sems.at[1]),
        pltpu.make_async_copy(above_hbm, pad_ref.at[:, :, 8 + ROWS : 10 + ROWS, :], sems.at[2]),
    ]
    for copy in copies:
        copy.start()
    coef_ref[0] = column_of(near_ref[...], ROWS)
    coef_ref[1] = column_of(far_ref[...], ROWS)
    for copy in copies:
        copy.wait()

    def tiled(column):
        return jnp.concatenate([column] * 8, axis=1)

    def one(c, carry):
        for x in range(CX):
            def layer(i, rows):
                if i < 0:
                    return before_ref[c, 2 + i, rows, :]
                if i >= CX:
                    return behind_ref[c, i - CX, rows, :]
                return pad_ref[c, i, pl.ds(8 + rows.start, 8), :]

            tips = [[None] * 8 for _ in range(4)]
            for t in range(ROWS // 8):
                rows = pl.ds(8 * t, 8)
                here = layer(x, rows)
                ddx = (8.0 / 12.0) * (layer(x + 1, rows) - layer(x - 1, rows)) - (1.0 / 12.0) * (
                    layer(x + 2, rows) - layer(x - 2, rows)
                )
                rolled = {k: pltpu.roll(here, (-k) % CZ, 1) for k in (1, -1, 2, -2)}
                ddz = (8.0 / 12.0) * (rolled[1] - rolled[-1]) - (1.0 / 12.0) * (
                    rolled[2] - rolled[-2]
                )

                def shifted(k):
                    return pad_ref[c, x, 8 + 8 * t + k : 16 + 8 * t + k, :]

                near = tiled(coef_ref[0, 8 * t : 8 * t + 8, :])
                far = tiled(coef_ref[1, 8 * t : 8 * t + 8, :])
                ddy = near * (shifted(1) - shifted(-1)) + far * (shifted(2) - shifted(-2))
                top = pl.ds(8 + 8 * t, 8)
                moved = (
                    pad_ref[0, x, top, :] * ddx
                    + pad_ref[1, x, top, :] * ddy
                    + pad_ref[2, x, top, :] * ddz
                )
                rhs = deposit_ref[c, x, rows, :] - moved
                new = SECTION_KEEP * section_ref[c, x, rows, :] + TIME_STEP * rhs
                out_ref[c, x, rows, :] = new
                scaled = new * tiled(scale_ref[8 * t : 8 * t + 8, :])
                for r in range(4):
                    weighted = scaled * tiled(tip_ref[r, 8 * t : 8 * t + 8, :])
                    tips[r] = weighted if t == 0 else tips[r] + weighted
            for r in range(4):
                tips_ref[c, x, r : r + 1, :] = jnp.sum(tips[r], axis=0, keepdims=True)
        return carry

    lax.fori_loop(0, 3, one, 0)


def right_side(velocity, below, above, before, behind, section, deposit, near, far, scale, tip):
    return pl.pallas_call(
        rhs_kernel,
        out_shape=(shaped(3, CX, ROWS, CZ), shaped(3, CX, 4, CZ)),
        in_specs=[ANY, ANY, ANY] + [VMEM] * 8,
        out_specs=(VMEM, VMEM),
        scratch_shapes=[
            pltpu.VMEM((3, CX, ROWS + 16, CZ), F32),
            pltpu.VMEM((2, ROWS, 128), F32),
            pltpu.SemaphoreType.DMA((3,)),
        ],
        compiler_params=params(),
        name="right_side",
    )(velocity, below, above, before, behind, section, deposit, near, far, scale, tip)


WIDTH = 3 * CX * CZ // SLABS


def spread_kernel(tips_ref, out_ref):
    for n in range(3 * CX * CZ // 128):
        plane, t = divmod(n, CZ // 128)
        m, k = divmod(n, WIDTH // 128)
        out_ref[m, :, 128 * k : 128 * k + 128] = tips_ref[
            plane // CX, plane % CX, :, 128 * t : 128 * t + 128
        ]


def spread_tips(tips):
    return pl.pallas_call(
        spread_kernel,
        out_shape=shaped(SLABS, 4, WIDTH),
        in_specs=[VMEM],
        out_specs=VMEM,
        name="spread_tips",
    )(tips)


def solve_kernel(tips_ref, green_ref, out_ref, all_ref):
    for s in range(SLABS):
        all_ref[4 * s : 4 * s + 4, :] = tips_ref[s]
    found = jnp.dot(green_ref[...], all_ref[...], precision=HIGH, preferred_element_type=F32)
    for s in range(SLABS):
        out_ref[s] = found[4 * s : 4 * s + 4, :]


def solved(tips, green):
    return pl.pallas_call(
        solve_kernel,
        out_shape=shaped(SLABS, 4, WIDTH),
        in_specs=[VMEM, VMEM],
        out_specs=VMEM,
        scratch_shapes=[pltpu.VMEM((4 * SLABS, WIDTH), F32)],
        name="solve",
    )(tips, green)


def local_kernel(section_ref, scale_ref, solve_ref, out_ref):
    whole = solve_ref[:, 0:ROWS]
    head = whole.astype(BF16)
    rest = (whole - head.astype(F32)).astype(BF16)
    left = jnp.concatenate([head, rest, head], axis=1)
    scale = jnp.concatenate([scale_ref[...]] * 8, axis=1)

    def one(c, carry):
        for x in range(CX):
            value = section_ref[c, x] * scale
            high = value.astype(BF16)
            low = (value - high.astype(F32)).astype(BF16)
            right = jnp.concatenate([high, high, low], axis=0)
            out_ref[c, x] = jnp.dot(left, right, preferred_element_type=F32)
        return carry

    lax.fori_loop(0, 3, one, 0)


def local_solve(section_new, scale, solve):
    return pl.pallas_call(
        local_kernel,
        out_shape=shaped(3, CX, ROWS, CZ),
        in_specs=[VMEM] * 3,
        out_specs=VMEM,
        compiler_params=params(),
        name="local_solve",
    )(section_new, scale, solve)


def final_kernel(vel_ref, partial_ref, edge_ref, fix_ref, out_ref):
    for plane in range(3 * CX):
        c, x = divmod(plane, CX)
        for t in range(CZ // 128):
            m, k = divmod(plane * (CZ // 128) + t, WIDTH // 128)
            lanes = slice(128 * t, 128 * t + 128)
            edge = edge_ref[m, :, 128 * k : 128 * k + 128]
            value = vel_ref[c, x, :, lanes] + partial_ref[c, x, :, lanes]
            for r in range(4):
                value = value - fix_ref[r] * edge[r : r + 1, :]
            out_ref[c, x, :, lanes] = value


def finished(velocity, partial, edges, fix):
    return pl.pallas_call(
        final_kernel,
        out_shape=shaped(3, CX, ROWS, CZ),
        in_specs=[VMEM] * 4,
        out_specs=VMEM,
        compiler_params=params(),
        name="finish",
    )(velocity, partial, edges, fix)


def local(velocity, section, diffusion, rhs_near, rhs_far, part_vel, part_rate, counts, cell_slot):
    n_gx, n_gy = lax.axis_size("gx"), lax.axis_size("gy")
    up_x = [(i, (i + 1) % n_gx) for i in range(n_gx)]
    down_x = [(t, s) for s, t in up_x]
    up_y = [(i, i + 1) for i in range(n_gy - 1)]
    down_y = [(t, s) for s, t in up_y]
    before = lax.ppermute(velocity[:, CX - 2 :], "gx", up_x)
    behind = lax.ppermute(velocity[:, :2], "gx", down_x)
    moved = lax.all_to_all(
        packed(part_vel, part_rate.reshape(1, TOTAL)),
        ("gx", "gy"), split_axis=0, concat_axis=0, tiled=True,
    )
    below = lax.ppermute(velocity[:, :, ROWS - 2 :], "gy", up_y)
    above = lax.ppermute(velocity[:, :, :2], "gy", down_y)
    place = lax.axis_index("gy").astype(jnp.int32).reshape(1)
    rate = jnp.pad(
        diffusion.reshape(SLABS, ROWS).T, ((0, 0), (0, 128 - SLABS)), constant_values=1000.0
    )
    scale, tip, fix, solve, green = factors(place, rate)
    fluid = gathered(velocity, cell_slot)
    part_new, deposit = deposited(moved, counts, cell_slot, fluid)
    section_new, tips = right_side(
        velocity, below, above, before, behind, section, deposit.reshape(3, CX, ROWS, CZ),
        rhs_near.reshape(1, ROWS), rhs_far.reshape(1, ROWS), scale, tip,
    )
    all_tips = lax.all_to_all(spread_tips(tips), "gy", split_axis=0, concat_axis=0, tiled=True)
    partial = local_solve(section_new, scale, solve)
    edges = lax.all_to_all(solved(all_tips, green), "gy", split_axis=0, concat_axis=0, tiled=True)
    velocity_new = finished(velocity, partial, edges, fix)
    return (velocity_new, section_new, part_new)


def solution(mesh):
    return jax.shard_map(
        local,
        mesh=mesh,
        in_specs=(
            P(None, "gx", "gy", None),
            P(None, "gx", "gy", None),
            P(),
            P("gy"),
            P("gy"),
            P(None, ("gx", "gy")),
            P(("gx", "gy")),
            P(("gx", "gy"), None),
            P(("gx", "gy"), None),
        ),
        out_specs=(P(None, "gx", "gy", None), P(None, "gx", "gy", None), P(None, ("gx", "gy"))),
        check_vma=False,
    )
```

```python
import jax
import jax.numpy as jnp
from jax import lax
from jax.experimental import pallas as pl
from jax.experimental.pallas import tpu as pltpu
from jax.sharding import PartitionSpec as P

TIME_STEP = 0.2
SECTION_KEEP = -5.0 / 9.0
SECTION_GAIN = 15.0 / 16.0
MAIN = 2.5
NEAR = -4.0 / 3.0
FAR = 1.0 / 12.0
SLABS = 32
ROWS = 32
CX = 4
CZ = 1024
PLANES = CX * ROWS
SLOTS = 64
PEERS = 128
TOTAL = PEERS * SLOTS
CHUNK = 2048
HIGH = lax.Precision.HIGHEST
F32 = jnp.float32
BF16 = jnp.bfloat16


def params(mib=60):
    return pltpu.CompilerParams(vmem_limit_bytes=mib * 1024 * 1024)


VMEM = pl.BlockSpec(memory_space=pltpu.MemorySpace.VMEM)
SMEM = pl.BlockSpec(memory_space=pltpu.MemorySpace.SMEM)
ANY = pl.BlockSpec(memory_space=pl.ANY)


def shaped(*shape):
    return jax.ShapeDtypeStruct(shape, F32)


def mm(a, b):
    return tuple(
        tuple(a[i][0] * b[0][j] + a[i][1] * b[1][j] for j in range(2)) for i in range(2)
    )


def add(a, b, sign=1.0):
    return tuple(tuple(a[i][j] + sign * b[i][j] for j in range(2)) for i in range(2))


def neg(a):
    return tuple(tuple(-e for e in row) for row in a)


def each(a, fn):
    return tuple(tuple(fn(e) for e in row) for row in a)


def inverse_of_one_minus(a):
    p, q, r, s = 1.0 - a[0][0], -a[0][1], -a[1][0], 1.0 - a[1][1]
    scale = 1.0 / (p * s - q * r)
    return ((s * scale, -q * scale), (-r * scale, p * scale))


def ldl(main_of, zero):
    recip, low1, low2 = [], [], []
    for k in range(ROWS):
        main = main_of(k)
        if k == 0:
            low1.append(zero)
            low2.append(zero)
            recip.append(1.0 / main)
            continue
        edge = NEAR - FAR * low1[k - 1]
        one = edge * recip[k - 1]
        two = FAR * recip[k - 2] if k > 1 else zero
        low1.append(one)
        low2.append(two)
        recip.append(1.0 / (main - edge * one - FAR * two))
    return recip, low1, low2


def substitute(rows, recip, low1, low2):
    half = []
    for k in range(ROWS):
        value = rows[k]
        if k > 0:
            value = value - low1[k] * half[k - 1]
        if k > 1:
            value = value - low2[k] * half[k - 2]
        half.append(value)
    full = [None] * ROWS
    for k in reversed(range(ROWS)):
        value = half[k] * recip[k]
        if k < ROWS - 1:
            value = value - low1[k + 1] * full[k + 1]
        if k < ROWS - 2:
            value = value - low2[k + 2] * full[k + 2]
        full[k] = value
    return full


ENDS = (0, 1, ROWS - 2, ROWS - 1)


def own_kernel(place_ref, rate_ref, scale_ref, tip_ref, fix_ref, solve_ref, wide_ref):
    slab = place_ref[0]
    lane8 = lax.broadcasted_iota(jnp.int32, (8, 128), 1)
    row = rate_ref[pl.ds(slab // 4, 1), :]
    row = pltpu.roll(jnp.broadcast_to(row, (8, 128)), 128 - ROWS * (slab % 4), 1)
    inv_rate = 1.0 / column_of(row[0:1, 0:ROWS], ROWS)
    scale_ref[...] = SECTION_GAIN * inv_rate
    wide_ref[...] = inv_rate + MAIN
    recip, low1, low2 = ldl(
        lambda k: jnp.broadcast_to(wide_ref[k : k + 1, :], (8, 128)), jnp.zeros((8, 128), F32)
    )
    full = substitute([(lane8 == k).astype(F32) for k in range(ROWS)], recip, low1, low2)
    for k in range(ROWS):
        solve_ref[k : k + 1, :] = full[k][0:1]
    solve = solve_ref[...]
    cols = [jnp.broadcast_to(solve[:, n : n + 1], (ROWS, 128)) for n in ENDS]
    for n in range(4):
        tip_ref[n] = cols[n]
    has_low = jnp.where(slab > 0, 1.0, 0.0)
    has_high = jnp.where(slab < SLABS - 1, 1.0, 0.0)
    fix_ref[0] = FAR * cols[0] * has_low
    fix_ref[1] = (NEAR * cols[0] + FAR * cols[1]) * has_low
    fix_ref[2] = (FAR * cols[2] + NEAR * cols[3]) * has_high
    fix_ref[3] = FAR * cols[3] * has_high


def own_factors(place, rate):
    return pl.pallas_call(
        own_kernel,
        out_shape=(
            shaped(ROWS, 128),
            shaped(4, ROWS, 128),
            shaped(4, ROWS, 128),
            shaped(ROWS, 128),
        ),
        in_specs=[SMEM, VMEM],
        out_specs=(VMEM,) * 4,
        scratch_shapes=[pltpu.VMEM((ROWS, 128), F32)],
        name="own_factors",
    )(place, rate)


def green_kernel(rate_ref, green_ref, wide_ref, coef_ref):
    lane8 = lax.broadcasted_iota(jnp.int32, (8, 128), 1)
    sub8 = lax.broadcasted_iota(jnp.int32, (8, 128), 0)
    wide_ref[...] = 1.0 / rate_ref[...] + MAIN
    zero = jnp.zeros((8, 128), F32)
    recip, low1, low2 = ldl(lambda k: jnp.broadcast_to(wide_ref[k : k + 1, :], (8, 128)), zero)
    units = [(sub8 == ENDS.index(k)).astype(F32) if k in ENDS else zero for k in range(ROWS)]
    full = substitute(units, recip, low1, low2)

    def entry(k, i):
        return jnp.broadcast_to(full[k][i : i + 1, :], (8, 128))

    not_first = ((lane8 > 0) & (lane8 < SLABS)).astype(F32)
    not_last = (lane8 < SLABS - 1).astype(F32)

    def lower(k):
        s0, s1 = entry(k, 0), entry(k, 1)
        return (FAR * s0 * not_first, (NEAR * s0 + FAR * s1) * not_first)

    def upper(k):
        s2, s3 = entry(k, 2), entry(k, 3)
        return ((FAR * s2 + NEAR * s3) * not_last, FAR * s3 * not_last)

    low_a = (lower(ENDS[0]), lower(ENDS[1]))
    low_c = (lower(ENDS[2]), lower(ENDS[3]))
    up_b = (upper(ENDS[0]), upper(ENDS[1]))
    up_e = (upper(ENDS[2]), upper(ENDS[3]))
    a, b, c, e = low_a, up_b, low_c, up_e
    for hop in (1, 2, 4, 8, 16):
        ax, bx, cx, ex = (each(m, lambda v: pltpu.roll(v, hop, 1)) for m in (a, b, c, e))
        w = inverse_of_one_minus(mm(a, ex))
        wa_c = mm(w, mm(a, cx))
        wb = mm(w, b)
        cy_ex = mm(c, ex)
        new_e = add(e, mm(cy_ex, wb))
        new_c = neg(add(mm(c, cx), mm(cy_ex, wa_c)))
        new_a = add(ax, mm(bx, wa_c))
        new_b = neg(mm(bx, wb))
        joined = lane8 >= hop

        def pick(new, old):
            return tuple(
                tuple(jnp.where(joined, new[i][j], old[i][j]) for j in range(2)) for i in range(2)
            )

        a, b, c, e = pick(new_a, a), pick(new_b, b), pick(new_c, c), pick(new_e, e)
    q = e
    q_prev = each(q, lambda v: jnp.where(lane8 > 0, pltpu.roll(v, 1, 1), 0.0))
    z = inverse_of_one_minus(mm(low_a, q_prev))
    gain = mm(mm(low_c, q_prev), z)
    carry = add(low_c, mm(gain, low_a))
    z_low = mm(z, low_a)
    z_up = mm(z, up_b)
    for group, mats in enumerate(((carry, gain), (z, z_low), (z_up, q))):
        block = jnp.zeros((8, 128), F32)
        for n, m in enumerate(mats):
            for i in range(2):
                for j in range(2):
                    block = jnp.where(sub8 == 4 * n + 2 * i + j, m[i][j], block)
        for s in range(SLABS):
            coef_ref[s, 8 * group : 8 * group + 8, :] = jnp.broadcast_to(block[:, s : s + 1], (8, 128))

    def coef(s, n):
        def one(i, j):
            at = 4 * n + 2 * i + j
            return jnp.broadcast_to(coef_ref[s, at : at + 1, :], (8, 128))

        return tuple(tuple(one(i, j) for j in range(2)) for i in range(2))

    def at_lane(n):
        return lane8 == n

    forward = []
    prev = None
    for s in range(SLABS):
        m, g = coef(s, 0), coef(s, 1)
        now = []
        for i in range(2):
            value = jnp.where(at_lane(4 * s), g[i][0], 0.0)
            value = jnp.where(at_lane(4 * s + 1), g[i][1], value)
            value = jnp.where(at_lane(4 * s + 2 + i), 1.0, value)
            if prev is not None:
                value = value - m[i][0] * prev[0] - m[i][1] * prev[1]
            now.append(value)
        forward.append(now)
        prev = now
    for row in (0, 1, 4 * SLABS - 2, 4 * SLABS - 1):
        green_ref[row : row + 1, :] = jnp.zeros((1, 128), F32)
    after = None
    for s in reversed(range(SLABS)):
        zc, zl, zu, qc = coef(s, 2), coef(s, 3), coef(s, 4), coef(s, 5)
        now = []
        for i in range(2):
            value = jnp.where(at_lane(4 * s), zc[i][0], 0.0)
            value = jnp.where(at_lane(4 * s + 1), zc[i][1], value)
            if s > 0:
                value = value - zl[i][0] * forward[s - 1][0] - zl[i][1] * forward[s - 1][1]
            if after is not None:
                value = value - zu[i][0] * after[0] - zu[i][1] * after[1]
            now.append(value)
        if s < SLABS - 1:
            for i in range(2):
                high = forward[s][i] - qc[i][0] * after[0] - qc[i][1] * after[1]
                green_ref[4 * (s + 1) + i : 4 * (s + 1) + i + 1, :] = high[0:1]
        if s > 0:
            for i in range(2):
                green_ref[4 * (s - 1) + 2 + i : 4 * (s - 1) + 3 + i, :] = now[i][0:1]
        after = now


def green_operator(rate):
    return pl.pallas_call(
        green_kernel,
        out_shape=shaped(128, 128),
        in_specs=[VMEM],
        out_specs=VMEM,
        scratch_shapes=[pltpu.VMEM((ROWS, 128), F32), pltpu.VMEM((SLABS, 24, 128), F32)],
        name="green_operator",
    )(rate)


def pack_kernel(vel_ref, rate_ref, out_ref):
    left = lax.broadcasted_iota(jnp.int32, (1, 128), 1) < SLOTS
    for r in range(PEERS // 2):
        part = [vel_ref[i : i + 1, 128 * r : 128 * r + 128] for i in range(3)]
        part.append(rate_ref[0:1, 128 * r : 128 * r + 128])
        for n in range(2):
            one, two = part[2 * n], part[2 * n + 1]
            out_ref[2 * r, n : n + 1, :] = jnp.where(left, one, pltpu.roll(two, SLOTS, 1))
            out_ref[2 * r + 1, n : n + 1, :] = jnp.where(left, pltpu.roll(one, SLOTS, 1), two)


def packed(part_vel, part_rate):
    return pl.pallas_call(
        pack_kernel,
        out_shape=shaped(PEERS, 2, 128),
        in_specs=[VMEM, VMEM],
        out_specs=VMEM,
        name="pack",
    )(part_vel, part_rate)


def halves(cells):
    plane = cells >> 10
    span = cells & (CZ - 1)
    return plane, span >> 7, span & 127


def span_table(high, low):
    width = high.shape[1]
    inner = lax.broadcasted_iota(jnp.int32, (128, width), 0) == low
    inner = inner.astype(F32).astype(BF16)
    rows = []
    for t in range(8):
        flag = (high == t).astype(F32).astype(BF16)
        rows.append(inner * flag)
    return jnp.concatenate(rows, axis=0)


def column_of(row, length):
    wide = jnp.broadcast_to(row, (length, length))
    here = lax.broadcasted_iota(jnp.int32, (length, length), 0) == lax.broadcasted_iota(
        jnp.int32, (length, length), 1
    )
    return jnp.broadcast_to(
        jnp.sum(jnp.where(here, wide, 0.0), axis=1, keepdims=True), (length, 128)
    )


def main_kernel(
    vel_hbm, below_hbm, above_hbm, before_hbm, behind_hbm, section_hbm, moved_ref, count_ref,
    cell_ref, near_ref, far_ref, scale_ref, tip_ref, part_ref, out_hbm, tips_ref,
    pad_ref, before_ref, behind_ref, section_ref, new_ref, bf_ref, table_ref, got_ref, deposit_ref,
    coef_ref, sems,
):
    copies = [
        pltpu.make_async_copy(vel_hbm, pad_ref.at[:, :, 8 : 8 + ROWS, :], sems.at[0]),
        pltpu.make_async_copy(below_hbm, pad_ref.at[:, :, 6:8, :], sems.at[1]),
        pltpu.make_async_copy(above_hbm, pad_ref.at[:, :, 8 + ROWS : 10 + ROWS, :], sems.at[2]),
        pltpu.make_async_copy(before_hbm, before_ref, sems.at[3]),
        pltpu.make_async_copy(behind_hbm, behind_ref, sems.at[4]),
        pltpu.make_async_copy(section_hbm, section_ref, sems.at[5]),
    ]
    for copy in copies:
        copy.start()
    coef_ref[0] = column_of(near_ref[...], ROWS)
    coef_ref[1] = column_of(far_ref[...], ROWS)
    left = lax.broadcasted_iota(jnp.int32, (1, 128), 1) < SLOTS
    lane = lax.broadcasted_iota(jnp.int32, (1, 128), 1)
    for r in range(PEERS // 2):
        lanes = slice(128 * r, 128 * r + 128)
        for n in range(2):
            one = moved_ref[2 * r, n : n + 1, :]
            two = moved_ref[2 * r + 1, n : n + 1, :]
            got_ref[2 * n : 2 * n + 1, lanes] = jnp.where(left, one, pltpu.roll(two, SLOTS, 1))
            got_ref[2 * n + 1 : 2 * n + 2, lanes] = jnp.where(left, pltpu.roll(one, SLOTS, 1), two)
        limit = jnp.where(left, count_ref[0, 2 * r], count_ref[0, 2 * r + 1])
        got_ref[4:5, lanes] = ((lane & (SLOTS - 1)) < limit).astype(F32)
    copies[0].wait()
    for c in range(3):
        for x in range(CX):
            top = c * PLANES + x * ROWS
            bf_ref[top : top + ROWS, :] = pad_ref[c, x, 8 : 8 + ROWS, :].astype(BF16)

    for step in range(TOTAL // CHUNK):
        lanes = slice(step * CHUNK, (step + 1) * CHUNK)
        plane, high, low = halves(cell_ref[:, lanes])
        table_ref[...] = span_table(high, low)
        at = jnp.dot(bf_ref[...], table_ref[...], preferred_element_type=F32)
        mask = lax.broadcasted_iota(jnp.int32, (PLANES, CHUNK), 0) == plane
        mask_bf = mask.astype(F32).astype(BF16)
        live = got_ref[4:5, lanes] > 0.5
        rate = got_ref[3:4, lanes]
        spread = []
        for n in range(3):
            fluid = jnp.sum(
                jnp.where(mask, at[n * PLANES : (n + 1) * PLANES], 0.0), axis=0, keepdims=True
            )
            old = got_ref[n : n + 1, lanes]
            relative = fluid - old
            part_ref[n : n + 1, lanes] = jnp.where(live, old + TIME_STEP * rate * relative, 0.0)
            push = jnp.where(live, -rate * relative, 0.0).astype(BF16)
            spread.append(mask_bf * push)
        new = lax.dot_general(
            jnp.concatenate(spread, axis=0), table_ref[...], (((1,), (1,)), ((), ())),
            preferred_element_type=F32,
        )
        if step == 0:
            deposit_ref[...] = new
        else:
            deposit_ref[...] += new

    for copy in copies[1:]:
        copy.wait()

    def tiled(column):
        return jnp.concatenate([column] * 8, axis=1)

    def stored(c):
        return pltpu.make_async_copy(new_ref.at[c], out_hbm.at[c], sems.at[6 + c])

    for c in range(3):
        for x in range(CX):
            def layer(i, top):
                if i < 0:
                    return before_ref[c, 2 + i, top : top + 8, :]
                if i >= CX:
                    return behind_ref[c, i - CX, top : top + 8, :]
                return pad_ref[c, i, 8 + top : 16 + top, :]

            tips = [None] * 4
            for t in range(ROWS // 8):
                top = 8 * t
                here = layer(x, top)
                ddx = (8.0 / 12.0) * (layer(x + 1, top) - layer(x - 1, top)) - (1.0 / 12.0) * (
                    layer(x + 2, top) - layer(x - 2, top)
                )
                rolled = {k: pltpu.roll(here, (-k) % CZ, 1) for k in (1, -1, 2, -2)}
                ddz = (8.0 / 12.0) * (rolled[1] - rolled[-1]) - (1.0 / 12.0) * (
                    rolled[2] - rolled[-2]
                )

                def shifted(k):
                    return pad_ref[c, x, 8 + top + k : 16 + top + k, :]

                near = tiled(coef_ref[0, top : top + 8, :])
                far = tiled(coef_ref[1, top : top + 8, :])
                ddy = near * (shifted(1) - shifted(-1)) + far * (shifted(2) - shifted(-2))
                moved = (
                    pad_ref[0, x, 8 + top : 16 + top, :] * ddx
                    + pad_ref[1, x, 8 + top : 16 + top, :] * ddy
                    + pad_ref[2, x, 8 + top : 16 + top, :] * ddz
                )
                base = c * PLANES + x * ROWS + top
                rhs = deposit_ref[base : base + 8, :] - moved
                new = SECTION_KEEP * section_ref[c, x, top : top + 8, :] + TIME_STEP * rhs
                new_ref[c, x, top : top + 8, :] = new
                scaled = new * tiled(scale_ref[top : top + 8, :])
                for r in range(4):
                    weighted = scaled * tiled(tip_ref[r, top : top + 8, :])
                    tips[r] = weighted if t == 0 else tips[r] + weighted
            for r in range(4):
                total = jnp.sum(tips[r], axis=0, keepdims=True)
                for t in range(CZ // 128):
                    tips_ref[8 * x + t, c, r : r + 1, :] = total[:, 128 * t : 128 * t + 128]
        stored(c).start()
    for c in range(3):
        stored(c).wait()


def main_part(*operands):
    return pl.pallas_call(
        main_kernel,
        out_shape=(
            shaped(3, TOTAL),
            shaped(3, CX, ROWS, CZ),
            shaped(SLABS, 3, 4, 128),
        ),
        in_specs=[ANY] * 6 + [VMEM, SMEM] + [VMEM] * 5,
        out_specs=(VMEM, ANY, VMEM),
        scratch_shapes=[
            pltpu.VMEM((3, CX, ROWS + 16, CZ), F32),
            pltpu.VMEM((3, 2, ROWS, CZ), F32),
            pltpu.VMEM((3, 2, ROWS, CZ), F32),
            pltpu.VMEM((3, CX, ROWS, CZ), F32),
            pltpu.VMEM((3, CX, ROWS, CZ), F32),
            pltpu.VMEM((3 * PLANES, CZ), BF16),
            pltpu.VMEM((CZ, CHUNK), BF16),
            pltpu.VMEM((8, TOTAL), F32),
            pltpu.VMEM((3 * PLANES, CZ), F32),
            pltpu.VMEM((2, ROWS, 128), F32),
            pltpu.SemaphoreType.DMA((9,)),
        ],
        compiler_params=params(),
        name="main_part",
    )(*operands)


WIDTH = 3 * CX * CZ // SLABS


def solve_kernel(tips_ref, green_ref, out_ref, all_ref):
    for s in range(SLABS):
        for c in range(3):
            all_ref[4 * s : 4 * s + 4, 128 * c : 128 * c + 128] = tips_ref[s, c]
    found = jnp.dot(green_ref[...], all_ref[...], precision=HIGH, preferred_element_type=F32)
    for s in range(SLABS):
        for c in range(3):
            out_ref[s, c] = found[4 * s : 4 * s + 4, 128 * c : 128 * c + 128]


def solved(tips, green):
    return pl.pallas_call(
        solve_kernel,
        out_shape=shaped(SLABS, 3, 4, 128),
        in_specs=[VMEM, VMEM],
        out_specs=VMEM,
        scratch_shapes=[pltpu.VMEM((4 * SLABS, WIDTH), F32)],
        name="solve",
    )(tips, green)


def local_kernel(vel_ref, section_ref, scale_ref, solve_ref, out_ref):
    whole = solve_ref[:, 0:ROWS]
    head = whole.astype(BF16)
    rest = (whole - head.astype(F32)).astype(BF16)
    left = jnp.concatenate([head, rest, head], axis=1)
    scale = jnp.concatenate([scale_ref[...]] * 8, axis=1)
    for x in range(CX):
        value = section_ref[0, x] * scale
        high = value.astype(BF16)
        low = (value - high.astype(F32)).astype(BF16)
        right = jnp.concatenate([high, high, low], axis=0)
        out_ref[0, x] = vel_ref[0, x] + jnp.dot(left, right, preferred_element_type=F32)


BLOCK = pl.BlockSpec((1, CX, ROWS, CZ), lambda c: (c, 0, 0, 0))


def local_solve(velocity, section_new, scale, solve):
    return pl.pallas_call(
        local_kernel,
        grid=(3,),
        out_shape=shaped(3, CX, ROWS, CZ),
        in_specs=[BLOCK, BLOCK, VMEM, VMEM],
        out_specs=BLOCK,
        compiler_params=params(),
        name="local_solve",
    )(velocity, section_new, scale, solve)


def final_kernel(partial_ref, edge_ref, fix_ref, out_ref):
    c = pl.program_id(0)
    for x in range(CX):
        for t in range(CZ // 128):
            lanes = slice(128 * t, 128 * t + 128)
            edge = edge_ref[8 * x + t, c]
            value = partial_ref[0, x, :, lanes]
            for r in range(4):
                value = value - fix_ref[r] * edge[r : r + 1, :]
            out_ref[0, x, :, lanes] = value


def finished(partial, edges, fix):
    return pl.pallas_call(
        final_kernel,
        grid=(3,),
        out_shape=shaped(3, CX, ROWS, CZ),
        in_specs=[BLOCK, VMEM, VMEM],
        out_specs=BLOCK,
        compiler_params=params(),
        name="finish",
    )(partial, edges, fix)


def local(velocity, section, diffusion, rhs_near, rhs_far, part_vel, part_rate, counts, cell_slot):
    n_gx, n_gy = lax.axis_size("gx"), lax.axis_size("gy")
    up_x = [(i, (i + 1) % n_gx) for i in range(n_gx)]
    down_x = [(t, s) for s, t in up_x]
    up_y = [(i, i + 1) for i in range(n_gy - 1)]
    down_y = [(t, s) for s, t in up_y]
    before = lax.ppermute(velocity[:, CX - 2 :], "gx", up_x)
    behind = lax.ppermute(velocity[:, :2], "gx", down_x)
    moved = lax.all_to_all(
        packed(part_vel, part_rate.reshape(1, TOTAL)),
        ("gx", "gy"), split_axis=0, concat_axis=0, tiled=True,
    )
    below = lax.ppermute(velocity[:, :, ROWS - 2 :], "gy", up_y)
    above = lax.ppermute(velocity[:, :, :2], "gy", down_y)
    place = lax.axis_index("gy").astype(jnp.int32).reshape(1)
    scale, tip, fix, solve = own_factors(place, diffusion.reshape(8, 128))
    part_new, section_new, tips = main_part(
        velocity, below, above, before, behind, section, moved, counts, cell_slot,
        rhs_near.reshape(1, ROWS), rhs_far.reshape(1, ROWS), scale, tip,
    )
    tips, diffusion = lax.optimization_barrier((tips, diffusion))
    all_tips = lax.all_to_all(tips, "gy", split_axis=0, concat_axis=0, tiled=True)
    rate = jnp.pad(
        diffusion.reshape(SLABS, ROWS).T, ((0, 0), (0, 128 - SLABS)), constant_values=1000.0
    )
    reply = solved(all_tips, green_operator(rate))
    reply, section_done = lax.optimization_barrier((reply, section_new))
    edges = lax.all_to_all(reply, "gy", split_axis=0, concat_axis=0, tiled=True)
    velocity_new = finished(local_solve(velocity, section_done, scale, solve), edges, fix)
    return (velocity_new, section_new, part_new)


def solution(mesh):
    return jax.shard_map(
        local,
        mesh=mesh,
        in_specs=(
            P(None, "gx", "gy", None),
            P(None, "gx", "gy", None),
            P(),
            P("gy"),
            P("gy"),
            P(None, ("gx", "gy")),
            P(("gx", "gy")),
            P(("gx", "gy"), None),
            P(("gx", "gy"), None),
        ),
        out_specs=(P(None, "gx", "gy", None), P(None, "gx", "gy", None), P(None, ("gx", "gy"))),
        check_vma=False,
    )
```

```python
import jax
import jax.numpy as jnp
from jax import lax
from jax.experimental import pallas as pl
from jax.experimental.pallas import tpu as pltpu
from jax.sharding import PartitionSpec as P

TIME_STEP = 0.2
SECTION_KEEP = -5.0 / 9.0
SECTION_GAIN = 15.0 / 16.0
MAIN = 2.5
NEAR = -4.0 / 3.0
FAR = 1.0 / 12.0
SLABS = 32
ROWS = 32
CX = 4
CZ = 1024
PLANES = CX * ROWS
SLOTS = 64
PEERS = 128
TOTAL = PEERS * SLOTS
CHUNK = 2048
HIGH = lax.Precision.HIGHEST
F32 = jnp.float32
BF16 = jnp.bfloat16


def params(mib=60):
    return pltpu.CompilerParams(vmem_limit_bytes=mib * 1024 * 1024)


VMEM = pl.BlockSpec(memory_space=pltpu.MemorySpace.VMEM)
SMEM = pl.BlockSpec(memory_space=pltpu.MemorySpace.SMEM)
ANY = pl.BlockSpec(memory_space=pltpu.MemorySpace.HBM)


def held(shape, dtype=F32):
    return pltpu.MemorySpace.VMEM(shape, dtype)


def shaped(*shape):
    return jax.ShapeDtypeStruct(shape, F32)


def far_out(*shape):
    return pltpu.MemorySpace.HBM(shape, F32)


def far_in(*arrays):
    return [pltpu.with_memory_space_constraint(a, pltpu.MemorySpace.HBM) for a in arrays]


def mm(a, b):
    return tuple(
        tuple(a[i][0] * b[0][j] + a[i][1] * b[1][j] for j in range(2)) for i in range(2)
    )


def add(a, b, sign=1.0):
    return tuple(tuple(a[i][j] + sign * b[i][j] for j in range(2)) for i in range(2))


def neg(a):
    return tuple(tuple(-e for e in row) for row in a)


def each(a, fn):
    return tuple(tuple(fn(e) for e in row) for row in a)


def inverse_of_one_minus(a):
    p, q, r, s = 1.0 - a[0][0], -a[0][1], -a[1][0], 1.0 - a[1][1]
    scale = 1.0 / (p * s - q * r)
    return ((s * scale, -q * scale), (-r * scale, p * scale))


def ldl(main_of, zero):
    recip, low1, low2 = [], [], []
    for k in range(ROWS):
        main = main_of(k)
        if k == 0:
            low1.append(zero)
            low2.append(zero)
            recip.append(1.0 / main)
            continue
        edge = NEAR - FAR * low1[k - 1]
        one = edge * recip[k - 1]
        two = FAR * recip[k - 2] if k > 1 else zero
        low1.append(one)
        low2.append(two)
        recip.append(1.0 / (main - edge * one - FAR * two))
    return recip, low1, low2


def substitute(rows, recip, low1, low2):
    half = []
    for k in range(ROWS):
        value = rows[k]
        if k > 0:
            value = value - low1[k] * half[k - 1]
        if k > 1:
            value = value - low2[k] * half[k - 2]
        half.append(value)
    full = [None] * ROWS
    for k in reversed(range(ROWS)):
        value = half[k] * recip[k]
        if k < ROWS - 1:
            value = value - low1[k + 1] * full[k + 1]
        if k < ROWS - 2:
            value = value - low2[k + 2] * full[k + 2]
        full[k] = value
    return full


ENDS = (0, 1, ROWS - 2, ROWS - 1)


def own_factors(slab, rate_ref, scale_ref, tip_ref, fix_ref, solve_ref, wide_ref):
    lane8 = lax.broadcasted_iota(jnp.int32, (8, 128), 1)
    row = rate_ref[pl.ds(slab // 4, 1), :]
    row = pltpu.roll(jnp.broadcast_to(row, (8, 128)), 128 - ROWS * (slab % 4), 1)
    inv_rate = 1.0 / column_of(row[0:1, 0:ROWS], ROWS)
    scale_ref[...] = SECTION_GAIN * inv_rate
    wide_ref[...] = inv_rate + MAIN
    recip, low1, low2 = ldl(
        lambda k: jnp.broadcast_to(wide_ref[k : k + 1, :], (8, 128)), jnp.zeros((8, 128), F32)
    )
    full = substitute([(lane8 == k).astype(F32) for k in range(ROWS)], recip, low1, low2)
    for k in range(ROWS):
        solve_ref[k : k + 1, :] = full[k][0:1]
    solve = solve_ref[...]
    cols = [jnp.broadcast_to(solve[:, n : n + 1], (ROWS, 128)) for n in ENDS]
    for n in range(4):
        tip_ref[n] = cols[n]
    has_low = jnp.where(slab > 0, 1.0, 0.0)
    has_high = jnp.where(slab < SLABS - 1, 1.0, 0.0)
    fix_ref[0] = FAR * cols[0] * has_low
    fix_ref[1] = (NEAR * cols[0] + FAR * cols[1]) * has_low
    fix_ref[2] = (FAR * cols[2] + NEAR * cols[3]) * has_high
    fix_ref[3] = FAR * cols[3] * has_high


def green_kernel(rate_ref, green_ref, wide_ref, coef_ref):
    lane8 = lax.broadcasted_iota(jnp.int32, (8, 128), 1)
    sub8 = lax.broadcasted_iota(jnp.int32, (8, 128), 0)
    wide_ref[...] = 1.0 / rate_ref[...] + MAIN
    zero = jnp.zeros((8, 128), F32)
    recip, low1, low2 = ldl(lambda k: jnp.broadcast_to(wide_ref[k : k + 1, :], (8, 128)), zero)
    units = [(sub8 == ENDS.index(k)).astype(F32) if k in ENDS else zero for k in range(ROWS)]
    full = substitute(units, recip, low1, low2)

    def entry(k, i):
        return jnp.broadcast_to(full[k][i : i + 1, :], (8, 128))

    not_first = ((lane8 > 0) & (lane8 < SLABS)).astype(F32)
    not_last = (lane8 < SLABS - 1).astype(F32)

    def lower(k):
        s0, s1 = entry(k, 0), entry(k, 1)
        return (FAR * s0 * not_first, (NEAR * s0 + FAR * s1) * not_first)

    def upper(k):
        s2, s3 = entry(k, 2), entry(k, 3)
        return ((FAR * s2 + NEAR * s3) * not_last, FAR * s3 * not_last)

    low_a = (lower(ENDS[0]), lower(ENDS[1]))
    low_c = (lower(ENDS[2]), lower(ENDS[3]))
    up_b = (upper(ENDS[0]), upper(ENDS[1]))
    up_e = (upper(ENDS[2]), upper(ENDS[3]))
    a, b, c, e = low_a, up_b, low_c, up_e
    for hop in (1, 2, 4, 8, 16):
        ax, bx, cx, ex = (each(m, lambda v: pltpu.roll(v, hop, 1)) for m in (a, b, c, e))
        w = inverse_of_one_minus(mm(a, ex))
        wa_c = mm(w, mm(a, cx))
        wb = mm(w, b)
        cy_ex = mm(c, ex)
        new_e = add(e, mm(cy_ex, wb))
        new_c = neg(add(mm(c, cx), mm(cy_ex, wa_c)))
        new_a = add(ax, mm(bx, wa_c))
        new_b = neg(mm(bx, wb))
        joined = lane8 >= hop

        def pick(new, old):
            return tuple(
                tuple(jnp.where(joined, new[i][j], old[i][j]) for j in range(2)) for i in range(2)
            )

        a, b, c, e = pick(new_a, a), pick(new_b, b), pick(new_c, c), pick(new_e, e)
    q = e
    q_prev = each(q, lambda v: jnp.where(lane8 > 0, pltpu.roll(v, 1, 1), 0.0))
    z = inverse_of_one_minus(mm(low_a, q_prev))
    gain = mm(mm(low_c, q_prev), z)
    carry = add(low_c, mm(gain, low_a))
    z_low = mm(z, low_a)
    z_up = mm(z, up_b)
    for group, mats in enumerate(((carry, gain), (z, z_low), (z_up, q))):
        block = jnp.zeros((8, 128), F32)
        for n, m in enumerate(mats):
            for i in range(2):
                for j in range(2):
                    block = jnp.where(sub8 == 4 * n + 2 * i + j, m[i][j], block)
        for s in range(SLABS):
            coef_ref[s, 8 * group : 8 * group + 8, :] = jnp.broadcast_to(block[:, s : s + 1], (8, 128))

    def coef(s, n):
        def one(i, j):
            at = 4 * n + 2 * i + j
            return jnp.broadcast_to(coef_ref[s, at : at + 1, :], (8, 128))

        return tuple(tuple(one(i, j) for j in range(2)) for i in range(2))

    def at_lane(n):
        return lane8 == n

    forward = []
    prev = None
    for s in range(SLABS):
        m, g = coef(s, 0), coef(s, 1)
        now = []
        for i in range(2):
            value = jnp.where(at_lane(4 * s), g[i][0], 0.0)
            value = jnp.where(at_lane(4 * s + 1), g[i][1], value)
            value = jnp.where(at_lane(4 * s + 2 + i), 1.0, value)
            if prev is not None:
                value = value - m[i][0] * prev[0] - m[i][1] * prev[1]
            now.append(value)
        forward.append(now)
        prev = now
    for row in (0, 1, 4 * SLABS - 2, 4 * SLABS - 1):
        green_ref[row : row + 1, :] = jnp.zeros((1, 128), F32)
    after = None
    for s in reversed(range(SLABS)):
        zc, zl, zu, qc = coef(s, 2), coef(s, 3), coef(s, 4), coef(s, 5)
        now = []
        for i in range(2):
            value = jnp.where(at_lane(4 * s), zc[i][0], 0.0)
            value = jnp.where(at_lane(4 * s + 1), zc[i][1], value)
            if s > 0:
                value = value - zl[i][0] * forward[s - 1][0] - zl[i][1] * forward[s - 1][1]
            if after is not None:
                value = value - zu[i][0] * after[0] - zu[i][1] * after[1]
            now.append(value)
        if s < SLABS - 1:
            for i in range(2):
                high = forward[s][i] - qc[i][0] * after[0] - qc[i][1] * after[1]
                green_ref[4 * (s + 1) + i : 4 * (s + 1) + i + 1, :] = high[0:1]
        if s > 0:
            for i in range(2):
                green_ref[4 * (s - 1) + 2 + i : 4 * (s - 1) + 3 + i, :] = now[i][0:1]
        after = now


def green_operator(rate):
    return pl.pallas_call(
        green_kernel,
        out_shape=shaped(128, 128),
        in_specs=[VMEM],
        out_specs=VMEM,
        scratch_shapes=[pltpu.VMEM((ROWS, 128), F32), pltpu.VMEM((SLABS, 24, 128), F32)],
        compiler_params=params(4),
        name="green_operator",
    )(rate)


def pre_kernel(
    vel_hbm, part_hbm, rate_hbm, high_hbm, low_hbm, below_hbm, above_hbm, packed_hbm, vel_ref,
    part_ref, rate_ref, out_ref, sems,
):
    into = [
        pltpu.make_async_copy(vel_hbm.at[:, 2:4], vel_ref.at[:, 2:4], sems.at[0]),
        pltpu.make_async_copy(vel_hbm.at[:, 0:2], vel_ref.at[:, 0:2], sems.at[1]),
        pltpu.make_async_copy(part_hbm, part_ref, sems.at[2]),
        pltpu.make_async_copy(rate_hbm, rate_ref, sems.at[3]),
    ]
    for copy in into:
        copy.start()
    out = [
        pltpu.make_async_copy(vel_ref.at[:, 2:4], high_hbm, sems.at[4]),
        pltpu.make_async_copy(vel_ref.at[:, 0:2], low_hbm, sems.at[5]),
        pltpu.make_async_copy(vel_ref.at[:, :, ROWS - 2 : ROWS], below_hbm, sems.at[6]),
        pltpu.make_async_copy(vel_ref.at[:, :, 0:2], above_hbm, sems.at[7]),
        pltpu.make_async_copy(out_ref, packed_hbm, sems.at[8]),
    ]
    into[2].wait()
    into[3].wait()
    left = lax.broadcasted_iota(jnp.int32, (1, 128), 1) < SLOTS
    for r in range(PEERS // 2):
        part = [part_ref[i : i + 1, 128 * r : 128 * r + 128] for i in range(3)]
        part.append(rate_ref[0:1, 128 * r : 128 * r + 128])
        for n in range(2):
            one, two = part[2 * n], part[2 * n + 1]
            out_ref[2 * r, n : n + 1, :] = jnp.where(left, one, pltpu.roll(two, SLOTS, 1))
            out_ref[2 * r + 1, n : n + 1, :] = jnp.where(left, pltpu.roll(one, SLOTS, 1), two)
    out[4].start()
    into[0].wait()
    out[0].start()
    into[1].wait()
    out[1].start()
    out[2].start()
    out[3].start()
    for copy in out:
        copy.wait()


def prepared(velocity, part_vel, part_rate):
    return pl.pallas_call(
        pre_kernel,
        out_shape=(
            far_out(3, 2, ROWS, CZ),
            far_out(3, 2, ROWS, CZ),
            far_out(3, CX, 2, CZ),
            far_out(3, CX, 2, CZ),
            far_out(PEERS, 2, 128),
            held((3, CX, ROWS, CZ)),
        ),
        in_specs=[ANY] * 3,
        out_specs=(ANY,) * 5 + (VMEM,),
        scratch_shapes=[
            pltpu.VMEM((3, TOTAL), F32),
            pltpu.VMEM((1, TOTAL), F32),
            pltpu.VMEM((PEERS, 2, 128), F32),
            pltpu.SemaphoreType.DMA((9,)),
        ],
        compiler_params=params(16),
        name="prepare",
    )(*far_in(velocity, part_vel, part_rate))


def halves(cells):
    plane = cells >> 10
    span = cells & (CZ - 1)
    return plane, span >> 7, span & 127


def span_table(high, low):
    width = high.shape[1]
    inner = lax.broadcasted_iota(jnp.int32, (128, width), 0) == low
    inner = inner.astype(F32).astype(BF16)
    rows = []
    for t in range(8):
        flag = (high == t).astype(F32).astype(BF16)
        rows.append(inner * flag)
    return jnp.concatenate(rows, axis=0)


def column_of(row, length):
    wide = jnp.broadcast_to(row, (length, length))
    here = lax.broadcasted_iota(jnp.int32, (length, length), 0) == lax.broadcasted_iota(
        jnp.int32, (length, length), 1
    )
    return jnp.broadcast_to(
        jnp.sum(jnp.where(here, wide, 0.0), axis=1, keepdims=True), (length, 128)
    )


def find_kernel(
    place_ref, vel_ref, cell_hbm, rate_hbm, fluid_ref, scale_ref, tip_ref, fix_ref, solve_ref,
    bf_ref, table_ref, cell_ref, rate_ref, wide_ref, sems,
):
    copies = [
        pltpu.make_async_copy(cell_hbm, cell_ref, sems.at[0]),
        pltpu.make_async_copy(rate_hbm, rate_ref, sems.at[1]),
    ]
    for copy in copies:
        copy.start()
    for c in range(3):
        for x in range(CX):
            top = c * PLANES + x * ROWS
            bf_ref[top : top + ROWS, :] = vel_ref[c, x].astype(BF16)
    for copy in copies:
        copy.wait()
    own_factors(place_ref[0], rate_ref, scale_ref, tip_ref, fix_ref, solve_ref, wide_ref)
    for step in range(TOTAL // CHUNK):
        lanes = slice(step * CHUNK, (step + 1) * CHUNK)
        plane, high, low = halves(cell_ref[:, lanes])
        table_ref[...] = span_table(high, low)
        at = jnp.dot(bf_ref[...], table_ref[...], preferred_element_type=F32)
        mask = lax.broadcasted_iota(jnp.int32, (PLANES, CHUNK), 0) == plane
        for n in range(3):
            fluid_ref[n : n + 1, lanes] = jnp.sum(
                jnp.where(mask, at[n * PLANES : (n + 1) * PLANES], 0.0), axis=0, keepdims=True
            )


def find(place, vel_held, cells, rate):
    return pl.pallas_call(
        find_kernel,
        out_shape=(
            far_out(3, TOTAL),
            far_out(ROWS, 128),
            far_out(4, ROWS, 128),
            far_out(4, ROWS, 128),
            far_out(ROWS, 128),
        ),
        in_specs=[SMEM, VMEM, ANY, ANY],
        out_specs=(VMEM,) * 5,
        scratch_shapes=[
            pltpu.VMEM((3 * PLANES, CZ), BF16),
            pltpu.VMEM((CZ, CHUNK), BF16),
            pltpu.VMEM((1, TOTAL), jnp.int32),
            pltpu.VMEM((8, 128), F32),
            pltpu.VMEM((ROWS, 128), F32),
            pltpu.SemaphoreType.DMA((2,)),
        ],
        compiler_params=params(28),
        name="find",
    )(place, vel_held, *far_in(cells, rate))


def main_kernel(
    below_hbm, above_hbm, before_hbm, behind_hbm, moved_hbm,
    fluid_hbm, scale_hbm, tip_hbm, vel_hbm, section_hbm, count_hbm, cell_hbm, near_hbm, far_hbm,
    part_hbm, tips_hbm, new_ref,
    pad_ref, before_ref, behind_ref, section_ref, table_ref, got_ref, deposit_ref, moved_ref,
    count_ref, cell_ref, near_ref, far_ref, part_ref, tips_ref, coef_ref,
    fluid_ref, scale_ref, tip_ref, sems,
):
    sources = [
        (cell_hbm, cell_ref),
        (moved_hbm, moved_ref),
        (count_hbm, count_ref),
        (fluid_hbm, fluid_ref),
        (scale_hbm, scale_ref),
        (tip_hbm, tip_ref),
        (near_hbm, near_ref),
        (far_hbm, far_ref),
        (vel_hbm, pad_ref.at[:, :, 8 : 8 + ROWS, :]),
        (below_hbm, pad_ref.at[:, :, 6:8, :]),
        (above_hbm, pad_ref.at[:, :, 8 + ROWS : 10 + ROWS, :]),
        (before_hbm, before_ref),
        (behind_hbm, behind_ref),
        (section_hbm, section_ref),
    ]
    copies = [pltpu.make_async_copy(a, b, sems.at[n]) for n, (a, b) in enumerate(sources)]
    for copy in copies:
        copy.start()
    steps = TOTAL // CHUNK

    def lanes_of(step):
        return slice(step * CHUNK, (step + 1) * CHUNK)

    def spread_of(step):
        lanes = lanes_of(step)
        plane, high, low = halves(cell_ref[:, lanes])
        table_ref[...] = span_table(high, low)
        mask = lax.broadcasted_iota(jnp.int32, (PLANES, CHUNK), 0) == plane
        mask = mask.astype(F32).astype(BF16)
        live = got_ref[4:5, lanes] > 0.5
        rate = got_ref[3:4, lanes]
        spread = []
        for n in range(3):
            old = got_ref[n : n + 1, lanes]
            relative = fluid_ref[n : n + 1, lanes] - old
            part_ref[n : n + 1, lanes] = jnp.where(live, old + TIME_STEP * rate * relative, 0.0)
            push = jnp.where(live, -rate * relative, 0.0).astype(BF16)
            spread.append(mask * push)
        return jnp.concatenate(spread, axis=0)

    def unpack():
        left = lax.broadcasted_iota(jnp.int32, (1, 128), 1) < SLOTS
        lane = lax.broadcasted_iota(jnp.int32, (1, 128), 1)
        for r in range(PEERS // 2):
            lanes = slice(128 * r, 128 * r + 128)
            for n in range(2):
                one = moved_ref[2 * r, n : n + 1, :]
                two = moved_ref[2 * r + 1, n : n + 1, :]
                got_ref[2 * n : 2 * n + 1, lanes] = jnp.where(left, one, pltpu.roll(two, SLOTS, 1))
                got_ref[2 * n + 1 : 2 * n + 2, lanes] = jnp.where(
                    left, pltpu.roll(one, SLOTS, 1), two
                )
            limit = jnp.where(left, count_ref[0, 2 * r], count_ref[0, 2 * r + 1])
            got_ref[4:5, lanes] = ((lane & (SLOTS - 1)) < limit).astype(F32)

    def tiled(column, times):
        return jnp.concatenate([column] * times, axis=1)

    def stencil(c, x):
        def layer(i, top):
            if i < 0:
                return before_ref[c, 2 + i, top : top + 8, :]
            if i >= CX:
                return behind_ref[c, i - CX, top : top + 8, :]
            return pad_ref[c, i, 8 + top : 16 + top, :]

        for t in range(ROWS // 8):
            top = 8 * t
            here = layer(x, top)
            ddx = (8.0 / 12.0) * (layer(x + 1, top) - layer(x - 1, top)) - (1.0 / 12.0) * (
                layer(x + 2, top) - layer(x - 2, top)
            )
            rolled = {k: pltpu.roll(here, (-k) % CZ, 1) for k in (1, -1, 2, -2)}
            ddz = (8.0 / 12.0) * (rolled[1] - rolled[-1]) - (1.0 / 12.0) * (rolled[2] - rolled[-2])

            def shifted(k):
                return pad_ref[c, x, 8 + top + k : 16 + top + k, :]

            near = tiled(coef_ref[0, top : top + 8, :], 8)
            far = tiled(coef_ref[1, top : top + 8, :], 8)
            ddy = near * (shifted(1) - shifted(-1)) + far * (shifted(2) - shifted(-2))
            moved = (
                pad_ref[0, x, 8 + top : 16 + top, :] * ddx
                + pad_ref[1, x, 8 + top : 16 + top, :] * ddy
                + pad_ref[2, x, 8 + top : 16 + top, :] * ddz
            )
            new_ref[c, x, top : top + 8, :] = (
                SECTION_KEEP * section_ref[c, x, top : top + 8, :] - TIME_STEP * moved
            )

    planes = [(c, x) for c in range(3) for x in range(CX)]
    share = len(planes) // (steps - 1)
    for copy in copies[:4]:
        copy.wait()
    unpack()
    for step in range(steps):
        spread = spread_of(step)
        if step > 0:
            for c, x in planes[share * (step - 1) : share * step]:
                stencil(c, x)
        last = step == steps - 1
        wide = CZ // 4 if last else CZ
        for z in range(0, CZ, wide):
            new = lax.dot_general(
                spread, table_ref[z : z + wide, :], (((1,), (1,)), ((), ())),
                preferred_element_type=F32,
            )
            if step == 0:
                deposit_ref[...] = new
                continue
            if not last:
                deposit_ref[...] += new
                continue
            for c, x in planes:
                base = c * PLANES + x * ROWS
                total = [None] * 4
                for t in range(ROWS // 8):
                    top = 8 * t
                    full = new_ref[c, x, top : top + 8, z : z + wide] + TIME_STEP * (
                        deposit_ref[base + top : base + top + 8, z : z + wide]
                        + new[base + top : base + top + 8]
                    )
                    new_ref[c, x, top : top + 8, z : z + wide] = full
                    scaled = full * tiled(scale_ref[top : top + 8, :], wide // 128)
                    for r in range(4):
                        weighted = scaled * tiled(tip_ref[r, top : top + 8, :], wide // 128)
                        total[r] = weighted if t == 0 else total[r] + weighted
                for r in range(4):
                    summed = jnp.sum(total[r], axis=0, keepdims=True)
                    for k in range(wide // 128):
                        tips_ref[8 * x + z // 128 + k, c, r : r + 1, :] = summed[
                            :, 128 * k : 128 * k + 128
                        ]
        if step == 0:
            for copy in copies[4:]:
                copy.wait()
            coef_ref[0] = column_of(near_ref[...], ROWS)
            coef_ref[1] = column_of(far_ref[...], ROWS)
    stores = [
        pltpu.make_async_copy(tips_ref, tips_hbm, sems.at[14]),
        pltpu.make_async_copy(part_ref, part_hbm, sems.at[15]),
    ]
    for copy in stores:
        copy.start()
    for copy in stores:
        copy.wait()


def main_part(halos, moved, others):
    return pl.pallas_call(
        main_kernel,
        out_shape=(
            far_out(3, TOTAL),
            far_out(SLABS, 3, 4, 128),
            held((3, CX, ROWS, CZ)),
        ),
        in_specs=[ANY] * 14,
        out_specs=(ANY, ANY, VMEM),
        scratch_shapes=[
            pltpu.VMEM((3, CX, ROWS + 16, CZ), F32),
            pltpu.VMEM((3, 2, ROWS, CZ), F32),
            pltpu.VMEM((3, 2, ROWS, CZ), F32),
            pltpu.VMEM((3, CX, ROWS, CZ), F32),
            pltpu.VMEM((CZ, CHUNK), BF16),
            pltpu.VMEM((8, TOTAL), F32),
            pltpu.VMEM((3 * PLANES, CZ), F32),
            pltpu.VMEM((PEERS, 2, 128), F32),
            pltpu.SMEM((1, PEERS), jnp.int32),
            pltpu.VMEM((1, TOTAL), jnp.int32),
            pltpu.VMEM((1, ROWS), F32),
            pltpu.VMEM((1, ROWS), F32),
            pltpu.VMEM((3, TOTAL), F32),
            pltpu.VMEM((SLABS, 3, 4, 128), F32),
            pltpu.VMEM((2, ROWS, 128), F32),
            pltpu.VMEM((3, TOTAL), F32),
            pltpu.VMEM((ROWS, 128), F32),
            pltpu.VMEM((4, ROWS, 128), F32),
            pltpu.SemaphoreType.DMA((16,)),
        ],
        compiler_params=params(36),
        name="main_part",
    )(*halos, moved, *far_in(*others))


WIDTH = 3 * CX * CZ // SLABS


def solve_kernel(tips_ref, green_ref, out_ref, all_ref):
    for s in range(SLABS):
        for c in range(3):
            all_ref[4 * s : 4 * s + 4, 128 * c : 128 * c + 128] = tips_ref[s, c]
    found = jnp.dot(green_ref[...], all_ref[...], precision=HIGH, preferred_element_type=F32)
    for s in range(SLABS):
        for c in range(3):
            out_ref[s, c] = found[4 * s : 4 * s + 4, 128 * c : 128 * c + 128]


def solved(tips, green):
    return pl.pallas_call(
        solve_kernel,
        out_shape=shaped(SLABS, 3, 4, 128),
        in_specs=[VMEM, VMEM],
        out_specs=VMEM,
        scratch_shapes=[pltpu.VMEM((4 * SLABS, WIDTH), F32)],
        compiler_params=params(4),
        name="solve",
    )(tips, green)


def local_kernel(vel_hbm, section_ref, scale_ref, solve_ref, section_hbm, out_ref, sems):
    loads = [pltpu.make_async_copy(vel_hbm.at[c], out_ref.at[c], sems.at[c]) for c in range(3)]
    for load in loads:
        load.start()
    store = pltpu.make_async_copy(section_ref, section_hbm, sems.at[3])
    store.start()
    whole = solve_ref[:, 0:ROWS]
    head = whole.astype(BF16)
    rest = (whole - head.astype(F32)).astype(BF16)
    left = jnp.concatenate([head, rest, head], axis=1)
    scale = jnp.concatenate([scale_ref[...]] * 8, axis=1)
    for c in range(3):
        loads[c].wait()
        for x in range(CX):
            value = section_ref[c, x] * scale
            high = value.astype(BF16)
            low = (value - high.astype(F32)).astype(BF16)
            right = jnp.concatenate([high, high, low], axis=0)
            out_ref[c, x] += jnp.dot(left, right, preferred_element_type=F32)
    store.wait()


def local_solve(velocity, section_new, scale, solve):
    return pl.pallas_call(
        local_kernel,
        out_shape=(far_out(3, CX, ROWS, CZ), held((3, CX, ROWS, CZ))),
        in_specs=[ANY, VMEM, VMEM, VMEM],
        out_specs=(ANY, VMEM),
        scratch_shapes=[pltpu.SemaphoreType.DMA((4,))],
        compiler_params=params(16),
        name="local_solve",
    )(*far_in(velocity), section_new, scale, solve)


def final_kernel(partial_ref, edge_ref, fix_ref, out_hbm, out_ref, sems):
    stores = []
    for c in range(3):
        for x in range(CX):
            for t in range(CZ // 128):
                lanes = slice(128 * t, 128 * t + 128)
                edge = edge_ref[8 * x + t, c]
                value = partial_ref[c, x, :, lanes]
                for r in range(4):
                    value = value - fix_ref[r] * edge[r : r + 1, :]
                out_ref[c, x, :, lanes] = value
            if x % 2 == 1:
                span = pl.ds(x - 1, 2)
                stores.append(
                    pltpu.make_async_copy(
                        out_ref.at[c, span], out_hbm.at[c, span], sems.at[len(stores)]
                    )
                )
                stores[-1].start()
    for copy in stores:
        copy.wait()


def finished(partial, edges, fix):
    return pl.pallas_call(
        final_kernel,
        out_shape=far_out(3, CX, ROWS, CZ),
        in_specs=[VMEM] * 3,
        out_specs=ANY,
        scratch_shapes=[pltpu.VMEM((3, CX, ROWS, CZ), F32), pltpu.SemaphoreType.DMA((6,))],
        compiler_params=params(16),
        name="finish",
    )(partial, edges, fix)


def local(velocity, section, diffusion, rhs_near, rhs_far, part_vel, part_rate, counts, cell_slot):
    n_gx, n_gy = lax.axis_size("gx"), lax.axis_size("gy")
    up_x = [(i, (i + 1) % n_gx) for i in range(n_gx)]
    down_x = [(t, s) for s, t in up_x]
    up_y = [(i, i + 1) for i in range(n_gy - 1)]
    down_y = [(t, s) for s, t in up_y]
    high, low, top, bottom, packed, vel_held = prepared(
        velocity, part_vel, part_rate.reshape(1, TOTAL)
    )
    before = lax.ppermute(high, "gx", up_x)
    behind = lax.ppermute(low, "gx", down_x)
    below = lax.ppermute(top, "gy", up_y)
    above = lax.ppermute(bottom, "gy", down_y)
    moved = lax.all_to_all(packed, ("gx", "gy"), split_axis=0, concat_axis=0, tiled=True)
    place = lax.axis_index("gy").astype(jnp.int32).reshape(1)
    fluid, scale, tip, fix, solve = find(place, vel_held, cell_slot, diffusion.reshape(8, 128))
    part_new, tips, new_held = main_part(
        (below, above, before, behind), moved,
        (fluid, scale, tip, velocity, section, counts, cell_slot, rhs_near.reshape(1, ROWS), rhs_far.reshape(1, ROWS)),
    )
    tips, diffusion = lax.optimization_barrier((tips, diffusion))
    all_tips = lax.all_to_all(tips, "gy", split_axis=0, concat_axis=0, tiled=True)
    rate = jnp.pad(
        diffusion.reshape(SLABS, ROWS).T, ((0, 0), (0, 128 - SLABS)), constant_values=1000.0
    )
    reply = solved(all_tips, green_operator(rate))
    reply, solve = lax.optimization_barrier((reply, solve))
    edges = lax.all_to_all(reply, "gy", split_axis=0, concat_axis=0, tiled=True)
    section_new, partial = local_solve(velocity, new_held, scale, solve)
    velocity_new = finished(partial, edges, fix)
    return (velocity_new, section_new, part_new)


def solution(mesh):
    return jax.shard_map(
        local,
        mesh=mesh,
        in_specs=(
            P(None, "gx", "gy", None),
            P(None, "gx", "gy", None),
            P(),
            P("gy"),
            P("gy"),
            P(None, ("gx", "gy")),
            P(("gx", "gy")),
            P(("gx", "gy"), None),
            P(("gx", "gy"), None),
        ),
        out_specs=(P(None, "gx", "gy", None), P(None, "gx", "gy", None), P(None, ("gx", "gy"))),
        check_vma=False,
    )
```

```python
import jax
import jax.numpy as jnp
from jax import lax
from jax.experimental import pallas as pl
from jax.experimental.pallas import tpu as pltpu
from jax.sharding import PartitionSpec as P

TIME_STEP = 0.2
SECTION_KEEP = -5.0 / 9.0
SECTION_GAIN = 15.0 / 16.0
MAIN = 2.5
NEAR = -4.0 / 3.0
FAR = 1.0 / 12.0
SLABS = 32
ROWS = 32
CX = 4
CZ = 1024
PLANES = CX * ROWS
SLOTS = 64
PEERS = 128
TOTAL = PEERS * SLOTS
CHUNK = 2048
HIGH = lax.Precision.HIGHEST
F32 = jnp.float32
BF16 = jnp.bfloat16


def params(mib=60):
    return pltpu.CompilerParams(vmem_limit_bytes=mib * 1024 * 1024)


VMEM = pl.BlockSpec(memory_space=pltpu.MemorySpace.VMEM)
SMEM = pl.BlockSpec(memory_space=pltpu.MemorySpace.SMEM)
ANY = pl.BlockSpec(memory_space=pltpu.MemorySpace.HBM)


def held(shape, dtype=F32):
    return pltpu.MemorySpace.VMEM(shape, dtype)


def shaped(*shape):
    return jax.ShapeDtypeStruct(shape, F32)


def far_out(*shape):
    return pltpu.MemorySpace.HBM(shape, F32)


def far_in(*arrays):
    return [pltpu.with_memory_space_constraint(a, pltpu.MemorySpace.HBM) for a in arrays]


def mm(a, b):
    return tuple(
        tuple(a[i][0] * b[0][j] + a[i][1] * b[1][j] for j in range(2)) for i in range(2)
    )


def add(a, b, sign=1.0):
    return tuple(tuple(a[i][j] + sign * b[i][j] for j in range(2)) for i in range(2))


def neg(a):
    return tuple(tuple(-e for e in row) for row in a)


def each(a, fn):
    return tuple(tuple(fn(e) for e in row) for row in a)


def inverse_of_one_minus(a):
    p, q, r, s = 1.0 - a[0][0], -a[0][1], -a[1][0], 1.0 - a[1][1]
    scale = 1.0 / (p * s - q * r)
    return ((s * scale, -q * scale), (-r * scale, p * scale))


def ldl(main_of, zero):
    recip, low1, low2 = [], [], []
    for k in range(ROWS):
        main = main_of(k)
        if k == 0:
            low1.append(zero)
            low2.append(zero)
            recip.append(1.0 / main)
            continue
        edge = NEAR - FAR * low1[k - 1]
        one = edge * recip[k - 1]
        two = FAR * recip[k - 2] if k > 1 else zero
        low1.append(one)
        low2.append(two)
        recip.append(1.0 / (main - edge * one - FAR * two))
    return recip, low1, low2


def substitute(rows, recip, low1, low2):
    half = []
    for k in range(ROWS):
        value = rows[k]
        if k > 0:
            value = value - low1[k] * half[k - 1]
        if k > 1:
            value = value - low2[k] * half[k - 2]
        half.append(value)
    full = [None] * ROWS
    for k in reversed(range(ROWS)):
        value = half[k] * recip[k]
        if k < ROWS - 1:
            value = value - low1[k + 1] * full[k + 1]
        if k < ROWS - 2:
            value = value - low2[k + 2] * full[k + 2]
        full[k] = value
    return full


ENDS = (0, 1, ROWS - 2, ROWS - 1)


def own_factors(slab, rate_ref, scale_ref, tip_ref, fix_ref, solve_ref, wide_ref):
    lane8 = lax.broadcasted_iota(jnp.int32, (8, 128), 1)
    row = rate_ref[pl.ds(slab // 4, 1), :]
    row = pltpu.roll(jnp.broadcast_to(row, (8, 128)), 128 - ROWS * (slab % 4), 1)
    inv_rate = 1.0 / column_of(row[0:1, 0:ROWS], ROWS)
    scale_ref[...] = SECTION_GAIN * inv_rate
    wide_ref[...] = inv_rate + MAIN
    recip, low1, low2 = ldl(
        lambda k: jnp.broadcast_to(wide_ref[k : k + 1, :], (8, 128)), jnp.zeros((8, 128), F32)
    )
    full = substitute([(lane8 == k).astype(F32) for k in range(ROWS)], recip, low1, low2)
    for k in range(ROWS):
        solve_ref[k : k + 1, :] = full[k][0:1]
    solve = solve_ref[...]
    cols = [jnp.broadcast_to(solve[:, n : n + 1], (ROWS, 128)) for n in ENDS]
    for n in range(4):
        tip_ref[n] = cols[n]
    has_low = jnp.where(slab > 0, 1.0, 0.0)
    has_high = jnp.where(slab < SLABS - 1, 1.0, 0.0)
    fix_ref[0] = FAR * cols[0] * has_low
    fix_ref[1] = (NEAR * cols[0] + FAR * cols[1]) * has_low
    fix_ref[2] = (FAR * cols[2] + NEAR * cols[3]) * has_high
    fix_ref[3] = FAR * cols[3] * has_high


def green_kernel(rate_ref, green_ref, wide_ref, coef_ref):
    lane8 = lax.broadcasted_iota(jnp.int32, (8, 128), 1)
    sub8 = lax.broadcasted_iota(jnp.int32, (8, 128), 0)
    wide_ref[...] = 1.0 / rate_ref[...] + MAIN
    zero = jnp.zeros((8, 128), F32)
    recip, low1, low2 = ldl(lambda k: jnp.broadcast_to(wide_ref[k : k + 1, :], (8, 128)), zero)
    units = [(sub8 == ENDS.index(k)).astype(F32) if k in ENDS else zero for k in range(ROWS)]
    full = substitute(units, recip, low1, low2)

    def entry(k, i):
        return jnp.broadcast_to(full[k][i : i + 1, :], (8, 128))

    not_first = ((lane8 > 0) & (lane8 < SLABS)).astype(F32)
    not_last = (lane8 < SLABS - 1).astype(F32)

    def lower(k):
        s0, s1 = entry(k, 0), entry(k, 1)
        return (FAR * s0 * not_first, (NEAR * s0 + FAR * s1) * not_first)

    def upper(k):
        s2, s3 = entry(k, 2), entry(k, 3)
        return ((FAR * s2 + NEAR * s3) * not_last, FAR * s3 * not_last)

    low_a = (lower(ENDS[0]), lower(ENDS[1]))
    low_c = (lower(ENDS[2]), lower(ENDS[3]))
    up_b = (upper(ENDS[0]), upper(ENDS[1]))
    up_e = (upper(ENDS[2]), upper(ENDS[3]))
    a, b, c, e = low_a, up_b, low_c, up_e
    for hop in (1, 2, 4, 8, 16):
        ax, bx, cx, ex = (each(m, lambda v: pltpu.roll(v, hop, 1)) for m in (a, b, c, e))
        w = inverse_of_one_minus(mm(a, ex))
        wa_c = mm(w, mm(a, cx))
        wb = mm(w, b)
        cy_ex = mm(c, ex)
        new_e = add(e, mm(cy_ex, wb))
        new_c = neg(add(mm(c, cx), mm(cy_ex, wa_c)))
        new_a = add(ax, mm(bx, wa_c))
        new_b = neg(mm(bx, wb))
        joined = lane8 >= hop

        def pick(new, old):
            return tuple(
                tuple(jnp.where(joined, new[i][j], old[i][j]) for j in range(2)) for i in range(2)
            )

        a, b, c, e = pick(new_a, a), pick(new_b, b), pick(new_c, c), pick(new_e, e)
    q = e
    q_prev = each(q, lambda v: jnp.where(lane8 > 0, pltpu.roll(v, 1, 1), 0.0))
    z = inverse_of_one_minus(mm(low_a, q_prev))
    gain = mm(mm(low_c, q_prev), z)
    carry = add(low_c, mm(gain, low_a))
    z_low = mm(z, low_a)
    z_up = mm(z, up_b)
    for group, mats in enumerate(((carry, gain), (z, z_low), (z_up, q))):
        block = jnp.zeros((8, 128), F32)
        for n, m in enumerate(mats):
            for i in range(2):
                for j in range(2):
                    block = jnp.where(sub8 == 4 * n + 2 * i + j, m[i][j], block)
        for s in range(SLABS):
            coef_ref[s, 8 * group : 8 * group + 8, :] = jnp.broadcast_to(block[:, s : s + 1], (8, 128))

    def coef(s, n):
        def one(i, j):
            at = 4 * n + 2 * i + j
            return jnp.broadcast_to(coef_ref[s, at : at + 1, :], (8, 128))

        return tuple(tuple(one(i, j) for j in range(2)) for i in range(2))

    def at_lane(n):
        return lane8 == n

    forward = []
    prev = None
    for s in range(SLABS):
        m, g = coef(s, 0), coef(s, 1)
        now = []
        for i in range(2):
            value = jnp.where(at_lane(4 * s), g[i][0], 0.0)
            value = jnp.where(at_lane(4 * s + 1), g[i][1], value)
            value = jnp.where(at_lane(4 * s + 2 + i), 1.0, value)
            if prev is not None:
                value = value - m[i][0] * prev[0] - m[i][1] * prev[1]
            now.append(value)
        forward.append(now)
        prev = now
    for row in (0, 1, 4 * SLABS - 2, 4 * SLABS - 1):
        green_ref[row : row + 1, :] = jnp.zeros((1, 128), F32)
    after = None
    for s in reversed(range(SLABS)):
        zc, zl, zu, qc = coef(s, 2), coef(s, 3), coef(s, 4), coef(s, 5)
        now = []
        for i in range(2):
            value = jnp.where(at_lane(4 * s), zc[i][0], 0.0)
            value = jnp.where(at_lane(4 * s + 1), zc[i][1], value)
            if s > 0:
                value = value - zl[i][0] * forward[s - 1][0] - zl[i][1] * forward[s - 1][1]
            if after is not None:
                value = value - zu[i][0] * after[0] - zu[i][1] * after[1]
            now.append(value)
        if s < SLABS - 1:
            for i in range(2):
                high = forward[s][i] - qc[i][0] * after[0] - qc[i][1] * after[1]
                green_ref[4 * (s + 1) + i : 4 * (s + 1) + i + 1, :] = high[0:1]
        if s > 0:
            for i in range(2):
                green_ref[4 * (s - 1) + 2 + i : 4 * (s - 1) + 3 + i, :] = now[i][0:1]
        after = now


def green_operator(rate):
    return pl.pallas_call(
        green_kernel,
        out_shape=shaped(128, 128),
        in_specs=[VMEM],
        out_specs=VMEM,
        scratch_shapes=[pltpu.VMEM((ROWS, 128), F32), pltpu.VMEM((SLABS, 24, 128), F32)],
        compiler_params=params(4),
        name="green_operator",
    )(rate)


def pre_kernel(
    place_ref, vel_hbm, part_hbm, rate_hbm, high_hbm, low_hbm, inner_hbm, outer_hbm, packed_hbm,
    vel_ref, part_ref, rate_ref, out_ref, sems,
):
    even = place_ref[0] % 2 == 0
    into = [
        pltpu.make_async_copy(vel_hbm.at[:, 2:4], vel_ref.at[:, 2:4], sems.at[0]),
        pltpu.make_async_copy(vel_hbm.at[:, 0:2], vel_ref.at[:, 0:2], sems.at[1]),
        pltpu.make_async_copy(part_hbm, part_ref, sems.at[2]),
        pltpu.make_async_copy(rate_hbm, rate_ref, sems.at[3]),
    ]
    for copy in into:
        copy.start()
    out = [
        pltpu.make_async_copy(vel_ref.at[:, 2:4], high_hbm, sems.at[4]),
        pltpu.make_async_copy(vel_ref.at[:, 0:2], low_hbm, sems.at[5]),
        pltpu.make_async_copy(vel_ref.at[:, :, ROWS - 2 : ROWS], inner_hbm, sems.at[6]),
        pltpu.make_async_copy(vel_ref.at[:, :, 0:2], outer_hbm, sems.at[7]),
        pltpu.make_async_copy(out_ref, packed_hbm, sems.at[8]),
    ]
    into[2].wait()
    into[3].wait()
    left = lax.broadcasted_iota(jnp.int32, (1, 128), 1) < SLOTS
    for r in range(PEERS // 2):
        part = [part_ref[i : i + 1, 128 * r : 128 * r + 128] for i in range(3)]
        part.append(rate_ref[0:1, 128 * r : 128 * r + 128])
        for n in range(2):
            one, two = part[2 * n], part[2 * n + 1]
            out_ref[2 * r, n : n + 1, :] = jnp.where(left, one, pltpu.roll(two, SLOTS, 1))
            out_ref[2 * r + 1, n : n + 1, :] = jnp.where(left, pltpu.roll(one, SLOTS, 1), two)
    out[4].start()
    into[0].wait()
    out[0].start()
    into[1].wait()
    out[1].start()

    @pl.when(even)
    def _():
        out[2].start()
        out[3].start()

    @pl.when(jnp.logical_not(even))
    def _():
        pltpu.make_async_copy(vel_ref.at[:, :, 0:2], inner_hbm, sems.at[6]).start()
        pltpu.make_async_copy(vel_ref.at[:, :, ROWS - 2 : ROWS], outer_hbm, sems.at[7]).start()

    for copy in out:
        copy.wait()


def prepared(place, velocity, part_vel, part_rate):
    return pl.pallas_call(
        pre_kernel,
        out_shape=(
            far_out(3, 2, ROWS, CZ),
            far_out(3, 2, ROWS, CZ),
            far_out(3, CX, 2, CZ),
            far_out(3, CX, 2, CZ),
            far_out(PEERS, 2, 128),
            held((3, CX, ROWS, CZ)),
        ),
        in_specs=[SMEM] + [ANY] * 3,
        out_specs=(ANY,) * 5 + (VMEM,),
        scratch_shapes=[
            pltpu.VMEM((3, TOTAL), F32),
            pltpu.VMEM((1, TOTAL), F32),
            pltpu.VMEM((PEERS, 2, 128), F32),
            pltpu.SemaphoreType.DMA((9,)),
        ],
        compiler_params=params(16),
        name="prepare",
    )(place, *far_in(velocity, part_vel, part_rate))


def halves(cells):
    plane = cells >> 10
    span = cells & (CZ - 1)
    return plane, span >> 7, span & 127


def span_table(high, low):
    width = high.shape[1]
    inner = lax.broadcasted_iota(jnp.int32, (128, width), 0) == low
    inner = inner.astype(F32).astype(BF16)
    rows = []
    for t in range(8):
        flag = (high == t).astype(F32).astype(BF16)
        rows.append(inner * flag)
    return jnp.concatenate(rows, axis=0)


def column_of(row, length):
    wide = jnp.broadcast_to(row, (length, length))
    here = lax.broadcasted_iota(jnp.int32, (length, length), 0) == lax.broadcasted_iota(
        jnp.int32, (length, length), 1
    )
    return jnp.broadcast_to(
        jnp.sum(jnp.where(here, wide, 0.0), axis=1, keepdims=True), (length, 128)
    )


def find_kernel(
    place_ref, vel_ref, cell_hbm, rate_hbm, *refs,
):
    outs, held_refs = refs[:5], refs[5:10]
    fluid_ref, scale_ref, tip_ref, fix_ref, solve_ref = held_refs
    bf_ref, table_ref, cell_ref, rate_ref, wide_ref, sems = refs[10:]
    copies = [
        pltpu.make_async_copy(cell_hbm, cell_ref, sems.at[0]),
        pltpu.make_async_copy(rate_hbm, rate_ref, sems.at[1]),
    ]
    for copy in copies:
        copy.start()
    for c in range(3):
        for x in range(CX):
            top = c * PLANES + x * ROWS
            bf_ref[top : top + ROWS, :] = vel_ref[c, x].astype(BF16)
    for copy in copies:
        copy.wait()
    own_factors(place_ref[0], rate_ref, scale_ref, tip_ref, fix_ref, solve_ref, wide_ref)
    stores = [
        pltpu.make_async_copy(held_refs[n], outs[n], sems.at[1 + n]) for n in range(1, 5)
    ]
    for store in stores:
        store.start()
    for step in range(TOTAL // CHUNK):
        lanes = slice(step * CHUNK, (step + 1) * CHUNK)
        plane, high, low = halves(cell_ref[:, lanes])
        table_ref[...] = span_table(high, low)
        at = jnp.dot(bf_ref[...], table_ref[...], preferred_element_type=F32)
        mask = lax.broadcasted_iota(jnp.int32, (PLANES, CHUNK), 0) == plane
        for n in range(3):
            fluid_ref[n : n + 1, lanes] = jnp.sum(
                jnp.where(mask, at[n * PLANES : (n + 1) * PLANES], 0.0), axis=0, keepdims=True
            )
        stores.append(
            pltpu.make_async_copy(
                fluid_ref.at[:, lanes], outs[0].at[:, lanes], sems.at[6 + step]
            )
        )
        stores[-1].start()
    for store in stores:
        store.wait()


def find(place, vel_held, cells, rate):
    return pl.pallas_call(
        find_kernel,
        out_shape=(
            far_out(3, TOTAL),
            far_out(ROWS, 128),
            far_out(4, ROWS, 128),
            far_out(4, ROWS, 128),
            far_out(ROWS, 128),
        ),
        in_specs=[SMEM, VMEM, ANY, ANY],
        out_specs=(ANY,) * 5,
        scratch_shapes=[
            pltpu.VMEM((3, TOTAL), F32),
            pltpu.VMEM((ROWS, 128), F32),
            pltpu.VMEM((4, ROWS, 128), F32),
            pltpu.VMEM((4, ROWS, 128), F32),
            pltpu.VMEM((ROWS, 128), F32),
            pltpu.VMEM((3 * PLANES, CZ), BF16),
            pltpu.VMEM((CZ, CHUNK), BF16),
            pltpu.VMEM((1, TOTAL), jnp.int32),
            pltpu.VMEM((8, 128), F32),
            pltpu.VMEM((ROWS, 128), F32),
            pltpu.SemaphoreType.DMA((6 + TOTAL // CHUNK,)),
        ],
        compiler_params=params(28),
        name="find",
    )(place, vel_held, *far_in(cells, rate))


def main_kernel(
    place_ref, inner_hbm, outer_hbm, before_hbm, behind_hbm, moved_hbm,
    fluid_hbm, scale_hbm, tip_hbm, vel_hbm, section_hbm, count_hbm, cell_hbm, near_hbm, far_hbm,
    part_hbm, tips_hbm, new_ref,
    pad_ref, before_ref, behind_ref, section_ref, table_ref, got_ref, deposit_ref, moved_ref,
    count_ref, cell_ref, near_ref, far_ref, part_ref, tips_ref, coef_ref,
    fluid_ref, scale_ref, tip_ref, sems,
):
    sources = [
        (cell_hbm, cell_ref),
        (moved_hbm, moved_ref),
        (count_hbm, count_ref),
        (fluid_hbm, fluid_ref),
        (scale_hbm, scale_ref),
        (tip_hbm, tip_ref),
        (near_hbm, near_ref),
        (far_hbm, far_ref),
        (vel_hbm, pad_ref.at[:, :, 8 : 8 + ROWS, :]),
        (inner_hbm, pad_ref.at[:, :, 6:8, :]),
        (outer_hbm, pad_ref.at[:, :, 8 + ROWS : 10 + ROWS, :]),
        (before_hbm, before_ref),
        (behind_hbm, behind_ref),
        (section_hbm, section_ref),
    ]
    copies = [pltpu.make_async_copy(a, b, sems.at[n]) for n, (a, b) in enumerate(sources)]
    swaps = [n for n, (a, b) in enumerate(sources) if a is inner_hbm or a is outer_hbm]
    for n, copy in enumerate(copies):
        if n not in swaps:
            copy.start()
    even = place_ref[0] % 2 == 0

    @pl.when(even)
    def _():
        for n, source in zip(swaps, (outer_hbm, inner_hbm)):
            pltpu.make_async_copy(source, sources[n][1], sems.at[n]).start()

    @pl.when(jnp.logical_not(even))
    def _():
        for n in swaps:
            copies[n].start()

    steps = TOTAL // CHUNK

    def lanes_of(step):
        return slice(step * CHUNK, (step + 1) * CHUNK)

    def spread_of(step):
        lanes = lanes_of(step)
        plane, high, low = halves(cell_ref[:, lanes])
        table_ref[...] = span_table(high, low)
        mask = lax.broadcasted_iota(jnp.int32, (PLANES, CHUNK), 0) == plane
        mask = mask.astype(F32).astype(BF16)
        live = got_ref[4:5, lanes] > 0.5
        rate = got_ref[3:4, lanes]
        spread = []
        for n in range(3):
            old = got_ref[n : n + 1, lanes]
            relative = fluid_ref[n : n + 1, lanes] - old
            part_ref[n : n + 1, lanes] = jnp.where(live, old + TIME_STEP * rate * relative, 0.0)
            push = jnp.where(live, -rate * relative, 0.0).astype(BF16)
            spread.append(mask * push)
        return jnp.concatenate(spread, axis=0)

    def unpack():
        left = lax.broadcasted_iota(jnp.int32, (1, 128), 1) < SLOTS
        lane = lax.broadcasted_iota(jnp.int32, (1, 128), 1)
        for r in range(PEERS // 2):
            lanes = slice(128 * r, 128 * r + 128)
            for n in range(2):
                one = moved_ref[2 * r, n : n + 1, :]
                two = moved_ref[2 * r + 1, n : n + 1, :]
                got_ref[2 * n : 2 * n + 1, lanes] = jnp.where(left, one, pltpu.roll(two, SLOTS, 1))
                got_ref[2 * n + 1 : 2 * n + 2, lanes] = jnp.where(
                    left, pltpu.roll(one, SLOTS, 1), two
                )
            limit = jnp.where(left, count_ref[0, 2 * r], count_ref[0, 2 * r + 1])
            got_ref[4:5, lanes] = ((lane & (SLOTS - 1)) < limit).astype(F32)

    def tiled(column, times):
        return jnp.concatenate([column] * times, axis=1)

    def stencil(c, x):
        def layer(i, top):
            if i < 0:
                return before_ref[c, 2 + i, top : top + 8, :]
            if i >= CX:
                return behind_ref[c, i - CX, top : top + 8, :]
            return pad_ref[c, i, 8 + top : 16 + top, :]

        for t in range(ROWS // 8):
            top = 8 * t
            here = layer(x, top)
            ddx = (8.0 / 12.0) * (layer(x + 1, top) - layer(x - 1, top)) - (1.0 / 12.0) * (
                layer(x + 2, top) - layer(x - 2, top)
            )
            rolled = {k: pltpu.roll(here, (-k) % CZ, 1) for k in (1, -1, 2, -2)}
            ddz = (8.0 / 12.0) * (rolled[1] - rolled[-1]) - (1.0 / 12.0) * (rolled[2] - rolled[-2])

            def shifted(k):
                return pad_ref[c, x, 8 + top + k : 16 + top + k, :]

            near = tiled(coef_ref[0, top : top + 8, :], 8)
            far = tiled(coef_ref[1, top : top + 8, :], 8)
            ddy = near * (shifted(1) - shifted(-1)) + far * (shifted(2) - shifted(-2))
            moved = (
                pad_ref[0, x, 8 + top : 16 + top, :] * ddx
                + pad_ref[1, x, 8 + top : 16 + top, :] * ddy
                + pad_ref[2, x, 8 + top : 16 + top, :] * ddz
            )
            new_ref[c, x, top : top + 8, :] = (
                SECTION_KEEP * section_ref[c, x, top : top + 8, :] - TIME_STEP * moved
            )

    planes = [(c, x) for c in range(3) for x in range(CX)]
    share = len(planes) // (steps - 1)
    for copy in copies[:4]:
        copy.wait()
    unpack()
    for step in range(steps):
        spread = spread_of(step)
        if step > 0:
            for c, x in planes[share * (step - 1) : share * step]:
                stencil(c, x)
        last = step == steps - 1
        if last:
            stores = [pltpu.make_async_copy(part_ref, part_hbm, sems.at[14])]
            stores[0].start()
        wide = CZ // 4 if last else CZ
        for z in range(0, CZ, wide):
            new = lax.dot_general(
                spread, table_ref[z : z + wide, :], (((1,), (1,)), ((), ())),
                preferred_element_type=F32,
            )
            if step == 0:
                deposit_ref[...] = new
                continue
            if not last:
                deposit_ref[...] += new
                continue
            for c, x in planes:
                base = c * PLANES + x * ROWS
                total = [None] * 4
                for t in range(ROWS // 8):
                    top = 8 * t
                    full = new_ref[c, x, top : top + 8, z : z + wide] + TIME_STEP * (
                        deposit_ref[base + top : base + top + 8, z : z + wide]
                        + new[base + top : base + top + 8]
                    )
                    new_ref[c, x, top : top + 8, z : z + wide] = full
                    scaled = full * tiled(scale_ref[top : top + 8, :], wide // 128)
                    for r in range(4):
                        weighted = scaled * tiled(tip_ref[r, top : top + 8, :], wide // 128)
                        total[r] = weighted if t == 0 else total[r] + weighted
                for r in range(4):
                    summed = jnp.sum(total[r], axis=0, keepdims=True)
                    for k in range(wide // 128):
                        tips_ref[8 * x + z // 128 + k, c, r : r + 1, :] = summed[
                            :, 128 * k : 128 * k + 128
                        ]
            for x in range(CX if last else 0):
                span = pl.ds(8 * x + z // 128, wide // 128)
                stores.append(
                    pltpu.make_async_copy(
                        tips_ref.at[span], tips_hbm.at[span], sems.at[14 + len(stores)]
                    )
                )
                stores[-1].start()
        if step == 0:
            for copy in copies[4:]:
                copy.wait()
            coef_ref[0] = column_of(near_ref[...], ROWS)
            coef_ref[1] = column_of(far_ref[...], ROWS)
    for store in stores:
        store.wait()


def main_part(place, halos, moved, others):
    return pl.pallas_call(
        main_kernel,
        out_shape=(
            far_out(3, TOTAL),
            far_out(SLABS, 3, 4, 128),
            held((3, CX, ROWS, CZ)),
        ),
        in_specs=[SMEM] + [ANY] * 14,
        out_specs=(ANY, ANY, VMEM),
        scratch_shapes=[
            pltpu.VMEM((3, CX, ROWS + 16, CZ), F32),
            pltpu.VMEM((3, 2, ROWS, CZ), F32),
            pltpu.VMEM((3, 2, ROWS, CZ), F32),
            pltpu.VMEM((3, CX, ROWS, CZ), F32),
            pltpu.VMEM((CZ, CHUNK), BF16),
            pltpu.VMEM((8, TOTAL), F32),
            pltpu.VMEM((3 * PLANES, CZ), F32),
            pltpu.VMEM((PEERS, 2, 128), F32),
            pltpu.SMEM((1, PEERS), jnp.int32),
            pltpu.VMEM((1, TOTAL), jnp.int32),
            pltpu.VMEM((1, ROWS), F32),
            pltpu.VMEM((1, ROWS), F32),
            pltpu.VMEM((3, TOTAL), F32),
            pltpu.VMEM((SLABS, 3, 4, 128), F32),
            pltpu.VMEM((2, ROWS, 128), F32),
            pltpu.VMEM((3, TOTAL), F32),
            pltpu.VMEM((ROWS, 128), F32),
            pltpu.VMEM((4, ROWS, 128), F32),
            pltpu.SemaphoreType.DMA((31,)),
        ],
        compiler_params=params(36),
        name="main_part",
    )(place, *halos, moved, *far_in(*others))


WIDTH = 3 * CX * CZ // SLABS


def solve_kernel(tips_ref, green_ref, out_ref, all_ref):
    for s in range(SLABS):
        for c in range(3):
            all_ref[4 * s : 4 * s + 4, 128 * c : 128 * c + 128] = tips_ref[s, c]
    found = jnp.dot(green_ref[...], all_ref[...], precision=HIGH, preferred_element_type=F32)
    for s in range(SLABS):
        for c in range(3):
            out_ref[s, c] = found[4 * s : 4 * s + 4, 128 * c : 128 * c + 128]


def solved(tips, green):
    return pl.pallas_call(
        solve_kernel,
        out_shape=shaped(SLABS, 3, 4, 128),
        in_specs=[VMEM, VMEM],
        out_specs=VMEM,
        scratch_shapes=[pltpu.VMEM((4 * SLABS, WIDTH), F32)],
        compiler_params=params(4),
        name="solve",
    )(tips, green)


def local_kernel(vel_hbm, section_ref, scale_ref, solve_ref, section_hbm, out_ref, sems):
    loads = [pltpu.make_async_copy(vel_hbm.at[c], out_ref.at[c], sems.at[c]) for c in range(3)]
    for load in loads:
        load.start()
    store = pltpu.make_async_copy(section_ref, section_hbm, sems.at[3])
    store.start()
    whole = solve_ref[:, 0:ROWS]
    head = whole.astype(BF16)
    rest = (whole - head.astype(F32)).astype(BF16)
    left = jnp.concatenate([head, rest, head], axis=1)
    scale = jnp.concatenate([scale_ref[...]] * 8, axis=1)
    for c in range(3):
        loads[c].wait()
        for x in range(CX):
            value = section_ref[c, x] * scale
            high = value.astype(BF16)
            low = (value - high.astype(F32)).astype(BF16)
            right = jnp.concatenate([high, high, low], axis=0)
            out_ref[c, x] += jnp.dot(left, right, preferred_element_type=F32)
    store.wait()


def local_solve(velocity, section_new, scale, solve):
    return pl.pallas_call(
        local_kernel,
        out_shape=(far_out(3, CX, ROWS, CZ), held((3, CX, ROWS, CZ))),
        in_specs=[ANY, VMEM, VMEM, VMEM],
        out_specs=(ANY, VMEM),
        scratch_shapes=[pltpu.SemaphoreType.DMA((4,))],
        compiler_params=params(16),
        name="local_solve",
    )(*far_in(velocity), section_new, scale, solve)


def final_kernel(partial_ref, edge_ref, fix_ref, out_hbm, out_ref, sems):
    stores = []
    for c in range(3):
        for x in range(CX):
            for t in range(CZ // 128):
                lanes = slice(128 * t, 128 * t + 128)
                edge = edge_ref[8 * x + t, c]
                value = partial_ref[c, x, :, lanes]
                for r in range(4):
                    value = value - fix_ref[r] * edge[r : r + 1, :]
                out_ref[c, x, :, lanes] = value
            if x % 2 == 1:
                span = pl.ds(x - 1, 2)
                stores.append(
                    pltpu.make_async_copy(
                        out_ref.at[c, span], out_hbm.at[c, span], sems.at[len(stores)]
                    )
                )
                stores[-1].start()
    for copy in stores:
        copy.wait()


def finished(partial, edges, fix):
    return pl.pallas_call(
        final_kernel,
        out_shape=far_out(3, CX, ROWS, CZ),
        in_specs=[VMEM] * 3,
        out_specs=ANY,
        scratch_shapes=[pltpu.VMEM((3, CX, ROWS, CZ), F32), pltpu.SemaphoreType.DMA((6,))],
        compiler_params=params(16),
        name="finish",
    )(partial, edges, fix)


def local(velocity, section, diffusion, rhs_near, rhs_far, part_vel, part_rate, counts, cell_slot):
    n_gx, n_gy = lax.axis_size("gx"), lax.axis_size("gy")
    up_x = [(i, (i + 1) % n_gx) for i in range(n_gx)]
    down_x = [(t, s) for s, t in up_x]
    place = lax.axis_index("gy").astype(jnp.int32).reshape(1)
    high, low, inner, outer, packed, vel_held = prepared(
        place, velocity, part_vel, part_rate.reshape(1, TOTAL)
    )
    before = lax.ppermute(high, "gx", up_x)
    behind = lax.ppermute(low, "gx", down_x)
    inner = lax.ppermute(inner, "gy", [(i, i ^ 1) for i in range(n_gy)])
    outer = lax.ppermute(
        outer, "gy", [pair for i in range(1, n_gy - 1, 2) for pair in ((i, i + 1), (i + 1, i))]
    )
    moved = lax.all_to_all(packed, ("gx", "gy"), split_axis=0, concat_axis=0, tiled=True)
    fluid, scale, tip, fix, solve = find(place, vel_held, cell_slot, diffusion.reshape(8, 128))
    part_new, tips, new_held = main_part(
        place, (inner, outer, before, behind), moved,
        (fluid, scale, tip, velocity, section, counts, cell_slot, rhs_near.reshape(1, ROWS), rhs_far.reshape(1, ROWS)),
    )
    tips, diffusion = lax.optimization_barrier((tips, diffusion))
    all_tips = lax.all_to_all(tips, "gy", split_axis=0, concat_axis=0, tiled=True)
    rate = jnp.pad(
        diffusion.reshape(SLABS, ROWS).T, ((0, 0), (0, 128 - SLABS)), constant_values=1000.0
    )
    reply = solved(all_tips, green_operator(rate))
    reply, solve = lax.optimization_barrier((reply, solve))
    edges = lax.all_to_all(reply, "gy", split_axis=0, concat_axis=0, tiled=True)
    section_new, partial = local_solve(velocity, new_held, scale, solve)
    velocity_new = finished(partial, edges, fix)
    return (velocity_new, section_new, part_new)


def solution(mesh):
    return jax.shard_map(
        local,
        mesh=mesh,
        in_specs=(
            P(None, "gx", "gy", None),
            P(None, "gx", "gy", None),
            P(),
            P("gy"),
            P("gy"),
            P(None, ("gx", "gy")),
            P(("gx", "gy")),
            P(("gx", "gy"), None),
            P(("gx", "gy"), None),
        ),
        out_specs=(P(None, "gx", "gy", None), P(None, "gx", "gy", None), P(None, ("gx", "gy"))),
        check_vma=False,
    )
```

```python
import jax
import jax.numpy as jnp
from jax import lax
from jax.experimental import pallas as pl
from jax.experimental.pallas import tpu as pltpu
from jax.sharding import PartitionSpec as P

TIME_STEP = 0.2
SECTION_KEEP = -5.0 / 9.0
SECTION_GAIN = 15.0 / 16.0
MAIN = 2.5
NEAR = -4.0 / 3.0
FAR = 1.0 / 12.0
SLABS = 32
ROWS = 32
CX = 4
CZ = 1024
PLANES = CX * ROWS
SLOTS = 64
PEERS = 128
TOTAL = PEERS * SLOTS
CHUNK = 2048
HIGH = lax.Precision.HIGHEST
F32 = jnp.float32
BF16 = jnp.bfloat16


def params(mib=60):
    return pltpu.CompilerParams(vmem_limit_bytes=mib * 1024 * 1024)


VMEM = pl.BlockSpec(memory_space=pltpu.MemorySpace.VMEM)
SMEM = pl.BlockSpec(memory_space=pltpu.MemorySpace.SMEM)
ANY = pl.BlockSpec(memory_space=pltpu.MemorySpace.HBM)


def held(shape, dtype=F32):
    return pltpu.MemorySpace.VMEM(shape, dtype)


def shaped(*shape):
    return jax.ShapeDtypeStruct(shape, F32)


def far_out(*shape):
    return pltpu.MemorySpace.HBM(shape, F32)


def far_in(*arrays):
    return [pltpu.with_memory_space_constraint(a, pltpu.MemorySpace.HBM) for a in arrays]


def mm(a, b):
    return tuple(
        tuple(a[i][0] * b[0][j] + a[i][1] * b[1][j] for j in range(2)) for i in range(2)
    )


def add(a, b, sign=1.0):
    return tuple(tuple(a[i][j] + sign * b[i][j] for j in range(2)) for i in range(2))


def neg(a):
    return tuple(tuple(-e for e in row) for row in a)


def each(a, fn):
    return tuple(tuple(fn(e) for e in row) for row in a)


def inverse_of_one_minus(a):
    p, q, r, s = 1.0 - a[0][0], -a[0][1], -a[1][0], 1.0 - a[1][1]
    scale = 1.0 / (p * s - q * r)
    return ((s * scale, -q * scale), (-r * scale, p * scale))


def ldl(main_of, zero):
    recip, low1, low2 = [], [], []
    for k in range(ROWS):
        main = main_of(k)
        if k == 0:
            low1.append(zero)
            low2.append(zero)
            recip.append(1.0 / main)
            continue
        edge = NEAR - FAR * low1[k - 1]
        one = edge * recip[k - 1]
        two = FAR * recip[k - 2] if k > 1 else zero
        low1.append(one)
        low2.append(two)
        recip.append(1.0 / (main - edge * one - FAR * two))
    return recip, low1, low2


def substitute(rows, recip, low1, low2):
    half = []
    for k in range(ROWS):
        value = rows[k]
        if k > 0:
            value = value - low1[k] * half[k - 1]
        if k > 1:
            value = value - low2[k] * half[k - 2]
        half.append(value)
    full = [None] * ROWS
    for k in reversed(range(ROWS)):
        value = half[k] * recip[k]
        if k < ROWS - 1:
            value = value - low1[k + 1] * full[k + 1]
        if k < ROWS - 2:
            value = value - low2[k + 2] * full[k + 2]
        full[k] = value
    return full


ENDS = (0, 1, ROWS - 2, ROWS - 1)


def own_factors(slab, rate_ref, scale_ref, tip_ref, fix_ref, solve_ref, wide_ref):
    lane8 = lax.broadcasted_iota(jnp.int32, (8, 128), 1)
    row = rate_ref[pl.ds(slab // 4, 1), :]
    row = pltpu.roll(jnp.broadcast_to(row, (8, 128)), 128 - ROWS * (slab % 4), 1)
    inv_rate = 1.0 / column_of(row[0:1, 0:ROWS], ROWS)
    scale_ref[...] = SECTION_GAIN * inv_rate
    wide_ref[...] = inv_rate + MAIN
    recip, low1, low2 = ldl(
        lambda k: jnp.broadcast_to(wide_ref[k : k + 1, :], (8, 128)), jnp.zeros((8, 128), F32)
    )
    full = substitute([(lane8 == k).astype(F32) for k in range(ROWS)], recip, low1, low2)
    for k in range(ROWS):
        solve_ref[k : k + 1, :] = full[k][0:1]
    solve = solve_ref[...]
    cols = [jnp.broadcast_to(solve[:, n : n + 1], (ROWS, 128)) for n in ENDS]
    for n in range(4):
        tip_ref[n] = cols[n]
    has_low = jnp.where(slab > 0, 1.0, 0.0)
    has_high = jnp.where(slab < SLABS - 1, 1.0, 0.0)
    fix_ref[0] = FAR * cols[0] * has_low
    fix_ref[1] = (NEAR * cols[0] + FAR * cols[1]) * has_low
    fix_ref[2] = (FAR * cols[2] + NEAR * cols[3]) * has_high
    fix_ref[3] = FAR * cols[3] * has_high


def green_kernel(rate_ref, green_ref, wide_ref, coef_ref):
    lane8 = lax.broadcasted_iota(jnp.int32, (8, 128), 1)
    sub8 = lax.broadcasted_iota(jnp.int32, (8, 128), 0)
    wide_ref[...] = 1.0 / rate_ref[...] + MAIN
    zero = jnp.zeros((8, 128), F32)
    recip, low1, low2 = ldl(lambda k: jnp.broadcast_to(wide_ref[k : k + 1, :], (8, 128)), zero)
    units = [(sub8 == ENDS.index(k)).astype(F32) if k in ENDS else zero for k in range(ROWS)]
    full = substitute(units, recip, low1, low2)

    def entry(k, i):
        return jnp.broadcast_to(full[k][i : i + 1, :], (8, 128))

    not_first = ((lane8 > 0) & (lane8 < SLABS)).astype(F32)
    not_last = (lane8 < SLABS - 1).astype(F32)

    def lower(k):
        s0, s1 = entry(k, 0), entry(k, 1)
        return (FAR * s0 * not_first, (NEAR * s0 + FAR * s1) * not_first)

    def upper(k):
        s2, s3 = entry(k, 2), entry(k, 3)
        return ((FAR * s2 + NEAR * s3) * not_last, FAR * s3 * not_last)

    low_a = (lower(ENDS[0]), lower(ENDS[1]))
    low_c = (lower(ENDS[2]), lower(ENDS[3]))
    up_b = (upper(ENDS[0]), upper(ENDS[1]))
    up_e = (upper(ENDS[2]), upper(ENDS[3]))
    a, b, c, e = low_a, up_b, low_c, up_e
    for hop in (1, 2, 4, 8, 16):
        ax, bx, cx, ex = (each(m, lambda v: pltpu.roll(v, hop, 1)) for m in (a, b, c, e))
        w = inverse_of_one_minus(mm(a, ex))
        wa_c = mm(w, mm(a, cx))
        wb = mm(w, b)
        cy_ex = mm(c, ex)
        new_e = add(e, mm(cy_ex, wb))
        new_c = neg(add(mm(c, cx), mm(cy_ex, wa_c)))
        new_a = add(ax, mm(bx, wa_c))
        new_b = neg(mm(bx, wb))
        joined = lane8 >= hop

        def pick(new, old):
            return tuple(
                tuple(jnp.where(joined, new[i][j], old[i][j]) for j in range(2)) for i in range(2)
            )

        a, b, c, e = pick(new_a, a), pick(new_b, b), pick(new_c, c), pick(new_e, e)
    q = e
    q_prev = each(q, lambda v: jnp.where(lane8 > 0, pltpu.roll(v, 1, 1), 0.0))
    z = inverse_of_one_minus(mm(low_a, q_prev))
    gain = mm(mm(low_c, q_prev), z)
    carry = add(low_c, mm(gain, low_a))
    z_low = mm(z, low_a)
    z_up = mm(z, up_b)
    for group, mats in enumerate(((carry, gain), (z, z_low), (z_up, q))):
        block = jnp.zeros((8, 128), F32)
        for n, m in enumerate(mats):
            for i in range(2):
                for j in range(2):
                    block = jnp.where(sub8 == 4 * n + 2 * i + j, m[i][j], block)
        for s in range(SLABS):
            coef_ref[s, 8 * group : 8 * group + 8, :] = jnp.broadcast_to(block[:, s : s + 1], (8, 128))

    def coef(s, n):
        def one(i, j):
            at = 4 * n + 2 * i + j
            return jnp.broadcast_to(coef_ref[s, at : at + 1, :], (8, 128))

        return tuple(tuple(one(i, j) for j in range(2)) for i in range(2))

    def at_lane(n):
        return lane8 == n

    forward = []
    prev = None
    for s in range(SLABS):
        m, g = coef(s, 0), coef(s, 1)
        now = []
        for i in range(2):
            value = jnp.where(at_lane(4 * s), g[i][0], 0.0)
            value = jnp.where(at_lane(4 * s + 1), g[i][1], value)
            value = jnp.where(at_lane(4 * s + 2 + i), 1.0, value)
            if prev is not None:
                value = value - m[i][0] * prev[0] - m[i][1] * prev[1]
            now.append(value)
        forward.append(now)
        prev = now
    for row in (0, 1, 4 * SLABS - 2, 4 * SLABS - 1):
        green_ref[row : row + 1, :] = jnp.zeros((1, 128), F32)
    after = None
    for s in reversed(range(SLABS)):
        zc, zl, zu, qc = coef(s, 2), coef(s, 3), coef(s, 4), coef(s, 5)
        now = []
        for i in range(2):
            value = jnp.where(at_lane(4 * s), zc[i][0], 0.0)
            value = jnp.where(at_lane(4 * s + 1), zc[i][1], value)
            if s > 0:
                value = value - zl[i][0] * forward[s - 1][0] - zl[i][1] * forward[s - 1][1]
            if after is not None:
                value = value - zu[i][0] * after[0] - zu[i][1] * after[1]
            now.append(value)
        if s < SLABS - 1:
            for i in range(2):
                high = forward[s][i] - qc[i][0] * after[0] - qc[i][1] * after[1]
                green_ref[4 * (s + 1) + i : 4 * (s + 1) + i + 1, :] = high[0:1]
        if s > 0:
            for i in range(2):
                green_ref[4 * (s - 1) + 2 + i : 4 * (s - 1) + 3 + i, :] = now[i][0:1]
        after = now


def green_operator(rate):
    return pl.pallas_call(
        green_kernel,
        out_shape=shaped(128, 128),
        in_specs=[VMEM],
        out_specs=VMEM,
        scratch_shapes=[pltpu.VMEM((ROWS, 128), F32), pltpu.VMEM((SLABS, 24, 128), F32)],
        compiler_params=params(4),
        name="green_operator",
    )(rate)


def pre_kernel(
    place_ref, vel_hbm, part_hbm, rate_hbm, cell_hbm, high_hbm, low_hbm, inner_hbm, outer_hbm,
    packed_hbm, vel_ref, cell_ref, part_ref, rate_ref, out_ref, sems,
):
    even = place_ref[0] % 2 == 0
    order = (2, 3, 0, 1)
    into = [
        pltpu.make_async_copy(part_hbm, part_ref, sems.at[0]),
        pltpu.make_async_copy(rate_hbm, rate_ref, sems.at[1]),
    ]
    layers = [
        pltpu.make_async_copy(vel_hbm.at[:, x], vel_ref.at[:, x], sems.at[2 + x]) for x in order
    ]
    cells = pltpu.make_async_copy(cell_hbm, cell_ref, sems.at[6])
    for copy in into + layers + [cells]:
        copy.start()
    for copy in into:
        copy.wait()
    left = lax.broadcasted_iota(jnp.int32, (1, 128), 1) < SLOTS

    def pack(first, last):
        for r in range(first, last):
            part = [part_ref[i : i + 1, 128 * r : 128 * r + 128] for i in range(3)]
            part.append(rate_ref[0:1, 128 * r : 128 * r + 128])
            for n in range(2):
                one, two = part[2 * n], part[2 * n + 1]
                out_ref[2 * r, n : n + 1, :] = jnp.where(left, one, pltpu.roll(two, SLOTS, 1))
                out_ref[2 * r + 1, n : n + 1, :] = jnp.where(left, pltpu.roll(one, SLOTS, 1), two)

    out = []
    for n, x in enumerate(order):
        pack(16 * n, 16 * n + 16)
        layers[n].wait()
        target = high_hbm.at[:, x - 2] if x >= 2 else low_hbm.at[:, x]
        flat = pltpu.make_async_copy(vel_ref.at[:, x], target, sems.at[7 + n])
        flat.start()
        out.append(flat)
        bottom, top = vel_ref.at[:, x, 0:2], vel_ref.at[:, x, ROWS - 2 : ROWS]
        out.append(pltpu.make_async_copy(top, inner_hbm.at[:, x], sems.at[11 + n]))
        out.append(pltpu.make_async_copy(bottom, outer_hbm.at[:, x], sems.at[15 + n]))

        @pl.when(even)
        def _():
            out[-2].start()
            out[-1].start()

        @pl.when(jnp.logical_not(even))
        def _():
            pltpu.make_async_copy(bottom, inner_hbm.at[:, x], sems.at[11 + n]).start()
            pltpu.make_async_copy(top, outer_hbm.at[:, x], sems.at[15 + n]).start()

    out.append(pltpu.make_async_copy(out_ref, packed_hbm, sems.at[19]))
    out[-1].start()
    cells.wait()
    for copy in out:
        copy.wait()


def prepared(place, velocity, part_vel, part_rate, cells):
    return pl.pallas_call(
        pre_kernel,
        out_shape=(
            far_out(3, 2, ROWS, CZ),
            far_out(3, 2, ROWS, CZ),
            far_out(3, CX, 2, CZ),
            far_out(3, CX, 2, CZ),
            far_out(PEERS, 2, 128),
            held((3, CX, ROWS, CZ)),
            held((1, TOTAL), jnp.int32),
        ),
        in_specs=[SMEM] + [ANY] * 4,
        out_specs=(ANY,) * 5 + (VMEM,) * 2,
        scratch_shapes=[
            pltpu.VMEM((3, TOTAL), F32),
            pltpu.VMEM((1, TOTAL), F32),
            pltpu.VMEM((PEERS, 2, 128), F32),
            pltpu.SemaphoreType.DMA((20,)),
        ],
        compiler_params=params(16),
        name="prepare",
    )(place, *far_in(velocity, part_vel, part_rate, cells))


def halves(cells):
    plane = cells >> 10
    span = cells & (CZ - 1)
    return plane, span >> 7, span & 127


def span_table(high, low):
    width = high.shape[1]
    inner = lax.broadcasted_iota(jnp.int32, (128, width), 0) == low
    inner = inner.astype(F32).astype(BF16)
    rows = []
    for t in range(8):
        flag = (high == t).astype(F32).astype(BF16)
        rows.append(inner * flag)
    return jnp.concatenate(rows, axis=0)


def column_of(row, length):
    wide = jnp.broadcast_to(row, (length, length))
    here = lax.broadcasted_iota(jnp.int32, (length, length), 0) == lax.broadcasted_iota(
        jnp.int32, (length, length), 1
    )
    return jnp.broadcast_to(
        jnp.sum(jnp.where(here, wide, 0.0), axis=1, keepdims=True), (length, 128)
    )


def find_kernel(
    place_ref, vel_ref, cell_ref, rate_hbm, *refs,
):
    outs, held_refs = refs[:5], refs[5:10]
    fluid_ref, scale_ref, tip_ref, fix_ref, solve_ref = held_refs
    bf_ref, table_ref, rate_ref, wide_ref, sems = refs[10:]
    copies = [
        pltpu.make_async_copy(rate_hbm, rate_ref, sems.at[0]),
    ]
    for copy in copies:
        copy.start()
    for c in range(3):
        for x in range(CX):
            top = c * PLANES + x * ROWS
            bf_ref[top : top + ROWS, :] = vel_ref[c, x].astype(BF16)
    for copy in copies:
        copy.wait()
    own_factors(place_ref[0], rate_ref, scale_ref, tip_ref, fix_ref, solve_ref, wide_ref)
    stores = [
        pltpu.make_async_copy(held_refs[n], outs[n], sems.at[1 + n]) for n in range(1, 5)
    ]
    for store in stores:
        store.start()
    for step in range(TOTAL // CHUNK):
        lanes = slice(step * CHUNK, (step + 1) * CHUNK)
        plane, high, low = halves(cell_ref[:, lanes])
        table_ref[...] = span_table(high, low)
        at = jnp.dot(bf_ref[...], table_ref[...], preferred_element_type=F32)
        mask = lax.broadcasted_iota(jnp.int32, (PLANES, CHUNK), 0) == plane
        for n in range(3):
            fluid_ref[n : n + 1, lanes] = jnp.sum(
                jnp.where(mask, at[n * PLANES : (n + 1) * PLANES], 0.0), axis=0, keepdims=True
            )
        stores.append(
            pltpu.make_async_copy(
                fluid_ref.at[:, lanes], outs[0].at[:, lanes], sems.at[6 + step]
            )
        )
        stores[-1].start()
    for store in stores:
        store.wait()


def find(place, vel_held, cells, rate):
    return pl.pallas_call(
        find_kernel,
        out_shape=(
            far_out(3, TOTAL),
            far_out(ROWS, 128),
            far_out(4, ROWS, 128),
            far_out(4, ROWS, 128),
            far_out(ROWS, 128),
        ),
        in_specs=[SMEM, VMEM, VMEM, ANY],
        out_specs=(ANY,) * 5,
        scratch_shapes=[
            pltpu.VMEM((3, TOTAL), F32),
            pltpu.VMEM((ROWS, 128), F32),
            pltpu.VMEM((4, ROWS, 128), F32),
            pltpu.VMEM((4, ROWS, 128), F32),
            pltpu.VMEM((ROWS, 128), F32),
            pltpu.VMEM((3 * PLANES, CZ), BF16),
            pltpu.VMEM((CZ, CHUNK), BF16),
            pltpu.VMEM((8, 128), F32),
            pltpu.VMEM((ROWS, 128), F32),
            pltpu.SemaphoreType.DMA((6 + TOTAL // CHUNK,)),
        ],
        compiler_params=params(28),
        name="find",
    )(place, vel_held, cells, *far_in(rate))


def main_kernel(
    place_ref, cell_ref, inner_hbm, outer_hbm, before_hbm, behind_hbm, moved_hbm,
    fluid_hbm, scale_hbm, tip_hbm, vel_hbm, section_hbm, count_hbm, near_hbm, far_hbm,
    part_hbm, tips_hbm, new_ref,
    pad_ref, before_ref, behind_ref, section_ref, table_ref, got_ref, deposit_ref, moved_ref,
    count_ref, near_ref, far_ref, part_ref, tips_ref, coef_ref,
    fluid_ref, scale_ref, tip_ref, sems,
):
    sources = [
        (moved_hbm, moved_ref),
        (count_hbm, count_ref),
        (fluid_hbm, fluid_ref),
        (scale_hbm, scale_ref),
        (tip_hbm, tip_ref),
        (near_hbm, near_ref),
        (far_hbm, far_ref),
        (vel_hbm, pad_ref.at[:, :, 8 : 8 + ROWS, :]),
        (inner_hbm, pad_ref.at[:, :, 6:8, :]),
        (outer_hbm, pad_ref.at[:, :, 8 + ROWS : 10 + ROWS, :]),
        (before_hbm, before_ref),
        (behind_hbm, behind_ref),
        (section_hbm, section_ref),
    ]
    copies = [pltpu.make_async_copy(a, b, sems.at[n]) for n, (a, b) in enumerate(sources)]
    swaps = [n for n, (a, b) in enumerate(sources) if a is inner_hbm or a is outer_hbm]
    for n, copy in enumerate(copies):
        if n not in swaps:
            copy.start()
    even = place_ref[0] % 2 == 0

    @pl.when(even)
    def _():
        for n, source in zip(swaps, (outer_hbm, inner_hbm)):
            pltpu.make_async_copy(source, sources[n][1], sems.at[n]).start()

    @pl.when(jnp.logical_not(even))
    def _():
        for n in swaps:
            copies[n].start()

    steps = TOTAL // CHUNK

    def lanes_of(step):
        return slice(step * CHUNK, (step + 1) * CHUNK)

    def spread_of(step):
        lanes = lanes_of(step)
        plane, high, low = halves(cell_ref[:, lanes])
        table_ref[...] = span_table(high, low)
        mask = lax.broadcasted_iota(jnp.int32, (PLANES, CHUNK), 0) == plane
        mask = mask.astype(F32).astype(BF16)
        live = got_ref[4:5, lanes] > 0.5
        rate = got_ref[3:4, lanes]
        spread = []
        for n in range(3):
            old = got_ref[n : n + 1, lanes]
            relative = fluid_ref[n : n + 1, lanes] - old
            part_ref[n : n + 1, lanes] = jnp.where(live, old + TIME_STEP * rate * relative, 0.0)
            push = jnp.where(live, -rate * relative, 0.0).astype(BF16)
            spread.append(mask * push)
        return jnp.concatenate(spread, axis=0)

    def unpack():
        left = lax.broadcasted_iota(jnp.int32, (1, 128), 1) < SLOTS
        lane = lax.broadcasted_iota(jnp.int32, (1, 128), 1)
        for r in range(PEERS // 2):
            lanes = slice(128 * r, 128 * r + 128)
            for n in range(2):
                one = moved_ref[2 * r, n : n + 1, :]
                two = moved_ref[2 * r + 1, n : n + 1, :]
                got_ref[2 * n : 2 * n + 1, lanes] = jnp.where(left, one, pltpu.roll(two, SLOTS, 1))
                got_ref[2 * n + 1 : 2 * n + 2, lanes] = jnp.where(
                    left, pltpu.roll(one, SLOTS, 1), two
                )
            limit = jnp.where(left, count_ref[0, 2 * r], count_ref[0, 2 * r + 1])
            got_ref[4:5, lanes] = ((lane & (SLOTS - 1)) < limit).astype(F32)

    def tiled(column, times):
        return jnp.concatenate([column] * times, axis=1)

    def stencil(c, x):
        def layer(i, top):
            if i < 0:
                return before_ref[c, 2 + i, top : top + 8, :]
            if i >= CX:
                return behind_ref[c, i - CX, top : top + 8, :]
            return pad_ref[c, i, 8 + top : 16 + top, :]

        for t in range(ROWS // 8):
            top = 8 * t
            here = layer(x, top)
            ddx = (TIME_STEP * 8.0 / 12.0) * (layer(x + 1, top) - layer(x - 1, top)) - (
                TIME_STEP / 12.0
            ) * (
                layer(x + 2, top) - layer(x - 2, top)
            )
            rolled = {k: pltpu.roll(here, (-k) % CZ, 1) for k in (1, -1, 2, -2)}
            ddz = (TIME_STEP * 8.0 / 12.0) * (rolled[1] - rolled[-1]) - (TIME_STEP / 12.0) * (
                rolled[2] - rolled[-2]
            )

            def shifted(k):
                return pad_ref[c, x, 8 + top + k : 16 + top + k, :]

            near = tiled(coef_ref[0, top : top + 8, :], 8)
            far = tiled(coef_ref[1, top : top + 8, :], 8)
            ddy = near * (shifted(1) - shifted(-1)) + far * (shifted(2) - shifted(-2))
            moved = (
                pad_ref[0, x, 8 + top : 16 + top, :] * ddx
                + pad_ref[1, x, 8 + top : 16 + top, :] * ddy
                + pad_ref[2, x, 8 + top : 16 + top, :] * ddz
            )
            new_ref[c, x, top : top + 8, :] = (
                SECTION_KEEP * section_ref[c, x, top : top + 8, :] - moved
            )

    planes = [(c, x) for c in range(3) for x in range(CX)]
    share = len(planes) // steps
    for copy in copies[:3]:
        copy.wait()
    unpack()
    for step in range(steps):
        spread = spread_of(step)
        if step == 0:
            for copy in copies[3:]:
                copy.wait()
            coef_ref[0] = TIME_STEP * column_of(near_ref[...], ROWS)
            coef_ref[1] = TIME_STEP * column_of(far_ref[...], ROWS)
        for c, x in planes[share * step : share * (step + 1)]:
            stencil(c, x)
        last = step == steps - 1
        if last:
            stores = [pltpu.make_async_copy(part_ref, part_hbm, sems.at[14])]
            stores[0].start()
        wide = CZ // 2 if last else CZ
        for z in range(0, CZ, wide):
            new = lax.dot_general(
                spread, table_ref[z : z + wide, :], (((1,), (1,)), ((), ())),
                preferred_element_type=F32,
            )
            if step == 0:
                deposit_ref[...] = new
                continue
            if not last:
                deposit_ref[...] += new
                continue
            for c, x in planes:
                base = c * PLANES + x * ROWS
                total = [None] * 4
                for t in range(ROWS // 8):
                    top = 8 * t
                    full = new_ref[c, x, top : top + 8, z : z + wide] + TIME_STEP * (
                        deposit_ref[base + top : base + top + 8, z : z + wide]
                        + new[base + top : base + top + 8]
                    )
                    new_ref[c, x, top : top + 8, z : z + wide] = full
                    scaled = full * tiled(scale_ref[top : top + 8, :], wide // 128)
                    for r in range(4):
                        weighted = scaled * tiled(tip_ref[r, top : top + 8, :], wide // 128)
                        total[r] = weighted if t == 0 else total[r] + weighted
                for r in (0, 2):
                    one, two = total[r], total[r + 1]
                    upper = lax.broadcasted_iota(jnp.int32, one.shape, 0) < 4
                    both = jnp.where(upper, one, two) + pltpu.roll(jnp.where(upper, two, one), 4, 0)
                    both = both + pltpu.roll(both, 6, 0)
                    both = both + pltpu.roll(both, 7, 0)
                    for k in range(wide // 128):
                        at = 8 * x + z // 128 + k
                        lanes = slice(128 * k, 128 * k + 128)
                        tips_ref[at, c, r : r + 1, :] = both[0:1, lanes]
                        tips_ref[at, c, r + 1 : r + 2, :] = both[4:5, lanes]
            for x in range(CX if last else 0):
                span = pl.ds(8 * x + z // 128, wide // 128)
                stores.append(
                    pltpu.make_async_copy(
                        tips_ref.at[span], tips_hbm.at[span], sems.at[14 + len(stores)]
                    )
                )
                stores[-1].start()
    for store in stores:
        store.wait()


def main_part(place, cells, halos, moved, others):
    return pl.pallas_call(
        main_kernel,
        out_shape=(
            far_out(3, TOTAL),
            far_out(SLABS, 3, 4, 128),
            held((3, CX, ROWS, CZ)),
        ),
        in_specs=[SMEM, VMEM] + [ANY] * 13,
        out_specs=(ANY, ANY, VMEM),
        scratch_shapes=[
            pltpu.VMEM((3, CX, ROWS + 16, CZ), F32),
            pltpu.VMEM((3, 2, ROWS, CZ), F32),
            pltpu.VMEM((3, 2, ROWS, CZ), F32),
            pltpu.VMEM((3, CX, ROWS, CZ), F32),
            pltpu.VMEM((CZ, CHUNK), BF16),
            pltpu.VMEM((8, TOTAL), F32),
            pltpu.VMEM((3 * PLANES, CZ), F32),
            pltpu.VMEM((PEERS, 2, 128), F32),
            pltpu.SMEM((1, PEERS), jnp.int32),
            pltpu.VMEM((1, ROWS), F32),
            pltpu.VMEM((1, ROWS), F32),
            pltpu.VMEM((3, TOTAL), F32),
            pltpu.VMEM((SLABS, 3, 4, 128), F32),
            pltpu.VMEM((2, ROWS, 128), F32),
            pltpu.VMEM((3, TOTAL), F32),
            pltpu.VMEM((ROWS, 128), F32),
            pltpu.VMEM((4, ROWS, 128), F32),
            pltpu.SemaphoreType.DMA((31,)),
        ],
        compiler_params=params(36),
        name="main_part",
    )(place, cells, *halos, moved, *far_in(*others))


WIDTH = 3 * CX * CZ // SLABS


def solve_kernel(tips_ref, green_ref, out_ref, all_ref):
    for s in range(SLABS):
        for c in range(3):
            all_ref[4 * s : 4 * s + 4, 128 * c : 128 * c + 128] = tips_ref[s, c]
    found = jnp.dot(green_ref[...], all_ref[...], precision=HIGH, preferred_element_type=F32)
    for s in range(SLABS):
        for c in range(3):
            out_ref[s, c] = found[4 * s : 4 * s + 4, 128 * c : 128 * c + 128]


def solved(tips, green):
    return pl.pallas_call(
        solve_kernel,
        out_shape=shaped(SLABS, 3, 4, 128),
        in_specs=[VMEM, VMEM],
        out_specs=VMEM,
        scratch_shapes=[pltpu.VMEM((4 * SLABS, WIDTH), F32)],
        compiler_params=params(4),
        name="solve",
    )(tips, green)


def local_kernel(vel_hbm, section_ref, scale_ref, solve_ref, section_hbm, out_ref, sems):
    loads = [pltpu.make_async_copy(vel_hbm.at[c], out_ref.at[c], sems.at[c]) for c in range(3)]
    for load in loads:
        load.start()
    store = pltpu.make_async_copy(section_ref, section_hbm, sems.at[3])
    store.start()
    whole = solve_ref[:, 0:ROWS]
    head = whole.astype(BF16)
    rest = (whole - head.astype(F32)).astype(BF16)
    left = jnp.concatenate([head, rest, head], axis=1)
    scale = jnp.concatenate([scale_ref[...]] * 8, axis=1)
    for c in range(3):
        loads[c].wait()
        for x in range(CX):
            value = section_ref[c, x] * scale
            high = value.astype(BF16)
            low = (value - high.astype(F32)).astype(BF16)
            right = jnp.concatenate([high, high, low], axis=0)
            out_ref[c, x] += jnp.dot(left, right, preferred_element_type=F32)
    store.wait()


def local_solve(velocity, section_new, scale, solve):
    return pl.pallas_call(
        local_kernel,
        out_shape=(far_out(3, CX, ROWS, CZ), held((3, CX, ROWS, CZ))),
        in_specs=[ANY, VMEM, VMEM, VMEM],
        out_specs=(ANY, VMEM),
        scratch_shapes=[pltpu.SemaphoreType.DMA((4,))],
        compiler_params=params(16),
        name="local_solve",
    )(*far_in(velocity), section_new, scale, solve)


def final_kernel(partial_ref, edge_ref, fix_ref, out_hbm, out_ref, sems):
    stores = []
    for c in range(3):
        for x in range(CX):
            for t in range(CZ // 128):
                lanes = slice(128 * t, 128 * t + 128)
                edge = edge_ref[8 * x + t, c]
                value = partial_ref[c, x, :, lanes]
                for r in range(4):
                    value = value - fix_ref[r] * edge[r : r + 1, :]
                out_ref[c, x, :, lanes] = value
            if x % 2 == 1:
                span = pl.ds(x - 1, 2)
                stores.append(
                    pltpu.make_async_copy(
                        out_ref.at[c, span], out_hbm.at[c, span], sems.at[len(stores)]
                    )
                )
                stores[-1].start()
    for copy in stores:
        copy.wait()


def finished(partial, edges, fix):
    return pl.pallas_call(
        final_kernel,
        out_shape=far_out(3, CX, ROWS, CZ),
        in_specs=[VMEM] * 3,
        out_specs=ANY,
        scratch_shapes=[pltpu.VMEM((3, CX, ROWS, CZ), F32), pltpu.SemaphoreType.DMA((6,))],
        compiler_params=params(16),
        name="finish",
    )(partial, edges, fix)


def local(velocity, section, diffusion, rhs_near, rhs_far, part_vel, part_rate, counts, cell_slot):
    n_gx, n_gy = lax.axis_size("gx"), lax.axis_size("gy")
    up_x = [(i, (i + 1) % n_gx) for i in range(n_gx)]
    down_x = [(t, s) for s, t in up_x]
    place = lax.axis_index("gy").astype(jnp.int32).reshape(1)
    high, low, inner, outer, packed, vel_held, cells = prepared(
        place, velocity, part_vel, part_rate.reshape(1, TOTAL), cell_slot
    )
    before = lax.ppermute(high, "gx", up_x)
    behind = lax.ppermute(low, "gx", down_x)
    inner = lax.ppermute(inner, "gy", [(i, i ^ 1) for i in range(n_gy)])
    outer = lax.ppermute(
        outer, "gy", [pair for i in range(1, n_gy - 1, 2) for pair in ((i, i + 1), (i + 1, i))]
    )
    moved = lax.all_to_all(packed, ("gx", "gy"), split_axis=0, concat_axis=0, tiled=True)
    fluid, scale, tip, fix, solve = find(place, vel_held, cells, diffusion.reshape(8, 128))
    part_new, tips, new_held = main_part(
        place, cells, (inner, outer, before, behind), moved,
        (fluid, scale, tip, velocity, section, counts, rhs_near.reshape(1, ROWS), rhs_far.reshape(1, ROWS)),
    )
    tips, diffusion = lax.optimization_barrier((tips, diffusion))
    all_tips = lax.all_to_all(tips, "gy", split_axis=0, concat_axis=0, tiled=True)
    rate = jnp.pad(
        diffusion.reshape(SLABS, ROWS).T, ((0, 0), (0, 128 - SLABS)), constant_values=1000.0
    )
    reply = solved(all_tips, green_operator(rate))
    reply, solve = lax.optimization_barrier((reply, solve))
    edges = lax.all_to_all(reply, "gy", split_axis=0, concat_axis=0, tiled=True)
    section_new, partial = local_solve(velocity, new_held, scale, solve)
    velocity_new = finished(partial, edges, fix)
    return (velocity_new, section_new, part_new)


def solution(mesh):
    return jax.shard_map(
        local,
        mesh=mesh,
        in_specs=(
            P(None, "gx", "gy", None),
            P(None, "gx", "gy", None),
            P(),
            P("gy"),
            P("gy"),
            P(None, ("gx", "gy")),
            P(("gx", "gy")),
            P(("gx", "gy"), None),
            P(("gx", "gy"), None),
        ),
        out_specs=(P(None, "gx", "gy", None), P(None, "gx", "gy", None), P(None, ("gx", "gy"))),
        check_vma=False,
    )
```

```python
import jax
import jax.numpy as jnp
from jax import lax
from jax.experimental import pallas as pl
from jax.experimental.pallas import tpu as pltpu
from jax.sharding import PartitionSpec as P

TIME_STEP = 0.2
SECTION_KEEP = -5.0 / 9.0
SECTION_GAIN = 15.0 / 16.0
MAIN = 2.5
NEAR = -4.0 / 3.0
FAR = 1.0 / 12.0
SLABS = 32
ROWS = 32
CX = 4
CZ = 1024
PLANES = CX * ROWS
SLOTS = 64
PEERS = 128
TOTAL = PEERS * SLOTS
CHUNK = 2048
HIGH = lax.Precision.HIGHEST
F32 = jnp.float32
BF16 = jnp.bfloat16


def params(mib=60):
    return pltpu.CompilerParams(vmem_limit_bytes=mib * 1024 * 1024)


VMEM = pl.BlockSpec(memory_space=pltpu.MemorySpace.VMEM)
SMEM = pl.BlockSpec(memory_space=pltpu.MemorySpace.SMEM)
ANY = pl.BlockSpec(memory_space=pltpu.MemorySpace.HBM)


def held(shape, dtype=F32):
    return pltpu.MemorySpace.VMEM(shape, dtype)


def shaped(*shape):
    return jax.ShapeDtypeStruct(shape, F32)


def far_out(*shape):
    return pltpu.MemorySpace.HBM(shape, F32)


def far_in(*arrays):
    return [pltpu.with_memory_space_constraint(a, pltpu.MemorySpace.HBM) for a in arrays]


def mm(a, b):
    return tuple(
        tuple(a[i][0] * b[0][j] + a[i][1] * b[1][j] for j in range(2)) for i in range(2)
    )


def add(a, b, sign=1.0):
    return tuple(tuple(a[i][j] + sign * b[i][j] for j in range(2)) for i in range(2))


def neg(a):
    return tuple(tuple(-e for e in row) for row in a)


def each(a, fn):
    return tuple(tuple(fn(e) for e in row) for row in a)


def inverse_of_one_minus(a):
    p, q, r, s = 1.0 - a[0][0], -a[0][1], -a[1][0], 1.0 - a[1][1]
    scale = 1.0 / (p * s - q * r)
    return ((s * scale, -q * scale), (-r * scale, p * scale))


def ldl(main_of, zero):
    recip, low1, low2 = [], [], []
    for k in range(ROWS):
        main = main_of(k)
        if k == 0:
            low1.append(zero)
            low2.append(zero)
            recip.append(1.0 / main)
            continue
        edge = NEAR - FAR * low1[k - 1]
        one = edge * recip[k - 1]
        two = FAR * recip[k - 2] if k > 1 else zero
        low1.append(one)
        low2.append(two)
        recip.append(1.0 / (main - edge * one - FAR * two))
    return recip, low1, low2


def substitute(rows, recip, low1, low2):
    half = []
    for k in range(ROWS):
        value = rows[k]
        if k > 0:
            value = value - low1[k] * half[k - 1]
        if k > 1:
            value = value - low2[k] * half[k - 2]
        half.append(value)
    full = [None] * ROWS
    for k in reversed(range(ROWS)):
        value = half[k] * recip[k]
        if k < ROWS - 1:
            value = value - low1[k + 1] * full[k + 1]
        if k < ROWS - 2:
            value = value - low2[k + 2] * full[k + 2]
        full[k] = value
    return full


ENDS = (0, 1, ROWS - 2, ROWS - 1)


def own_factors(slab, rate_ref, scale_ref, tip_ref, fix_ref, solve_ref, wide_ref):
    lane8 = lax.broadcasted_iota(jnp.int32, (8, 128), 1)
    row = rate_ref[pl.ds(slab // 4, 1), :]
    row = pltpu.roll(jnp.broadcast_to(row, (8, 128)), 128 - ROWS * (slab % 4), 1)
    inv_rate = 1.0 / column_of(row[0:1, 0:ROWS], ROWS)
    scale_ref[...] = SECTION_GAIN * inv_rate
    wide_ref[...] = inv_rate + MAIN
    recip, low1, low2 = ldl(
        lambda k: jnp.broadcast_to(wide_ref[k : k + 1, :], (8, 128)), jnp.zeros((8, 128), F32)
    )
    full = substitute([(lane8 == k).astype(F32) for k in range(ROWS)], recip, low1, low2)
    for k in range(ROWS):
        solve_ref[k : k + 1, :] = full[k][0:1]
    solve = solve_ref[...]
    cols = [jnp.broadcast_to(solve[:, n : n + 1], (ROWS, 128)) for n in ENDS]
    for n in range(4):
        tip_ref[n] = cols[n]
    has_low = jnp.where(slab > 0, 1.0, 0.0)
    has_high = jnp.where(slab < SLABS - 1, 1.0, 0.0)
    fix_ref[0] = FAR * cols[0] * has_low
    fix_ref[1] = (NEAR * cols[0] + FAR * cols[1]) * has_low
    fix_ref[2] = (FAR * cols[2] + NEAR * cols[3]) * has_high
    fix_ref[3] = FAR * cols[3] * has_high


def green_kernel(rate_ref, green_ref, wide_ref, coef_ref):
    lane8 = lax.broadcasted_iota(jnp.int32, (8, 128), 1)
    sub8 = lax.broadcasted_iota(jnp.int32, (8, 128), 0)
    wide_ref[...] = 1.0 / rate_ref[...] + MAIN
    zero = jnp.zeros((8, 128), F32)
    recip, low1, low2 = ldl(lambda k: jnp.broadcast_to(wide_ref[k : k + 1, :], (8, 128)), zero)
    units = [(sub8 == ENDS.index(k)).astype(F32) if k in ENDS else zero for k in range(ROWS)]
    full = substitute(units, recip, low1, low2)

    def entry(k, i):
        return jnp.broadcast_to(full[k][i : i + 1, :], (8, 128))

    not_first = ((lane8 > 0) & (lane8 < SLABS)).astype(F32)
    not_last = (lane8 < SLABS - 1).astype(F32)

    def lower(k):
        s0, s1 = entry(k, 0), entry(k, 1)
        return (FAR * s0 * not_first, (NEAR * s0 + FAR * s1) * not_first)

    def upper(k):
        s2, s3 = entry(k, 2), entry(k, 3)
        return ((FAR * s2 + NEAR * s3) * not_last, FAR * s3 * not_last)

    low_a = (lower(ENDS[0]), lower(ENDS[1]))
    low_c = (lower(ENDS[2]), lower(ENDS[3]))
    up_b = (upper(ENDS[0]), upper(ENDS[1]))
    up_e = (upper(ENDS[2]), upper(ENDS[3]))
    a, b, c, e = low_a, up_b, low_c, up_e
    for hop in (1, 2, 4, 8, 16):
        ax, bx, cx, ex = (each(m, lambda v: pltpu.roll(v, hop, 1)) for m in (a, b, c, e))
        w = inverse_of_one_minus(mm(a, ex))
        wa_c = mm(w, mm(a, cx))
        wb = mm(w, b)
        cy_ex = mm(c, ex)
        new_e = add(e, mm(cy_ex, wb))
        new_c = neg(add(mm(c, cx), mm(cy_ex, wa_c)))
        new_a = add(ax, mm(bx, wa_c))
        new_b = neg(mm(bx, wb))
        joined = lane8 >= hop

        def pick(new, old):
            return tuple(
                tuple(jnp.where(joined, new[i][j], old[i][j]) for j in range(2)) for i in range(2)
            )

        a, b, c, e = pick(new_a, a), pick(new_b, b), pick(new_c, c), pick(new_e, e)
    q = e
    q_prev = each(q, lambda v: jnp.where(lane8 > 0, pltpu.roll(v, 1, 1), 0.0))
    z = inverse_of_one_minus(mm(low_a, q_prev))
    gain = mm(mm(low_c, q_prev), z)
    carry = add(low_c, mm(gain, low_a))
    z_low = mm(z, low_a)
    z_up = mm(z, up_b)
    for group, mats in enumerate(((carry, gain), (z, z_low), (z_up, q))):
        block = jnp.zeros((8, 128), F32)
        for n, m in enumerate(mats):
            for i in range(2):
                for j in range(2):
                    block = jnp.where(sub8 == 4 * n + 2 * i + j, m[i][j], block)
        for s in range(SLABS):
            coef_ref[s, 8 * group : 8 * group + 8, :] = jnp.broadcast_to(block[:, s : s + 1], (8, 128))

    def coef(s, n):
        def one(i, j):
            at = 4 * n + 2 * i + j
            return jnp.broadcast_to(coef_ref[s, at : at + 1, :], (8, 128))

        return tuple(tuple(one(i, j) for j in range(2)) for i in range(2))

    def at_lane(n):
        return lane8 == n

    forward = []
    prev = None
    for s in range(SLABS):
        m, g = coef(s, 0), coef(s, 1)
        now = []
        for i in range(2):
            value = jnp.where(at_lane(4 * s), g[i][0], 0.0)
            value = jnp.where(at_lane(4 * s + 1), g[i][1], value)
            value = jnp.where(at_lane(4 * s + 2 + i), 1.0, value)
            if prev is not None:
                value = value - m[i][0] * prev[0] - m[i][1] * prev[1]
            now.append(value)
        forward.append(now)
        prev = now
    for row in (0, 1, 4 * SLABS - 2, 4 * SLABS - 1):
        green_ref[row : row + 1, :] = jnp.zeros((1, 128), F32)
    after = None
    for s in reversed(range(SLABS)):
        zc, zl, zu, qc = coef(s, 2), coef(s, 3), coef(s, 4), coef(s, 5)
        now = []
        for i in range(2):
            value = jnp.where(at_lane(4 * s), zc[i][0], 0.0)
            value = jnp.where(at_lane(4 * s + 1), zc[i][1], value)
            if s > 0:
                value = value - zl[i][0] * forward[s - 1][0] - zl[i][1] * forward[s - 1][1]
            if after is not None:
                value = value - zu[i][0] * after[0] - zu[i][1] * after[1]
            now.append(value)
        if s < SLABS - 1:
            for i in range(2):
                high = forward[s][i] - qc[i][0] * after[0] - qc[i][1] * after[1]
                green_ref[4 * (s + 1) + i : 4 * (s + 1) + i + 1, :] = high[0:1]
        if s > 0:
            for i in range(2):
                green_ref[4 * (s - 1) + 2 + i : 4 * (s - 1) + 3 + i, :] = now[i][0:1]
        after = now


def green_operator(rate):
    return pl.pallas_call(
        green_kernel,
        out_shape=shaped(128, 128),
        in_specs=[VMEM],
        out_specs=VMEM,
        scratch_shapes=[pltpu.VMEM((ROWS, 128), F32), pltpu.VMEM((SLABS, 24, 128), F32)],
        compiler_params=params(4),
        name="green_operator",
    )(rate)


def pre_kernel(
    place_ref, vel_hbm, part_hbm, rate_hbm, cell_hbm, high_hbm, low_hbm, inner_hbm, outer_hbm,
    packed_hbm, vel_ref, cell_ref, part_ref, rate_ref, out_ref, sems,
):
    even = place_ref[0] % 2 == 0
    order = (2, 3, 0, 1)
    into = [
        pltpu.make_async_copy(part_hbm, part_ref, sems.at[0]),
        pltpu.make_async_copy(rate_hbm, rate_ref, sems.at[1]),
    ]
    layers = [
        pltpu.make_async_copy(vel_hbm.at[:, x], vel_ref.at[:, x], sems.at[2 + x]) for x in order
    ]
    cells = pltpu.make_async_copy(cell_hbm, cell_ref, sems.at[6])
    for copy in into + layers + [cells]:
        copy.start()
    for copy in into:
        copy.wait()
    left = lax.broadcasted_iota(jnp.int32, (1, 128), 1) < SLOTS

    def pack(first, last):
        for r in range(first, last):
            part = [part_ref[i : i + 1, 128 * r : 128 * r + 128] for i in range(3)]
            part.append(rate_ref[0:1, 128 * r : 128 * r + 128])
            for n in range(2):
                one, two = part[2 * n], part[2 * n + 1]
                out_ref[2 * r, n : n + 1, :] = jnp.where(left, one, pltpu.roll(two, SLOTS, 1))
                out_ref[2 * r + 1, n : n + 1, :] = jnp.where(left, pltpu.roll(one, SLOTS, 1), two)

    out = []
    for n, x in enumerate(order):
        pack(16 * n, 16 * n + 16)
        layers[n].wait()
        target = high_hbm.at[:, x - 2] if x >= 2 else low_hbm.at[:, x]
        flat = pltpu.make_async_copy(vel_ref.at[:, x], target, sems.at[7 + n])
        flat.start()
        out.append(flat)
        bottom, top = vel_ref.at[:, x, 0:2], vel_ref.at[:, x, ROWS - 2 : ROWS]
        out.append(pltpu.make_async_copy(top, inner_hbm.at[:, x], sems.at[11 + n]))
        out.append(pltpu.make_async_copy(bottom, outer_hbm.at[:, x], sems.at[15 + n]))

        @pl.when(even)
        def _():
            out[-2].start()
            out[-1].start()

        @pl.when(jnp.logical_not(even))
        def _():
            pltpu.make_async_copy(bottom, inner_hbm.at[:, x], sems.at[11 + n]).start()
            pltpu.make_async_copy(top, outer_hbm.at[:, x], sems.at[15 + n]).start()

    out.append(pltpu.make_async_copy(out_ref, packed_hbm, sems.at[19]))
    out[-1].start()
    cells.wait()
    for copy in out:
        copy.wait()


def prepared(place, velocity, part_vel, part_rate, cells):
    return pl.pallas_call(
        pre_kernel,
        out_shape=(
            far_out(3, 2, ROWS, CZ),
            far_out(3, 2, ROWS, CZ),
            far_out(3, CX, 2, CZ),
            far_out(3, CX, 2, CZ),
            far_out(PEERS, 2, 128),
            held((3, CX, ROWS, CZ)),
            held((1, TOTAL), jnp.int32),
        ),
        in_specs=[SMEM] + [ANY] * 4,
        out_specs=(ANY,) * 5 + (VMEM,) * 2,
        scratch_shapes=[
            pltpu.VMEM((3, TOTAL), F32),
            pltpu.VMEM((1, TOTAL), F32),
            pltpu.VMEM((PEERS, 2, 128), F32),
            pltpu.SemaphoreType.DMA((20,)),
        ],
        compiler_params=params(16),
        name="prepare",
    )(place, *far_in(velocity, part_vel, part_rate, cells))


def halves(cells):
    plane = cells >> 10
    span = cells & (CZ - 1)
    return plane, span >> 7, span & 127


def span_table(high, low):
    width = high.shape[1]
    inner = lax.broadcasted_iota(jnp.int32, (128, width), 0) == low
    inner = inner.astype(F32).astype(BF16)
    rows = []
    for t in range(8):
        flag = (high == t).astype(F32).astype(BF16)
        rows.append(inner * flag)
    return jnp.concatenate(rows, axis=0)


def column_of(row, length):
    wide = jnp.broadcast_to(row, (length, length))
    here = lax.broadcasted_iota(jnp.int32, (length, length), 0) == lax.broadcasted_iota(
        jnp.int32, (length, length), 1
    )
    return jnp.broadcast_to(
        jnp.sum(jnp.where(here, wide, 0.0), axis=1, keepdims=True), (length, 128)
    )


def find_kernel(
    place_ref, vel_ref, cell_ref, inner_hbm, outer_hbm, rate_hbm, section_hbm, near_hbm, far_hbm, *refs
):
    outs, held_refs = refs[:6], refs[6:12]
    fluid_ref, scale_ref, tip_ref, fix_ref, solve_ref, base_ref = held_refs
    bf_ref, table_ref, rate_ref, wide_ref, pad_ref, section_ref, near_ref, far_ref, coef_ref, sems = (
        refs[12:]
    )
    below, above = pad_ref.at[:, :, 6:8, :], pad_ref.at[:, :, 8 + ROWS : 10 + ROWS, :]
    copies = [
        pltpu.make_async_copy(rate_hbm, rate_ref, sems.at[0]),
        pltpu.make_async_copy(near_hbm, near_ref, sems.at[1]),
        pltpu.make_async_copy(far_hbm, far_ref, sems.at[2]),
        pltpu.make_async_copy(section_hbm, section_ref, sems.at[3]),
        pltpu.make_async_copy(inner_hbm, below, sems.at[4]),
        pltpu.make_async_copy(outer_hbm, above, sems.at[5]),
    ]
    for copy in copies[:4]:
        copy.start()
    even = place_ref[0] % 2 == 0

    @pl.when(even)
    def _():
        pltpu.make_async_copy(outer_hbm, below, sems.at[4]).start()
        pltpu.make_async_copy(inner_hbm, above, sems.at[5]).start()

    @pl.when(jnp.logical_not(even))
    def _():
        copies[4].start()
        copies[5].start()

    for c in range(3):
        for x in range(CX):
            top = c * PLANES + x * ROWS
            bf_ref[top : top + ROWS, :] = vel_ref[c, x].astype(BF16)
    copies[0].wait()
    own_factors(place_ref[0], rate_ref, scale_ref, tip_ref, fix_ref, solve_ref, wide_ref)
    stores = [pltpu.make_async_copy(held_refs[n], outs[n], sems.at[5 + n]) for n in range(1, 5)]
    for store in stores:
        store.start()

    def stencil(c, x):
        for top in range(0, ROWS, 8):
            here = vel_ref[c, x, top : top + 8, :]
            rolled = {k: pltpu.roll(here, (-k) % CZ, 1) for k in (1, -1, 2, -2)}
            ddz = (TIME_STEP * 8.0 / 12.0) * (rolled[1] - rolled[-1]) - (TIME_STEP / 12.0) * (
                rolled[2] - rolled[-2]
            )

            def shifted(k):
                return pad_ref[c, x, 8 + top + k : 16 + top + k, :]

            near = jnp.concatenate([coef_ref[0, top : top + 8, :]] * 8, axis=1)
            far = jnp.concatenate([coef_ref[1, top : top + 8, :]] * 8, axis=1)
            ddy = near * (shifted(1) - shifted(-1)) + far * (shifted(2) - shifted(-2))
            base_ref[c, x, top : top + 8, :] = SECTION_KEEP * section_ref[c, x, top : top + 8, :] - (
                vel_ref[1, x, top : top + 8, :] * ddy + vel_ref[2, x, top : top + 8, :] * ddz
            )

    steps = TOTAL // CHUNK
    planes = [(c, x) for c in range(3) for x in range(CX)]
    share = len(planes) // (steps - 1)
    for step in range(steps):
        lanes = slice(step * CHUNK, (step + 1) * CHUNK)
        plane, high, low = halves(cell_ref[:, lanes])
        table_ref[...] = span_table(high, low)
        at = jnp.dot(bf_ref[...], table_ref[...], preferred_element_type=F32)
        mask = lax.broadcasted_iota(jnp.int32, (PLANES, CHUNK), 0) == plane
        for n in range(3):
            fluid_ref[n : n + 1, lanes] = jnp.sum(
                jnp.where(mask, at[n * PLANES : (n + 1) * PLANES], 0.0), axis=0, keepdims=True
            )
        stores.append(
            pltpu.make_async_copy(
                fluid_ref.at[:, lanes], outs[0].at[:, lanes], sems.at[13 + step]
            )
        )
        stores[-1].start()
        if step == 0:
            for copy in copies[1:]:
                copy.wait()
            coef_ref[0] = TIME_STEP * column_of(near_ref[...], ROWS)
            coef_ref[1] = TIME_STEP * column_of(far_ref[...], ROWS)
            for c, x in planes:
                pad_ref[c, x, 8 : 8 + ROWS, :] = vel_ref[c, x]
            continue
        for c, x in planes[share * (step - 1) : share * step]:
            stencil(c, x)
        stores.append(
            pltpu.make_async_copy(
                base_ref.at[step - 1], outs[5].at[step - 1], sems.at[9 + step]
            )
        )
        stores[-1].start()
    for store in stores:
        store.wait()


def find(place, vel_held, cells, inner, outer, *others):
    return pl.pallas_call(
        find_kernel,
        out_shape=(
            far_out(3, TOTAL),
            far_out(ROWS, 128),
            far_out(4, ROWS, 128),
            far_out(4, ROWS, 128),
            far_out(ROWS, 128),
            far_out(3, CX, ROWS, CZ),
        ),
        in_specs=[SMEM, VMEM, VMEM] + [ANY] * 6,
        out_specs=(ANY,) * 6,
        scratch_shapes=[
            pltpu.VMEM((3, TOTAL), F32),
            pltpu.VMEM((ROWS, 128), F32),
            pltpu.VMEM((4, ROWS, 128), F32),
            pltpu.VMEM((4, ROWS, 128), F32),
            pltpu.VMEM((ROWS, 128), F32),
            pltpu.VMEM((3, CX, ROWS, CZ), F32),
            pltpu.VMEM((3 * PLANES, CZ), BF16),
            pltpu.VMEM((CZ, CHUNK), BF16),
            pltpu.VMEM((8, 128), F32),
            pltpu.VMEM((ROWS, 128), F32),
            pltpu.VMEM((3, CX, ROWS + 16, CZ), F32),
            pltpu.VMEM((3, CX, ROWS, CZ), F32),
            pltpu.VMEM((1, ROWS), F32),
            pltpu.VMEM((1, ROWS), F32),
            pltpu.VMEM((2, ROWS, 128), F32),
            pltpu.SemaphoreType.DMA((13 + TOTAL // CHUNK,)),
        ],
        compiler_params=params(36),
        name="find",
    )(place, vel_held, cells, inner, outer, *far_in(*others))


def main_kernel(
    cell_ref, before_hbm, behind_hbm, moved_hbm,
    fluid_hbm, scale_hbm, tip_hbm, vel_hbm, base_hbm, count_hbm,
    part_hbm, tips_hbm, new_ref,
    vel_ref, before_ref, behind_ref, base_ref, table_ref, got_ref, deposit_ref, moved_ref,
    count_ref, part_ref, tips_ref,
    fluid_ref, scale_ref, tip_ref, sems,
):
    sources = [
        (moved_hbm, moved_ref),
        (count_hbm, count_ref),
        (fluid_hbm, fluid_ref),
        (scale_hbm, scale_ref),
        (tip_hbm, tip_ref),
        (vel_hbm, vel_ref),
        (before_hbm, before_ref),
        (behind_hbm, behind_ref),
        (base_hbm, base_ref),
    ]
    copies = [pltpu.make_async_copy(a, b, sems.at[n]) for n, (a, b) in enumerate(sources)]
    for copy in copies:
        copy.start()
    steps = TOTAL // CHUNK

    def lanes_of(step):
        return slice(step * CHUNK, (step + 1) * CHUNK)

    def spread_of(step):
        lanes = lanes_of(step)
        plane, high, low = halves(cell_ref[:, lanes])
        table_ref[...] = span_table(high, low)
        mask = lax.broadcasted_iota(jnp.int32, (PLANES, CHUNK), 0) == plane
        mask = mask.astype(F32).astype(BF16)
        live = got_ref[4:5, lanes] > 0.5
        rate = got_ref[3:4, lanes]
        spread = []
        for n in range(3):
            old = got_ref[n : n + 1, lanes]
            relative = fluid_ref[n : n + 1, lanes] - old
            part_ref[n : n + 1, lanes] = jnp.where(live, old + TIME_STEP * rate * relative, 0.0)
            push = jnp.where(live, -rate * relative, 0.0).astype(BF16)
            spread.append(mask * push)
        return jnp.concatenate(spread, axis=0)

    def unpack():
        left = lax.broadcasted_iota(jnp.int32, (1, 128), 1) < SLOTS
        lane = lax.broadcasted_iota(jnp.int32, (1, 128), 1)
        for r in range(PEERS // 2):
            lanes = slice(128 * r, 128 * r + 128)
            for n in range(2):
                one = moved_ref[2 * r, n : n + 1, :]
                two = moved_ref[2 * r + 1, n : n + 1, :]
                got_ref[2 * n : 2 * n + 1, lanes] = jnp.where(left, one, pltpu.roll(two, SLOTS, 1))
                got_ref[2 * n + 1 : 2 * n + 2, lanes] = jnp.where(
                    left, pltpu.roll(one, SLOTS, 1), two
                )
            limit = jnp.where(left, count_ref[0, 2 * r], count_ref[0, 2 * r + 1])
            got_ref[4:5, lanes] = ((lane & (SLOTS - 1)) < limit).astype(F32)

    def tiled(column, times):
        return jnp.concatenate([column] * times, axis=1)

    def stencil(c, x):
        def layer(i, top):
            if i < 0:
                return before_ref[c, 2 + i, top : top + 8, :]
            if i >= CX:
                return behind_ref[c, i - CX, top : top + 8, :]
            return vel_ref[c, i, top : top + 8, :]

        for top in range(0, ROWS, 8):
            ddx = (TIME_STEP * 8.0 / 12.0) * (layer(x + 1, top) - layer(x - 1, top)) - (
                TIME_STEP / 12.0
            ) * (layer(x + 2, top) - layer(x - 2, top))
            new_ref[c, x, top : top + 8, :] = (
                base_ref[c, x, top : top + 8, :] - vel_ref[0, x, top : top + 8, :] * ddx
            )

    planes = [(c, x) for c in range(3) for x in range(CX)]
    share = len(planes) // (steps - 1)
    for copy in copies[:3]:
        copy.wait()
    unpack()
    for step in range(steps):
        spread = spread_of(step)
        if step > 0:
            for c, x in planes[share * (step - 1) : share * step]:
                stencil(c, x)
        last = step == steps - 1
        if last:
            stores = [pltpu.make_async_copy(part_ref, part_hbm, sems.at[14])]
            stores[0].start()
        wide = CZ // 4 if last else CZ
        for z in range(0, CZ, wide):
            new = lax.dot_general(
                spread, table_ref[z : z + wide, :], (((1,), (1,)), ((), ())),
                preferred_element_type=F32,
            )
            if step == 0:
                deposit_ref[...] = new
                continue
            if not last:
                deposit_ref[...] += new
                continue
            for c, x in planes:
                base = c * PLANES + x * ROWS
                total = [None] * 4
                for t in range(ROWS // 8):
                    top = 8 * t
                    full = new_ref[c, x, top : top + 8, z : z + wide] + TIME_STEP * (
                        deposit_ref[base + top : base + top + 8, z : z + wide]
                        + new[base + top : base + top + 8]
                    )
                    new_ref[c, x, top : top + 8, z : z + wide] = full
                    scaled = full * tiled(scale_ref[top : top + 8, :], wide // 128)
                    for r in range(4):
                        weighted = scaled * tiled(tip_ref[r, top : top + 8, :], wide // 128)
                        total[r] = weighted if t == 0 else total[r] + weighted
                for r in (0, 2):
                    one, two = total[r], total[r + 1]
                    upper = lax.broadcasted_iota(jnp.int32, one.shape, 0) < 4
                    both = jnp.where(upper, one, two) + pltpu.roll(jnp.where(upper, two, one), 4, 0)
                    both = both + pltpu.roll(both, 6, 0)
                    both = both + pltpu.roll(both, 7, 0)
                    for k in range(wide // 128):
                        at = 8 * x + z // 128 + k
                        lanes = slice(128 * k, 128 * k + 128)
                        tips_ref[at, c, r : r + 1, :] = both[0:1, lanes]
                        tips_ref[at, c, r + 1 : r + 2, :] = both[4:5, lanes]
            for x in range(CX if last else 0):
                span = pl.ds(8 * x + z // 128, wide // 128)
                stores.append(
                    pltpu.make_async_copy(
                        tips_ref.at[span], tips_hbm.at[span], sems.at[14 + len(stores)]
                    )
                )
                stores[-1].start()
        if step == 0:
            for copy in copies[3:]:
                copy.wait()
    for store in stores:
        store.wait()


def main_part(cells, halos, moved, others):
    return pl.pallas_call(
        main_kernel,
        out_shape=(
            far_out(3, TOTAL),
            far_out(SLABS, 3, 4, 128),
            held((3, CX, ROWS, CZ)),
        ),
        in_specs=[VMEM] + [ANY] * 9,
        out_specs=(ANY, ANY, VMEM),
        scratch_shapes=[
            pltpu.VMEM((3, CX, ROWS, CZ), F32),
            pltpu.VMEM((3, 2, ROWS, CZ), F32),
            pltpu.VMEM((3, 2, ROWS, CZ), F32),
            pltpu.VMEM((3, CX, ROWS, CZ), F32),
            pltpu.VMEM((CZ, CHUNK), BF16),
            pltpu.VMEM((8, TOTAL), F32),
            pltpu.VMEM((3 * PLANES, CZ), F32),
            pltpu.VMEM((PEERS, 2, 128), F32),
            pltpu.SMEM((1, PEERS), jnp.int32),
            pltpu.VMEM((3, TOTAL), F32),
            pltpu.VMEM((SLABS, 3, 4, 128), F32),
            pltpu.VMEM((3, TOTAL), F32),
            pltpu.VMEM((ROWS, 128), F32),
            pltpu.VMEM((4, ROWS, 128), F32),
            pltpu.SemaphoreType.DMA((31,)),
        ],
        compiler_params=params(36),
        name="main_part",
    )(cells, *halos, moved, *far_in(*others))


WIDTH = 3 * CX * CZ // SLABS


def solve_kernel(tips_ref, green_ref, out_ref, all_ref):
    for s in range(SLABS):
        for c in range(3):
            all_ref[4 * s : 4 * s + 4, 128 * c : 128 * c + 128] = tips_ref[s, c]
    found = jnp.dot(green_ref[...], all_ref[...], precision=HIGH, preferred_element_type=F32)
    for s in range(SLABS):
        for c in range(3):
            out_ref[s, c] = found[4 * s : 4 * s + 4, 128 * c : 128 * c + 128]


def solved(tips, green):
    return pl.pallas_call(
        solve_kernel,
        out_shape=shaped(SLABS, 3, 4, 128),
        in_specs=[VMEM, VMEM],
        out_specs=VMEM,
        scratch_shapes=[pltpu.VMEM((4 * SLABS, WIDTH), F32)],
        compiler_params=params(4),
        name="solve",
    )(tips, green)


def local_kernel(vel_hbm, section_ref, scale_ref, solve_ref, section_hbm, out_ref, sems):
    loads = [pltpu.make_async_copy(vel_hbm.at[c], out_ref.at[c], sems.at[c]) for c in range(3)]
    for load in loads:
        load.start()
    store = pltpu.make_async_copy(section_ref, section_hbm, sems.at[3])
    store.start()
    whole = solve_ref[:, 0:ROWS]
    head = whole.astype(BF16)
    rest = (whole - head.astype(F32)).astype(BF16)
    left = jnp.concatenate([head, rest, head], axis=1)
    scale = jnp.concatenate([scale_ref[...]] * 8, axis=1)
    for c in range(3):
        loads[c].wait()
        for x in range(CX):
            value = section_ref[c, x] * scale
            high = value.astype(BF16)
            low = (value - high.astype(F32)).astype(BF16)
            right = jnp.concatenate([high, high, low], axis=0)
            out_ref[c, x] += jnp.dot(left, right, preferred_element_type=F32)
    store.wait()


def local_solve(velocity, section_new, scale, solve):
    return pl.pallas_call(
        local_kernel,
        out_shape=(far_out(3, CX, ROWS, CZ), held((3, CX, ROWS, CZ))),
        in_specs=[ANY, VMEM, VMEM, VMEM],
        out_specs=(ANY, VMEM),
        scratch_shapes=[pltpu.SemaphoreType.DMA((4,))],
        compiler_params=params(16),
        name="local_solve",
    )(*far_in(velocity), section_new, scale, solve)


def final_kernel(partial_ref, edge_ref, fix_ref, out_hbm, out_ref, sems):
    stores = []
    for c in range(3):
        for x in range(CX):
            for t in range(CZ // 128):
                lanes = slice(128 * t, 128 * t + 128)
                edge = edge_ref[8 * x + t, c]
                value = partial_ref[c, x, :, lanes]
                for r in range(4):
                    value = value - fix_ref[r] * edge[r : r + 1, :]
                out_ref[c, x, :, lanes] = value
            if x % 2 == 1:
                span = pl.ds(x - 1, 2)
                stores.append(
                    pltpu.make_async_copy(
                        out_ref.at[c, span], out_hbm.at[c, span], sems.at[len(stores)]
                    )
                )
                stores[-1].start()
    for copy in stores:
        copy.wait()


def finished(partial, edges, fix):
    return pl.pallas_call(
        final_kernel,
        out_shape=far_out(3, CX, ROWS, CZ),
        in_specs=[VMEM] * 3,
        out_specs=ANY,
        scratch_shapes=[pltpu.VMEM((3, CX, ROWS, CZ), F32), pltpu.SemaphoreType.DMA((6,))],
        compiler_params=params(16),
        name="finish",
    )(partial, edges, fix)


def local(velocity, section, diffusion, rhs_near, rhs_far, part_vel, part_rate, counts, cell_slot):
    n_gx, n_gy = lax.axis_size("gx"), lax.axis_size("gy")
    up_x = [(i, (i + 1) % n_gx) for i in range(n_gx)]
    down_x = [(t, s) for s, t in up_x]
    place = lax.axis_index("gy").astype(jnp.int32).reshape(1)
    high, low, inner, outer, packed, vel_held, cells = prepared(
        place, velocity, part_vel, part_rate.reshape(1, TOTAL), cell_slot
    )
    before = lax.ppermute(high, "gx", up_x)
    behind = lax.ppermute(low, "gx", down_x)
    inner = lax.ppermute(inner, "gy", [(i, i ^ 1) for i in range(n_gy)])
    outer = lax.ppermute(
        outer, "gy", [pair for i in range(1, n_gy - 1, 2) for pair in ((i, i + 1), (i + 1, i))]
    )
    moved = lax.all_to_all(packed, ("gx", "gy"), split_axis=0, concat_axis=0, tiled=True)
    fluid, scale, tip, fix, solve, base = find(
        place, vel_held, cells, inner, outer, diffusion.reshape(8, 128), section,
        rhs_near.reshape(1, ROWS), rhs_far.reshape(1, ROWS),
    )
    part_new, tips, new_held = main_part(
        cells, (before, behind), moved, (fluid, scale, tip, velocity, base, counts)
    )
    tips, diffusion = lax.optimization_barrier((tips, diffusion))
    all_tips = lax.all_to_all(tips, "gy", split_axis=0, concat_axis=0, tiled=True)
    rate = jnp.pad(
        diffusion.reshape(SLABS, ROWS).T, ((0, 0), (0, 128 - SLABS)), constant_values=1000.0
    )
    reply = solved(all_tips, green_operator(rate))
    reply, solve = lax.optimization_barrier((reply, solve))
    edges = lax.all_to_all(reply, "gy", split_axis=0, concat_axis=0, tiled=True)
    section_new, partial = local_solve(velocity, new_held, scale, solve)
    velocity_new = finished(partial, edges, fix)
    return (velocity_new, section_new, part_new)


def solution(mesh):
    return jax.shard_map(
        local,
        mesh=mesh,
        in_specs=(
            P(None, "gx", "gy", None),
            P(None, "gx", "gy", None),
            P(),
            P("gy"),
            P("gy"),
            P(None, ("gx", "gy")),
            P(("gx", "gy")),
            P(("gx", "gy"), None),
            P(("gx", "gy"), None),
        ),
        out_specs=(P(None, "gx", "gy", None), P(None, "gx", "gy", None), P(None, ("gx", "gy"))),
        check_vma=False,
    )
```

```python
import jax
import jax.numpy as jnp
from jax import lax
from jax.experimental import pallas as pl
from jax.experimental.pallas import tpu as pltpu
from jax.sharding import PartitionSpec as P

TIME_STEP = 0.2
SECTION_KEEP = -5.0 / 9.0
SECTION_GAIN = 15.0 / 16.0
MAIN = 2.5
NEAR = -4.0 / 3.0
FAR = 1.0 / 12.0
SLABS = 32
ROWS = 32
CX = 4
CZ = 1024
PLANES = CX * ROWS
SLOTS = 64
PEERS = 128
TOTAL = PEERS * SLOTS
CHUNK = 2048
HIGH = lax.Precision.HIGHEST
F32 = jnp.float32
BF16 = jnp.bfloat16


def params(mib=60):
    return pltpu.CompilerParams(vmem_limit_bytes=mib * 1024 * 1024)


VMEM = pl.BlockSpec(memory_space=pltpu.MemorySpace.VMEM)
SMEM = pl.BlockSpec(memory_space=pltpu.MemorySpace.SMEM)
ANY = pl.BlockSpec(memory_space=pltpu.MemorySpace.HBM)


def held(shape, dtype=F32):
    return pltpu.MemorySpace.VMEM(shape, dtype)


def shaped(*shape):
    return jax.ShapeDtypeStruct(shape, F32)


def far_out(*shape):
    return pltpu.MemorySpace.HBM(shape, F32)


def far_in(*arrays):
    return [pltpu.with_memory_space_constraint(a, pltpu.MemorySpace.HBM) for a in arrays]


def mm(a, b):
    return tuple(
        tuple(a[i][0] * b[0][j] + a[i][1] * b[1][j] for j in range(2)) for i in range(2)
    )


def add(a, b, sign=1.0):
    return tuple(tuple(a[i][j] + sign * b[i][j] for j in range(2)) for i in range(2))


def neg(a):
    return tuple(tuple(-e for e in row) for row in a)


def each(a, fn):
    return tuple(tuple(fn(e) for e in row) for row in a)


def inverse_of_one_minus(a):
    p, q, r, s = 1.0 - a[0][0], -a[0][1], -a[1][0], 1.0 - a[1][1]
    scale = 1.0 / (p * s - q * r)
    return ((s * scale, -q * scale), (-r * scale, p * scale))


def ldl(main_of, zero):
    recip, low1, low2 = [], [], []
    for k in range(ROWS):
        main = main_of(k)
        if k == 0:
            low1.append(zero)
            low2.append(zero)
            recip.append(1.0 / main)
            continue
        edge = NEAR - FAR * low1[k - 1]
        one = edge * recip[k - 1]
        two = FAR * recip[k - 2] if k > 1 else zero
        low1.append(one)
        low2.append(two)
        recip.append(1.0 / (main - edge * one - FAR * two))
    return recip, low1, low2


def substitute(rows, recip, low1, low2):
    half = []
    for k in range(ROWS):
        value = rows[k]
        if k > 0:
            value = value - low1[k] * half[k - 1]
        if k > 1:
            value = value - low2[k] * half[k - 2]
        half.append(value)
    full = [None] * ROWS
    for k in reversed(range(ROWS)):
        value = half[k] * recip[k]
        if k < ROWS - 1:
            value = value - low1[k + 1] * full[k + 1]
        if k < ROWS - 2:
            value = value - low2[k + 2] * full[k + 2]
        full[k] = value
    return full


ENDS = (0, 1, ROWS - 2, ROWS - 1)


def own_factors(slab, rate_ref, scale_ref, tip_ref, fix_ref, solve_ref, wide_ref):
    lane8 = lax.broadcasted_iota(jnp.int32, (8, 128), 1)
    row = rate_ref[pl.ds(slab // 4, 1), :]
    row = pltpu.roll(jnp.broadcast_to(row, (8, 128)), 128 - ROWS * (slab % 4), 1)
    inv_rate = 1.0 / column_of(row[0:1, 0:ROWS], ROWS)
    scale_ref[...] = SECTION_GAIN * inv_rate
    wide_ref[...] = inv_rate + MAIN
    recip, low1, low2 = ldl(
        lambda k: jnp.broadcast_to(wide_ref[k : k + 1, :], (8, 128)), jnp.zeros((8, 128), F32)
    )
    full = substitute([(lane8 == k).astype(F32) for k in range(ROWS)], recip, low1, low2)
    for k in range(ROWS):
        solve_ref[k : k + 1, :] = full[k][0:1]
    solve = solve_ref[...]
    cols = [jnp.broadcast_to(solve[:, n : n + 1], (ROWS, 128)) for n in ENDS]
    for n in range(4):
        tip_ref[n] = cols[n]
    has_low = jnp.where(slab > 0, 1.0, 0.0)
    has_high = jnp.where(slab < SLABS - 1, 1.0, 0.0)
    fix_ref[0] = FAR * cols[0] * has_low
    fix_ref[1] = (NEAR * cols[0] + FAR * cols[1]) * has_low
    fix_ref[2] = (FAR * cols[2] + NEAR * cols[3]) * has_high
    fix_ref[3] = FAR * cols[3] * has_high


def green_kernel(rate_ref, green_ref, wide_ref, coef_ref):
    lane8 = lax.broadcasted_iota(jnp.int32, (8, 128), 1)
    sub8 = lax.broadcasted_iota(jnp.int32, (8, 128), 0)
    wide_ref[...] = 1.0 / rate_ref[...] + MAIN
    zero = jnp.zeros((8, 128), F32)
    recip, low1, low2 = ldl(lambda k: jnp.broadcast_to(wide_ref[k : k + 1, :], (8, 128)), zero)
    units = [(sub8 == ENDS.index(k)).astype(F32) if k in ENDS else zero for k in range(ROWS)]
    full = substitute(units, recip, low1, low2)

    def entry(k, i):
        return jnp.broadcast_to(full[k][i : i + 1, :], (8, 128))

    not_first = ((lane8 > 0) & (lane8 < SLABS)).astype(F32)
    not_last = (lane8 < SLABS - 1).astype(F32)

    def lower(k):
        s0, s1 = entry(k, 0), entry(k, 1)
        return (FAR * s0 * not_first, (NEAR * s0 + FAR * s1) * not_first)

    def upper(k):
        s2, s3 = entry(k, 2), entry(k, 3)
        return ((FAR * s2 + NEAR * s3) * not_last, FAR * s3 * not_last)

    low_a = (lower(ENDS[0]), lower(ENDS[1]))
    low_c = (lower(ENDS[2]), lower(ENDS[3]))
    up_b = (upper(ENDS[0]), upper(ENDS[1]))
    up_e = (upper(ENDS[2]), upper(ENDS[3]))
    a, b, c, e = low_a, up_b, low_c, up_e
    for hop in (1, 2, 4, 8, 16):
        ax, bx, cx, ex = (each(m, lambda v: pltpu.roll(v, hop, 1)) for m in (a, b, c, e))
        w = inverse_of_one_minus(mm(a, ex))
        wa_c = mm(w, mm(a, cx))
        wb = mm(w, b)
        cy_ex = mm(c, ex)
        new_e = add(e, mm(cy_ex, wb))
        new_c = neg(add(mm(c, cx), mm(cy_ex, wa_c)))
        new_a = add(ax, mm(bx, wa_c))
        new_b = neg(mm(bx, wb))
        joined = lane8 >= hop

        def pick(new, old):
            return tuple(
                tuple(jnp.where(joined, new[i][j], old[i][j]) for j in range(2)) for i in range(2)
            )

        a, b, c, e = pick(new_a, a), pick(new_b, b), pick(new_c, c), pick(new_e, e)
    q = e
    q_prev = each(q, lambda v: jnp.where(lane8 > 0, pltpu.roll(v, 1, 1), 0.0))
    z = inverse_of_one_minus(mm(low_a, q_prev))
    gain = mm(mm(low_c, q_prev), z)
    carry = add(low_c, mm(gain, low_a))
    z_low = mm(z, low_a)
    z_up = mm(z, up_b)
    for group, mats in enumerate(((carry, gain), (z, z_low), (z_up, q))):
        block = jnp.zeros((8, 128), F32)
        for n, m in enumerate(mats):
            for i in range(2):
                for j in range(2):
                    block = jnp.where(sub8 == 4 * n + 2 * i + j, m[i][j], block)
        for s in range(SLABS):
            coef_ref[s, 8 * group : 8 * group + 8, :] = jnp.broadcast_to(block[:, s : s + 1], (8, 128))

    def coef(s, n):
        def one(i, j):
            at = 4 * n + 2 * i + j
            return jnp.broadcast_to(coef_ref[s, at : at + 1, :], (8, 128))

        return tuple(tuple(one(i, j) for j in range(2)) for i in range(2))

    def at_lane(n):
        return lane8 == n

    forward = []
    prev = None
    for s in range(SLABS):
        m, g = coef(s, 0), coef(s, 1)
        now = []
        for i in range(2):
            value = jnp.where(at_lane(4 * s), g[i][0], 0.0)
            value = jnp.where(at_lane(4 * s + 1), g[i][1], value)
            value = jnp.where(at_lane(4 * s + 2 + i), 1.0, value)
            if prev is not None:
                value = value - m[i][0] * prev[0] - m[i][1] * prev[1]
            now.append(value)
        forward.append(now)
        prev = now
    for row in (0, 1, 4 * SLABS - 2, 4 * SLABS - 1):
        green_ref[row : row + 1, :] = jnp.zeros((1, 128), F32)
    after = None
    for s in reversed(range(SLABS)):
        zc, zl, zu, qc = coef(s, 2), coef(s, 3), coef(s, 4), coef(s, 5)
        now = []
        for i in range(2):
            value = jnp.where(at_lane(4 * s), zc[i][0], 0.0)
            value = jnp.where(at_lane(4 * s + 1), zc[i][1], value)
            if s > 0:
                value = value - zl[i][0] * forward[s - 1][0] - zl[i][1] * forward[s - 1][1]
            if after is not None:
                value = value - zu[i][0] * after[0] - zu[i][1] * after[1]
            now.append(value)
        if s < SLABS - 1:
            for i in range(2):
                high = forward[s][i] - qc[i][0] * after[0] - qc[i][1] * after[1]
                green_ref[4 * (s + 1) + i : 4 * (s + 1) + i + 1, :] = high[0:1]
        if s > 0:
            for i in range(2):
                green_ref[4 * (s - 1) + 2 + i : 4 * (s - 1) + 3 + i, :] = now[i][0:1]
        after = now


def green_operator(rate):
    return pl.pallas_call(
        green_kernel,
        out_shape=shaped(128, 128),
        in_specs=[VMEM],
        out_specs=VMEM,
        scratch_shapes=[pltpu.VMEM((ROWS, 128), F32), pltpu.VMEM((SLABS, 24, 128), F32)],
        compiler_params=params(4),
        name="green_operator",
    )(rate)


def pre_kernel(
    place_ref, vel_hbm, part_hbm, rate_hbm, cell_hbm, high_hbm, low_hbm, inner_hbm, outer_hbm,
    packed_hbm, vel_ref, cell_ref, part_ref, rate_ref, out_ref, sems,
):
    even = place_ref[0] % 2 == 0
    order = (2, 3, 0, 1)
    into = [
        pltpu.make_async_copy(part_hbm, part_ref, sems.at[0]),
        pltpu.make_async_copy(rate_hbm, rate_ref, sems.at[1]),
    ]
    layers = [
        pltpu.make_async_copy(vel_hbm.at[:, x], vel_ref.at[:, x], sems.at[2 + x]) for x in order
    ]
    cells = pltpu.make_async_copy(cell_hbm, cell_ref, sems.at[6])
    for copy in into + layers + [cells]:
        copy.start()
    for copy in into:
        copy.wait()
    left = lax.broadcasted_iota(jnp.int32, (1, 128), 1) < SLOTS

    def pack(first, last):
        for r in range(first, last):
            part = [part_ref[i : i + 1, 128 * r : 128 * r + 128] for i in range(3)]
            part.append(rate_ref[0:1, 128 * r : 128 * r + 128])
            for n in range(2):
                one, two = part[2 * n], part[2 * n + 1]
                out_ref[2 * r, n : n + 1, :] = jnp.where(left, one, pltpu.roll(two, SLOTS, 1))
                out_ref[2 * r + 1, n : n + 1, :] = jnp.where(left, pltpu.roll(one, SLOTS, 1), two)

    out = []
    for n, x in enumerate(order):
        pack(16 * n, 16 * n + 16)
        layers[n].wait()
        target = high_hbm.at[:, x - 2] if x >= 2 else low_hbm.at[:, x]
        flat = pltpu.make_async_copy(vel_ref.at[:, x], target, sems.at[7 + n])
        flat.start()
        out.append(flat)
        bottom, top = vel_ref.at[:, x, 0:2], vel_ref.at[:, x, ROWS - 2 : ROWS]
        out.append(pltpu.make_async_copy(top, inner_hbm.at[:, x], sems.at[11 + n]))
        out.append(pltpu.make_async_copy(bottom, outer_hbm.at[:, x], sems.at[15 + n]))

        @pl.when(even)
        def _():
            out[-2].start()
            out[-1].start()

        @pl.when(jnp.logical_not(even))
        def _():
            pltpu.make_async_copy(bottom, inner_hbm.at[:, x], sems.at[11 + n]).start()
            pltpu.make_async_copy(top, outer_hbm.at[:, x], sems.at[15 + n]).start()

    out.append(pltpu.make_async_copy(out_ref, packed_hbm, sems.at[19]))
    out[-1].start()
    cells.wait()
    for copy in out:
        copy.wait()


def prepared(place, velocity, part_vel, part_rate, cells):
    return pl.pallas_call(
        pre_kernel,
        out_shape=(
            far_out(3, 2, ROWS, CZ),
            far_out(3, 2, ROWS, CZ),
            far_out(3, CX, 2, CZ),
            far_out(3, CX, 2, CZ),
            far_out(PEERS, 2, 128),
            held((3, CX, ROWS, CZ)),
            held((1, TOTAL), jnp.int32),
        ),
        in_specs=[SMEM] + [ANY] * 4,
        out_specs=(ANY,) * 5 + (VMEM,) * 2,
        scratch_shapes=[
            pltpu.VMEM((3, TOTAL), F32),
            pltpu.VMEM((1, TOTAL), F32),
            pltpu.VMEM((PEERS, 2, 128), F32),
            pltpu.SemaphoreType.DMA((20,)),
        ],
        compiler_params=params(16),
        name="prepare",
    )(place, *far_in(velocity, part_vel, part_rate, cells))


def halves(cells):
    plane = cells >> 10
    span = cells & (CZ - 1)
    return plane, span >> 7, span & 127


def span_table(high, low):
    width = high.shape[1]
    inner = lax.broadcasted_iota(jnp.int32, (128, width), 0) == low
    inner = inner.astype(F32).astype(BF16)
    rows = []
    for t in range(8):
        flag = (high == t).astype(F32).astype(BF16)
        rows.append(inner * flag)
    return jnp.concatenate(rows, axis=0)


def column_of(row, length):
    wide = jnp.broadcast_to(row, (length, length))
    here = lax.broadcasted_iota(jnp.int32, (length, length), 0) == lax.broadcasted_iota(
        jnp.int32, (length, length), 1
    )
    return jnp.broadcast_to(
        jnp.sum(jnp.where(here, wide, 0.0), axis=1, keepdims=True), (length, 128)
    )


def find_kernel(
    place_ref, vel_ref, cell_ref, rate_hbm, *refs,
):
    outs, held_refs = refs[:5], refs[5:10]
    fluid_ref, scale_ref, tip_ref, fix_ref, solve_ref = held_refs
    bf_ref, table_ref, rate_ref, wide_ref, sems = refs[10:]
    copies = [
        pltpu.make_async_copy(rate_hbm, rate_ref, sems.at[0]),
    ]
    for copy in copies:
        copy.start()
    for c in range(3):
        for x in range(CX):
            top = c * PLANES + x * ROWS
            bf_ref[top : top + ROWS, :] = vel_ref[c, x].astype(BF16)
    for copy in copies:
        copy.wait()
    own_factors(place_ref[0], rate_ref, scale_ref, tip_ref, fix_ref, solve_ref, wide_ref)
    stores = [
        pltpu.make_async_copy(held_refs[n], outs[n], sems.at[1 + n]) for n in range(1, 5)
    ]
    for store in stores:
        store.start()
    for step in range(TOTAL // CHUNK):
        lanes = slice(step * CHUNK, (step + 1) * CHUNK)
        plane, high, low = halves(cell_ref[:, lanes])
        table_ref[...] = span_table(high, low)
        at = jnp.dot(bf_ref[...], table_ref[...], preferred_element_type=F32)
        mask = lax.broadcasted_iota(jnp.int32, (PLANES, CHUNK), 0) == plane
        for n in range(3):
            fluid_ref[n : n + 1, lanes] = jnp.sum(
                jnp.where(mask, at[n * PLANES : (n + 1) * PLANES], 0.0), axis=0, keepdims=True
            )
        stores.append(
            pltpu.make_async_copy(
                fluid_ref.at[:, lanes], outs[0].at[:, lanes], sems.at[6 + step]
            )
        )
        stores[-1].start()
    for store in stores:
        store.wait()


def find(place, vel_held, cells, rate):
    return pl.pallas_call(
        find_kernel,
        out_shape=(
            far_out(3, TOTAL),
            far_out(ROWS, 128),
            far_out(4, ROWS, 128),
            far_out(4, ROWS, 128),
            far_out(ROWS, 128),
        ),
        in_specs=[SMEM, VMEM, VMEM, ANY],
        out_specs=(ANY,) * 5,
        scratch_shapes=[
            pltpu.VMEM((3, TOTAL), F32),
            pltpu.VMEM((ROWS, 128), F32),
            pltpu.VMEM((4, ROWS, 128), F32),
            pltpu.VMEM((4, ROWS, 128), F32),
            pltpu.VMEM((ROWS, 128), F32),
            pltpu.VMEM((3 * PLANES, CZ), BF16),
            pltpu.VMEM((CZ, CHUNK), BF16),
            pltpu.VMEM((8, 128), F32),
            pltpu.VMEM((ROWS, 128), F32),
            pltpu.SemaphoreType.DMA((6 + TOTAL // CHUNK,)),
        ],
        compiler_params=params(28),
        name="find",
    )(place, vel_held, cells, *far_in(rate))


def main_kernel(
    place_ref, cell_ref, inner_hbm, outer_hbm, before_hbm, behind_hbm, moved_hbm,
    fluid_hbm, scale_hbm, tip_hbm, vel_hbm, section_hbm, count_hbm, near_hbm, far_hbm,
    part_hbm, tips_hbm, new_ref,
    pad_ref, before_ref, behind_ref, section_ref, table_ref, got_ref, deposit_ref, moved_ref,
    count_ref, near_ref, far_ref, part_ref, tips_ref, coef_ref,
    fluid_ref, scale_ref, tip_ref, sems,
):
    sources = [
        (moved_hbm, moved_ref),
        (count_hbm, count_ref),
        (fluid_hbm, fluid_ref),
        (scale_hbm, scale_ref),
        (tip_hbm, tip_ref),
        (near_hbm, near_ref),
        (far_hbm, far_ref),
        (vel_hbm, pad_ref.at[:, :, 8 : 8 + ROWS, :]),
        (inner_hbm, pad_ref.at[:, :, 6:8, :]),
        (outer_hbm, pad_ref.at[:, :, 8 + ROWS : 10 + ROWS, :]),
        (before_hbm, before_ref),
        (behind_hbm, behind_ref),
        (section_hbm, section_ref),
    ]
    copies = [pltpu.make_async_copy(a, b, sems.at[n]) for n, (a, b) in enumerate(sources)]
    swaps = [n for n, (a, b) in enumerate(sources) if a is inner_hbm or a is outer_hbm]
    for n, copy in enumerate(copies):
        if n not in swaps:
            copy.start()
    even = place_ref[0] % 2 == 0

    @pl.when(even)
    def _():
        for n, source in zip(swaps, (outer_hbm, inner_hbm)):
            pltpu.make_async_copy(source, sources[n][1], sems.at[n]).start()

    @pl.when(jnp.logical_not(even))
    def _():
        for n in swaps:
            copies[n].start()

    steps = TOTAL // CHUNK

    def lanes_of(step):
        return slice(step * CHUNK, (step + 1) * CHUNK)

    def spread_of(step):
        lanes = lanes_of(step)
        plane, high, low = halves(cell_ref[:, lanes])
        table_ref[...] = span_table(high, low)
        mask = lax.broadcasted_iota(jnp.int32, (PLANES, CHUNK), 0) == plane
        mask = mask.astype(F32).astype(BF16)
        live = got_ref[4:5, lanes] > 0.5
        rate = got_ref[3:4, lanes]
        spread = []
        for n in range(3):
            old = got_ref[n : n + 1, lanes]
            relative = fluid_ref[n : n + 1, lanes] - old
            part_ref[n : n + 1, lanes] = jnp.where(live, old + TIME_STEP * rate * relative, 0.0)
            push = jnp.where(live, -rate * relative, 0.0).astype(BF16)
            spread.append(mask * push)
        return jnp.concatenate(spread, axis=0)

    def unpack():
        left = lax.broadcasted_iota(jnp.int32, (1, 128), 1) < SLOTS
        lane = lax.broadcasted_iota(jnp.int32, (1, 128), 1)
        for r in range(PEERS // 2):
            lanes = slice(128 * r, 128 * r + 128)
            for n in range(2):
                one = moved_ref[2 * r, n : n + 1, :]
                two = moved_ref[2 * r + 1, n : n + 1, :]
                got_ref[2 * n : 2 * n + 1, lanes] = jnp.where(left, one, pltpu.roll(two, SLOTS, 1))
                got_ref[2 * n + 1 : 2 * n + 2, lanes] = jnp.where(
                    left, pltpu.roll(one, SLOTS, 1), two
                )
            limit = jnp.where(left, count_ref[0, 2 * r], count_ref[0, 2 * r + 1])
            got_ref[4:5, lanes] = ((lane & (SLOTS - 1)) < limit).astype(F32)

    def tiled(column, times):
        return jnp.concatenate([column] * times, axis=1)

    def stencil(c, x):
        def layer(i, top):
            if i < 0:
                return before_ref[c, 2 + i, top : top + 8, :]
            if i >= CX:
                return behind_ref[c, i - CX, top : top + 8, :]
            return pad_ref[c, i, 8 + top : 16 + top, :]

        for t in range(ROWS // 8):
            top = 8 * t
            here = layer(x, top)
            ddx = (TIME_STEP * 8.0 / 12.0) * (layer(x + 1, top) - layer(x - 1, top)) - (
                TIME_STEP / 12.0
            ) * (
                layer(x + 2, top) - layer(x - 2, top)
            )
            rolled = {k: pltpu.roll(here, (-k) % CZ, 1) for k in (1, -1, 2, -2)}
            ddz = (TIME_STEP * 8.0 / 12.0) * (rolled[1] - rolled[-1]) - (TIME_STEP / 12.0) * (
                rolled[2] - rolled[-2]
            )

            def shifted(k):
                return pad_ref[c, x, 8 + top + k : 16 + top + k, :]

            near = tiled(coef_ref[0, top : top + 8, :], 8)
            far = tiled(coef_ref[1, top : top + 8, :], 8)
            ddy = near * (shifted(1) - shifted(-1)) + far * (shifted(2) - shifted(-2))
            moved = (
                pad_ref[0, x, 8 + top : 16 + top, :] * ddx
                + pad_ref[1, x, 8 + top : 16 + top, :] * ddy
                + pad_ref[2, x, 8 + top : 16 + top, :] * ddz
            )
            new_ref[c, x, top : top + 8, :] = (
                SECTION_KEEP * section_ref[c, x, top : top + 8, :] - moved
            )

    planes = [(c, x) for c in range(3) for x in range(CX)]
    share = len(planes) // (steps - 1)
    for copy in copies[:3]:
        copy.wait()
    unpack()
    for step in range(steps):
        spread = spread_of(step)
        if step > 0:
            for c, x in planes[share * (step - 1) : share * step]:
                stencil(c, x)
        last = step == steps - 1
        if last:
            stores = [pltpu.make_async_copy(part_ref, part_hbm, sems.at[14])]
            stores[0].start()
        wide = CZ // 4 if last else CZ
        for z in range(0, CZ, wide):
            new = lax.dot_general(
                spread, table_ref[z : z + wide, :], (((1,), (1,)), ((), ())),
                preferred_element_type=F32,
            )
            if step == 0:
                deposit_ref[...] = new
                continue
            if not last:
                deposit_ref[...] += new
                continue
            for c, x in planes:
                base = c * PLANES + x * ROWS
                total = [None] * 4
                for t in range(ROWS // 8):
                    top = 8 * t
                    full = new_ref[c, x, top : top + 8, z : z + wide] + TIME_STEP * (
                        deposit_ref[base + top : base + top + 8, z : z + wide]
                        + new[base + top : base + top + 8]
                    )
                    new_ref[c, x, top : top + 8, z : z + wide] = full
                    scaled = full * tiled(scale_ref[top : top + 8, :], wide // 128)
                    for r in range(4):
                        weighted = scaled * tiled(tip_ref[r, top : top + 8, :], wide // 128)
                        total[r] = weighted if t == 0 else total[r] + weighted
                for r in (0, 2):
                    one, two = total[r], total[r + 1]
                    upper = lax.broadcasted_iota(jnp.int32, one.shape, 0) < 4
                    both = jnp.where(upper, one, two) + pltpu.roll(jnp.where(upper, two, one), 4, 0)
                    both = both + pltpu.roll(both, 6, 0)
                    both = both + pltpu.roll(both, 7, 0)
                    for k in range(wide // 128):
                        at = 8 * x + z // 128 + k
                        lanes = slice(128 * k, 128 * k + 128)
                        tips_ref[at, c, r : r + 1, :] = both[0:1, lanes]
                        tips_ref[at, c, r + 1 : r + 2, :] = both[4:5, lanes]
            for x in range(CX if last else 0):
                span = pl.ds(8 * x + z // 128, wide // 128)
                stores.append(
                    pltpu.make_async_copy(
                        tips_ref.at[span], tips_hbm.at[span], sems.at[14 + len(stores)]
                    )
                )
                stores[-1].start()
        if step == 0:
            for copy in copies[3:]:
                copy.wait()
            coef_ref[0] = TIME_STEP * column_of(near_ref[...], ROWS)
            coef_ref[1] = TIME_STEP * column_of(far_ref[...], ROWS)
    for store in stores:
        store.wait()


def main_part(place, cells, halos, moved, others):
    return pl.pallas_call(
        main_kernel,
        out_shape=(
            far_out(3, TOTAL),
            far_out(SLABS, 3, 4, 128),
            held((3, CX, ROWS, CZ)),
        ),
        in_specs=[SMEM, VMEM] + [ANY] * 13,
        out_specs=(ANY, ANY, VMEM),
        scratch_shapes=[
            pltpu.VMEM((3, CX, ROWS + 16, CZ), F32),
            pltpu.VMEM((3, 2, ROWS, CZ), F32),
            pltpu.VMEM((3, 2, ROWS, CZ), F32),
            pltpu.VMEM((3, CX, ROWS, CZ), F32),
            pltpu.VMEM((CZ, CHUNK), BF16),
            pltpu.VMEM((8, TOTAL), F32),
            pltpu.VMEM((3 * PLANES, CZ), F32),
            pltpu.VMEM((PEERS, 2, 128), F32),
            pltpu.SMEM((1, PEERS), jnp.int32),
            pltpu.VMEM((1, ROWS), F32),
            pltpu.VMEM((1, ROWS), F32),
            pltpu.VMEM((3, TOTAL), F32),
            pltpu.VMEM((SLABS, 3, 4, 128), F32),
            pltpu.VMEM((2, ROWS, 128), F32),
            pltpu.VMEM((3, TOTAL), F32),
            pltpu.VMEM((ROWS, 128), F32),
            pltpu.VMEM((4, ROWS, 128), F32),
            pltpu.SemaphoreType.DMA((31,)),
        ],
        compiler_params=params(36),
        name="main_part",
    )(place, cells, *halos, moved, *far_in(*others))


WIDTH = 3 * CX * CZ // SLABS


def solve_kernel(tips_ref, green_ref, out_ref, all_ref):
    for s in range(SLABS):
        for c in range(3):
            all_ref[4 * s : 4 * s + 4, 128 * c : 128 * c + 128] = tips_ref[s, c]
    found = jnp.dot(green_ref[...], all_ref[...], precision=HIGH, preferred_element_type=F32)
    for s in range(SLABS):
        for c in range(3):
            out_ref[s, c] = found[4 * s : 4 * s + 4, 128 * c : 128 * c + 128]


def solved(tips, green):
    return pl.pallas_call(
        solve_kernel,
        out_shape=shaped(SLABS, 3, 4, 128),
        in_specs=[VMEM, VMEM],
        out_specs=VMEM,
        scratch_shapes=[pltpu.VMEM((4 * SLABS, WIDTH), F32)],
        compiler_params=params(4),
        name="solve",
    )(tips, green)


def local_kernel(vel_hbm, section_ref, scale_ref, solve_ref, section_hbm, out_ref, sems):
    loads = [pltpu.make_async_copy(vel_hbm.at[c], out_ref.at[c], sems.at[c]) for c in range(3)]
    for load in loads:
        load.start()
    store = pltpu.make_async_copy(section_ref, section_hbm, sems.at[3])
    store.start()
    whole = solve_ref[:, 0:ROWS]
    head = whole.astype(BF16)
    rest = (whole - head.astype(F32)).astype(BF16)
    left = jnp.concatenate([head, rest, head], axis=1)
    scale = jnp.concatenate([scale_ref[...]] * 8, axis=1)
    for c in range(3):
        loads[c].wait()
        for x in range(CX):
            value = section_ref[c, x] * scale
            high = value.astype(BF16)
            low = (value - high.astype(F32)).astype(BF16)
            right = jnp.concatenate([high, high, low], axis=0)
            out_ref[c, x] += jnp.dot(left, right, preferred_element_type=F32)
    store.wait()


def local_solve(velocity, section_new, scale, solve):
    return pl.pallas_call(
        local_kernel,
        out_shape=(far_out(3, CX, ROWS, CZ), held((3, CX, ROWS, CZ))),
        in_specs=[ANY, VMEM, VMEM, VMEM],
        out_specs=(ANY, VMEM),
        scratch_shapes=[pltpu.SemaphoreType.DMA((4,))],
        compiler_params=params(16),
        name="local_solve",
    )(*far_in(velocity), section_new, scale, solve)


def final_kernel(partial_ref, edge_ref, fix_ref, out_hbm, out_ref, sems):
    stores = []
    for c in range(3):
        for x in range(CX):
            for t in range(CZ // 128):
                lanes = slice(128 * t, 128 * t + 128)
                edge = edge_ref[8 * x + t, c]
                value = partial_ref[c, x, :, lanes]
                for r in range(4):
                    value = value - fix_ref[r] * edge[r : r + 1, :]
                out_ref[c, x, :, lanes] = value
            if x % 2 == 1:
                span = pl.ds(x - 1, 2)
                stores.append(
                    pltpu.make_async_copy(
                        out_ref.at[c, span], out_hbm.at[c, span], sems.at[len(stores)]
                    )
                )
                stores[-1].start()
    for copy in stores:
        copy.wait()


def finished(partial, edges, fix):
    return pl.pallas_call(
        final_kernel,
        out_shape=far_out(3, CX, ROWS, CZ),
        in_specs=[VMEM] * 3,
        out_specs=ANY,
        scratch_shapes=[pltpu.VMEM((3, CX, ROWS, CZ), F32), pltpu.SemaphoreType.DMA((6,))],
        compiler_params=params(16),
        name="finish",
    )(partial, edges, fix)


def local(velocity, section, diffusion, rhs_near, rhs_far, part_vel, part_rate, counts, cell_slot):
    n_gx, n_gy = lax.axis_size("gx"), lax.axis_size("gy")
    up_x = [(i, (i + 1) % n_gx) for i in range(n_gx)]
    down_x = [(t, s) for s, t in up_x]
    place = lax.axis_index("gy").astype(jnp.int32).reshape(1)
    high, low, inner, outer, packed, vel_held, cells = prepared(
        place, velocity, part_vel, part_rate.reshape(1, TOTAL), cell_slot
    )
    before = lax.ppermute(high, "gx", up_x)
    behind = lax.ppermute(low, "gx", down_x)
    inner = lax.ppermute(inner, "gy", [(i, i ^ 1) for i in range(n_gy)])
    outer = lax.ppermute(
        outer, "gy", [pair for i in range(1, n_gy - 1, 2) for pair in ((i, i + 1), (i + 1, i))]
    )
    moved = lax.all_to_all(packed, ("gx", "gy"), split_axis=0, concat_axis=0, tiled=True)
    fluid, scale, tip, fix, solve = find(place, vel_held, cells, diffusion.reshape(8, 128))
    part_new, tips, new_held = main_part(
        place, cells, (inner, outer, before, behind), moved,
        (fluid, scale, tip, velocity, section, counts, rhs_near.reshape(1, ROWS), rhs_far.reshape(1, ROWS)),
    )
    tips, diffusion = lax.optimization_barrier((tips, diffusion))
    all_tips = lax.all_to_all(tips, "gy", split_axis=0, concat_axis=0, tiled=True)
    rate = jnp.pad(
        diffusion.reshape(SLABS, ROWS).T, ((0, 0), (0, 128 - SLABS)), constant_values=1000.0
    )
    reply = solved(all_tips, green_operator(rate))
    reply, solve = lax.optimization_barrier((reply, solve))
    edges = lax.all_to_all(reply, "gy", split_axis=0, concat_axis=0, tiled=True)
    section_new, partial = local_solve(velocity, new_held, scale, solve)
    velocity_new = finished(partial, edges, fix)
    return (velocity_new, section_new, part_new)


def solution(mesh):
    return jax.shard_map(
        local,
        mesh=mesh,
        in_specs=(
            P(None, "gx", "gy", None),
            P(None, "gx", "gy", None),
            P(),
            P("gy"),
            P("gy"),
            P(None, ("gx", "gy")),
            P(("gx", "gy")),
            P(("gx", "gy"), None),
            P(("gx", "gy"), None),
        ),
        out_specs=(P(None, "gx", "gy", None), P(None, "gx", "gy", None), P(None, ("gx", "gy"))),
        check_vma=False,
    )
```

```python
import jax
import jax.numpy as jnp
from jax import lax
from jax.experimental import pallas as pl
from jax.experimental.pallas import tpu as pltpu
from jax.sharding import PartitionSpec as P

TIME_STEP = 0.2
SECTION_KEEP = -5.0 / 9.0
SECTION_GAIN = 15.0 / 16.0
MAIN = 2.5
NEAR = -4.0 / 3.0
FAR = 1.0 / 12.0
SLABS = 32
ROWS = 32
CX = 4
CZ = 1024
PLANES = CX * ROWS
SLOTS = 64
PEERS = 128
TOTAL = PEERS * SLOTS
CHUNK = 2048
HIGH = lax.Precision.HIGHEST
F32 = jnp.float32
BF16 = jnp.bfloat16


def params(mib=60):
    return pltpu.CompilerParams(vmem_limit_bytes=mib * 1024 * 1024)


VMEM = pl.BlockSpec(memory_space=pltpu.MemorySpace.VMEM)
SMEM = pl.BlockSpec(memory_space=pltpu.MemorySpace.SMEM)
ANY = pl.BlockSpec(memory_space=pltpu.MemorySpace.HBM)


def held(shape, dtype=F32):
    return pltpu.MemorySpace.VMEM(shape, dtype)


def shaped(*shape):
    return jax.ShapeDtypeStruct(shape, F32)


def far_out(*shape):
    return pltpu.MemorySpace.HBM(shape, F32)


def far_in(*arrays):
    return [pltpu.with_memory_space_constraint(a, pltpu.MemorySpace.HBM) for a in arrays]


def mm(a, b):
    return tuple(
        tuple(a[i][0] * b[0][j] + a[i][1] * b[1][j] for j in range(2)) for i in range(2)
    )


def add(a, b, sign=1.0):
    return tuple(tuple(a[i][j] + sign * b[i][j] for j in range(2)) for i in range(2))


def neg(a):
    return tuple(tuple(-e for e in row) for row in a)


def each(a, fn):
    return tuple(tuple(fn(e) for e in row) for row in a)


def inverse_of_one_minus(a):
    p, q, r, s = 1.0 - a[0][0], -a[0][1], -a[1][0], 1.0 - a[1][1]
    scale = 1.0 / (p * s - q * r)
    return ((s * scale, -q * scale), (-r * scale, p * scale))


def ldl(main_of, zero):
    recip, low1, low2 = [], [], []
    for k in range(ROWS):
        main = main_of(k)
        if k == 0:
            low1.append(zero)
            low2.append(zero)
            recip.append(1.0 / main)
            continue
        edge = NEAR - FAR * low1[k - 1]
        one = edge * recip[k - 1]
        two = FAR * recip[k - 2] if k > 1 else zero
        low1.append(one)
        low2.append(two)
        recip.append(1.0 / (main - edge * one - FAR * two))
    return recip, low1, low2


def substitute(rows, recip, low1, low2):
    half = []
    for k in range(ROWS):
        value = rows[k]
        if k > 0:
            value = value - low1[k] * half[k - 1]
        if k > 1:
            value = value - low2[k] * half[k - 2]
        half.append(value)
    full = [None] * ROWS
    for k in reversed(range(ROWS)):
        value = half[k] * recip[k]
        if k < ROWS - 1:
            value = value - low1[k + 1] * full[k + 1]
        if k < ROWS - 2:
            value = value - low2[k + 2] * full[k + 2]
        full[k] = value
    return full


ENDS = (0, 1, ROWS - 2, ROWS - 1)


def own_factors(slab, rate_ref, scale_ref, tip_ref, fix_ref, solve_ref, wide_ref):
    lane8 = lax.broadcasted_iota(jnp.int32, (8, 128), 1)
    row = rate_ref[pl.ds(slab // 4, 1), :]
    row = pltpu.roll(jnp.broadcast_to(row, (8, 128)), 128 - ROWS * (slab % 4), 1)
    inv_rate = 1.0 / column_of(row[0:1, 0:ROWS], ROWS)
    scale_ref[...] = SECTION_GAIN * inv_rate
    wide_ref[...] = inv_rate + MAIN
    recip, low1, low2 = ldl(
        lambda k: jnp.broadcast_to(wide_ref[k : k + 1, :], (8, 128)), jnp.zeros((8, 128), F32)
    )
    full = substitute([(lane8 == k).astype(F32) for k in range(ROWS)], recip, low1, low2)
    for k in range(ROWS):
        solve_ref[k : k + 1, :] = full[k][0:1]
    solve = solve_ref[...]
    cols = [jnp.broadcast_to(solve[:, n : n + 1], (ROWS, 128)) for n in ENDS]
    for n in range(4):
        tip_ref[n] = cols[n]
    has_low = jnp.where(slab > 0, 1.0, 0.0)
    has_high = jnp.where(slab < SLABS - 1, 1.0, 0.0)
    fix_ref[0] = FAR * cols[0] * has_low
    fix_ref[1] = (NEAR * cols[0] + FAR * cols[1]) * has_low
    fix_ref[2] = (FAR * cols[2] + NEAR * cols[3]) * has_high
    fix_ref[3] = FAR * cols[3] * has_high


def green_kernel(rate_ref, green_ref, wide_ref, coef_ref):
    lane8 = lax.broadcasted_iota(jnp.int32, (8, 128), 1)
    sub8 = lax.broadcasted_iota(jnp.int32, (8, 128), 0)
    wide_ref[...] = 1.0 / rate_ref[...] + MAIN
    zero = jnp.zeros((8, 128), F32)
    recip, low1, low2 = ldl(lambda k: jnp.broadcast_to(wide_ref[k : k + 1, :], (8, 128)), zero)
    units = [(sub8 == ENDS.index(k)).astype(F32) if k in ENDS else zero for k in range(ROWS)]
    full = substitute(units, recip, low1, low2)

    def entry(k, i):
        return jnp.broadcast_to(full[k][i : i + 1, :], (8, 128))

    not_first = ((lane8 > 0) & (lane8 < SLABS)).astype(F32)
    not_last = (lane8 < SLABS - 1).astype(F32)

    def lower(k):
        s0, s1 = entry(k, 0), entry(k, 1)
        return (FAR * s0 * not_first, (NEAR * s0 + FAR * s1) * not_first)

    def upper(k):
        s2, s3 = entry(k, 2), entry(k, 3)
        return ((FAR * s2 + NEAR * s3) * not_last, FAR * s3 * not_last)

    low_a = (lower(ENDS[0]), lower(ENDS[1]))
    low_c = (lower(ENDS[2]), lower(ENDS[3]))
    up_b = (upper(ENDS[0]), upper(ENDS[1]))
    up_e = (upper(ENDS[2]), upper(ENDS[3]))
    a, b, c, e = low_a, up_b, low_c, up_e
    for hop in (1, 2, 4, 8, 16):
        ax, bx, cx, ex = (each(m, lambda v: pltpu.roll(v, hop, 1)) for m in (a, b, c, e))
        w = inverse_of_one_minus(mm(a, ex))
        wa_c = mm(w, mm(a, cx))
        wb = mm(w, b)
        cy_ex = mm(c, ex)
        new_e = add(e, mm(cy_ex, wb))
        new_c = neg(add(mm(c, cx), mm(cy_ex, wa_c)))
        new_a = add(ax, mm(bx, wa_c))
        new_b = neg(mm(bx, wb))
        joined = lane8 >= hop

        def pick(new, old):
            return tuple(
                tuple(jnp.where(joined, new[i][j], old[i][j]) for j in range(2)) for i in range(2)
            )

        a, b, c, e = pick(new_a, a), pick(new_b, b), pick(new_c, c), pick(new_e, e)
    q = e
    q_prev = each(q, lambda v: jnp.where(lane8 > 0, pltpu.roll(v, 1, 1), 0.0))
    z = inverse_of_one_minus(mm(low_a, q_prev))
    gain = mm(mm(low_c, q_prev), z)
    carry = add(low_c, mm(gain, low_a))
    z_low = mm(z, low_a)
    z_up = mm(z, up_b)
    for group, mats in enumerate(((carry, gain), (z, z_low), (z_up, q))):
        block = jnp.zeros((8, 128), F32)
        for n, m in enumerate(mats):
            for i in range(2):
                for j in range(2):
                    block = jnp.where(sub8 == 4 * n + 2 * i + j, m[i][j], block)
        for s in range(SLABS):
            coef_ref[s, 8 * group : 8 * group + 8, :] = jnp.broadcast_to(block[:, s : s + 1], (8, 128))

    def coef(s, n):
        def one(i, j):
            at = 4 * n + 2 * i + j
            return jnp.broadcast_to(coef_ref[s, at : at + 1, :], (8, 128))

        return tuple(tuple(one(i, j) for j in range(2)) for i in range(2))

    def at_lane(n):
        return lane8 == n

    forward = []
    prev = None
    for s in range(SLABS):
        m, g = coef(s, 0), coef(s, 1)
        now = []
        for i in range(2):
            value = jnp.where(at_lane(4 * s), g[i][0], 0.0)
            value = jnp.where(at_lane(4 * s + 1), g[i][1], value)
            value = jnp.where(at_lane(4 * s + 2 + i), 1.0, value)
            if prev is not None:
                value = value - m[i][0] * prev[0] - m[i][1] * prev[1]
            now.append(value)
        forward.append(now)
        prev = now
    for row in (0, 1, 4 * SLABS - 2, 4 * SLABS - 1):
        green_ref[row : row + 1, :] = jnp.zeros((1, 128), F32)
    after = None
    for s in reversed(range(SLABS)):
        zc, zl, zu, qc = coef(s, 2), coef(s, 3), coef(s, 4), coef(s, 5)
        now = []
        for i in range(2):
            value = jnp.where(at_lane(4 * s), zc[i][0], 0.0)
            value = jnp.where(at_lane(4 * s + 1), zc[i][1], value)
            if s > 0:
                value = value - zl[i][0] * forward[s - 1][0] - zl[i][1] * forward[s - 1][1]
            if after is not None:
                value = value - zu[i][0] * after[0] - zu[i][1] * after[1]
            now.append(value)
        if s < SLABS - 1:
            for i in range(2):
                high = forward[s][i] - qc[i][0] * after[0] - qc[i][1] * after[1]
                green_ref[4 * (s + 1) + i : 4 * (s + 1) + i + 1, :] = high[0:1]
        if s > 0:
            for i in range(2):
                green_ref[4 * (s - 1) + 2 + i : 4 * (s - 1) + 3 + i, :] = now[i][0:1]
        after = now


def green_operator(rate):
    return pl.pallas_call(
        green_kernel,
        out_shape=shaped(128, 128),
        in_specs=[VMEM],
        out_specs=VMEM,
        scratch_shapes=[pltpu.VMEM((ROWS, 128), F32), pltpu.VMEM((SLABS, 24, 128), F32)],
        compiler_params=params(4),
        name="green_operator",
    )(rate)


def pre_kernel(
    place_ref, vel_hbm, part_hbm, rate_hbm, high_hbm, low_hbm, inner_hbm, outer_hbm,
    packed_hbm, bf_ref, vel_ref, part_ref, rate_ref, out_ref, sems,
):
    even = place_ref[0] % 2 == 0
    order = (2, 3, 0, 1)
    into = [
        pltpu.make_async_copy(part_hbm, part_ref, sems.at[0]),
        pltpu.make_async_copy(rate_hbm, rate_ref, sems.at[1]),
    ]
    layers = [
        pltpu.make_async_copy(vel_hbm.at[:, x], vel_ref.at[:, x], sems.at[2 + x]) for x in order
    ]
    for copy in into + layers:
        copy.start()
    for copy in into:
        copy.wait()
    left = lax.broadcasted_iota(jnp.int32, (1, 128), 1) < SLOTS

    def pack(first, last):
        for r in range(first, last):
            part = [part_ref[i : i + 1, 128 * r : 128 * r + 128] for i in range(3)]
            part.append(rate_ref[0:1, 128 * r : 128 * r + 128])
            for n in range(2):
                one, two = part[2 * n], part[2 * n + 1]
                out_ref[2 * r, n : n + 1, :] = jnp.where(left, one, pltpu.roll(two, SLOTS, 1))
                out_ref[2 * r + 1, n : n + 1, :] = jnp.where(left, pltpu.roll(one, SLOTS, 1), two)

    out = []
    for n, x in enumerate(order):
        pack(16 * n, 16 * n + 16)
        layers[n].wait()
        target = high_hbm.at[:, x - 2] if x >= 2 else low_hbm.at[:, x]
        flat = pltpu.make_async_copy(vel_ref.at[:, x], target, sems.at[7 + n])
        flat.start()
        out.append(flat)
        bottom, top = vel_ref.at[:, x, 0:2], vel_ref.at[:, x, ROWS - 2 : ROWS]
        out.append(pltpu.make_async_copy(top, inner_hbm.at[:, x], sems.at[11 + n]))
        out.append(pltpu.make_async_copy(bottom, outer_hbm.at[:, x], sems.at[15 + n]))

        @pl.when(even)
        def _():
            out[-2].start()
            out[-1].start()

        @pl.when(jnp.logical_not(even))
        def _():
            pltpu.make_async_copy(bottom, inner_hbm.at[:, x], sems.at[11 + n]).start()
            pltpu.make_async_copy(top, outer_hbm.at[:, x], sems.at[15 + n]).start()

    out.append(pltpu.make_async_copy(out_ref, packed_hbm, sems.at[19]))
    out[-1].start()
    for c in range(3):
        for x in range(CX):
            span = c * PLANES + x * ROWS
            bf_ref[span : span + ROWS, :] = vel_ref[c, x].astype(BF16)
    for copy in out:
        copy.wait()


def prepared(place, velocity, part_vel, part_rate):
    return pl.pallas_call(
        pre_kernel,
        out_shape=(
            far_out(3, 2, ROWS, CZ),
            far_out(3, 2, ROWS, CZ),
            far_out(3, CX, 2, CZ),
            far_out(3, CX, 2, CZ),
            far_out(PEERS, 2, 128),
            held((3 * PLANES, CZ), BF16),
        ),
        in_specs=[SMEM] + [ANY] * 3,
        out_specs=(ANY,) * 5 + (VMEM,),
        scratch_shapes=[
            pltpu.VMEM((3, CX, ROWS, CZ), F32),
            pltpu.VMEM((3, TOTAL), F32),
            pltpu.VMEM((1, TOTAL), F32),
            pltpu.VMEM((PEERS, 2, 128), F32),
            pltpu.SemaphoreType.DMA((20,)),
        ],
        compiler_params=params(16),
        name="prepare",
    )(place, *far_in(velocity, part_vel, part_rate))


def halves(cells):
    plane = cells >> 10
    span = cells & (CZ - 1)
    return plane, span >> 7, span & 127


def span_table(high, low):
    width = high.shape[1]
    inner = lax.broadcasted_iota(jnp.int32, (128, width), 0) == low
    inner = inner.astype(F32).astype(BF16)
    rows = []
    for t in range(8):
        flag = (high == t).astype(F32).astype(BF16)
        rows.append(inner * flag)
    return jnp.concatenate(rows, axis=0)


def column_of(row, length):
    wide = jnp.broadcast_to(row, (length, length))
    here = lax.broadcasted_iota(jnp.int32, (length, length), 0) == lax.broadcasted_iota(
        jnp.int32, (length, length), 1
    )
    return jnp.broadcast_to(
        jnp.sum(jnp.where(here, wide, 0.0), axis=1, keepdims=True), (length, 128)
    )


def find_kernel(
    place_ref, bf_ref, cell_hbm, rate_hbm, *refs,
):
    outs, held_refs = refs[:5], refs[5:10]
    fluid_ref, scale_ref, tip_ref, fix_ref, solve_ref = held_refs
    table_ref, cell_ref, rate_ref, wide_ref, sems = refs[10:]
    copies = [
        pltpu.make_async_copy(cell_hbm, cell_ref, sems.at[0]),
        pltpu.make_async_copy(rate_hbm, rate_ref, sems.at[1]),
    ]
    for copy in copies:
        copy.start()
    for copy in copies:
        copy.wait()
    own_factors(place_ref[0], rate_ref, scale_ref, tip_ref, fix_ref, solve_ref, wide_ref)
    stores = [
        pltpu.make_async_copy(held_refs[n], outs[n], sems.at[1 + n]) for n in range(1, 5)
    ]
    for store in stores:
        store.start()
    for step in range(TOTAL // CHUNK):
        lanes = slice(step * CHUNK, (step + 1) * CHUNK)
        plane, high, low = halves(cell_ref[:, lanes])
        table_ref[...] = span_table(high, low)
        at = jnp.dot(bf_ref[...], table_ref[...], preferred_element_type=F32)
        mask = lax.broadcasted_iota(jnp.int32, (PLANES, CHUNK), 0) == plane
        for n in range(3):
            fluid_ref[n : n + 1, lanes] = jnp.sum(
                jnp.where(mask, at[n * PLANES : (n + 1) * PLANES], 0.0), axis=0, keepdims=True
            )
        stores.append(
            pltpu.make_async_copy(
                fluid_ref.at[:, lanes], outs[0].at[:, lanes], sems.at[6 + step]
            )
        )
        stores[-1].start()
    for store in stores:
        store.wait()


def find(place, vel_held, cells, rate):
    return pl.pallas_call(
        find_kernel,
        out_shape=(
            far_out(3, TOTAL),
            far_out(ROWS, 128),
            far_out(4, ROWS, 128),
            far_out(4, ROWS, 128),
            far_out(ROWS, 128),
        ),
        in_specs=[SMEM, VMEM, ANY, ANY],
        out_specs=(ANY,) * 5,
        scratch_shapes=[
            pltpu.VMEM((3, TOTAL), F32),
            pltpu.VMEM((ROWS, 128), F32),
            pltpu.VMEM((4, ROWS, 128), F32),
            pltpu.VMEM((4, ROWS, 128), F32),
            pltpu.VMEM((ROWS, 128), F32),
            pltpu.VMEM((CZ, CHUNK), BF16),
            pltpu.VMEM((1, TOTAL), jnp.int32),
            pltpu.VMEM((8, 128), F32),
            pltpu.VMEM((ROWS, 128), F32),
            pltpu.SemaphoreType.DMA((6 + TOTAL // CHUNK,)),
        ],
        compiler_params=params(28),
        name="find",
    )(place, vel_held, *far_in(cells, rate))


def main_kernel(
    place_ref, inner_hbm, outer_hbm, before_hbm, behind_hbm, moved_hbm,
    fluid_hbm, scale_hbm, tip_hbm, vel_hbm, section_hbm, count_hbm, cell_hbm, near_hbm, far_hbm,
    part_hbm, tips_hbm, new_ref,
    pad_ref, before_ref, behind_ref, section_ref, table_ref, got_ref, deposit_ref, moved_ref,
    count_ref, cell_ref, near_ref, far_ref, part_ref, tips_ref, coef_ref,
    fluid_ref, scale_ref, tip_ref, sems,
):
    sources = [
        (cell_hbm, cell_ref),
        (moved_hbm, moved_ref),
        (count_hbm, count_ref),
        (fluid_hbm, fluid_ref),
        (scale_hbm, scale_ref),
        (tip_hbm, tip_ref),
        (near_hbm, near_ref),
        (far_hbm, far_ref),
        (vel_hbm, pad_ref.at[:, :, 8 : 8 + ROWS, :]),
        (inner_hbm, pad_ref.at[:, :, 6:8, :]),
        (outer_hbm, pad_ref.at[:, :, 8 + ROWS : 10 + ROWS, :]),
        (before_hbm, before_ref),
        (behind_hbm, behind_ref),
        (section_hbm, section_ref),
    ]
    copies = [pltpu.make_async_copy(a, b, sems.at[n]) for n, (a, b) in enumerate(sources)]
    swaps = [n for n, (a, b) in enumerate(sources) if a is inner_hbm or a is outer_hbm]
    for n, copy in enumerate(copies):
        if n not in swaps:
            copy.start()
    even = place_ref[0] % 2 == 0

    @pl.when(even)
    def _():
        for n, source in zip(swaps, (outer_hbm, inner_hbm)):
            pltpu.make_async_copy(source, sources[n][1], sems.at[n]).start()

    @pl.when(jnp.logical_not(even))
    def _():
        for n in swaps:
            copies[n].start()

    steps = TOTAL // CHUNK

    def lanes_of(step):
        return slice(step * CHUNK, (step + 1) * CHUNK)

    def spread_of(step):
        lanes = lanes_of(step)
        plane, high, low = halves(cell_ref[:, lanes])
        table_ref[...] = span_table(high, low)
        mask = lax.broadcasted_iota(jnp.int32, (PLANES, CHUNK), 0) == plane
        mask = mask.astype(F32).astype(BF16)
        live = got_ref[4:5, lanes] > 0.5
        rate = got_ref[3:4, lanes]
        spread = []
        for n in range(3):
            old = got_ref[n : n + 1, lanes]
            relative = fluid_ref[n : n + 1, lanes] - old
            part_ref[n : n + 1, lanes] = jnp.where(live, old + TIME_STEP * rate * relative, 0.0)
            push = jnp.where(live, -rate * relative, 0.0).astype(BF16)
            spread.append(mask * push)
        return jnp.concatenate(spread, axis=0)

    def unpack():
        left = lax.broadcasted_iota(jnp.int32, (1, 128), 1) < SLOTS
        lane = lax.broadcasted_iota(jnp.int32, (1, 128), 1)
        for r in range(PEERS // 2):
            lanes = slice(128 * r, 128 * r + 128)
            for n in range(2):
                one = moved_ref[2 * r, n : n + 1, :]
                two = moved_ref[2 * r + 1, n : n + 1, :]
                got_ref[2 * n : 2 * n + 1, lanes] = jnp.where(left, one, pltpu.roll(two, SLOTS, 1))
                got_ref[2 * n + 1 : 2 * n + 2, lanes] = jnp.where(
                    left, pltpu.roll(one, SLOTS, 1), two
                )
            limit = jnp.where(left, count_ref[0, 2 * r], count_ref[0, 2 * r + 1])
            got_ref[4:5, lanes] = ((lane & (SLOTS - 1)) < limit).astype(F32)

    def tiled(column, times):
        return jnp.concatenate([column] * times, axis=1)

    def stencil(c, x):
        def layer(i, top):
            if i < 0:
                return before_ref[c, 2 + i, top : top + 8, :]
            if i >= CX:
                return behind_ref[c, i - CX, top : top + 8, :]
            return pad_ref[c, i, 8 + top : 16 + top, :]

        for t in range(ROWS // 8):
            top = 8 * t
            here = layer(x, top)
            ddx = (8.0 / 12.0) * (layer(x + 1, top) - layer(x - 1, top)) - (1.0 / 12.0) * (
                layer(x + 2, top) - layer(x - 2, top)
            )
            rolled = {k: pltpu.roll(here, (-k) % CZ, 1) for k in (1, -1, 2, -2)}
            ddz = (8.0 / 12.0) * (rolled[1] - rolled[-1]) - (1.0 / 12.0) * (rolled[2] - rolled[-2])

            def shifted(k):
                return pad_ref[c, x, 8 + top + k : 16 + top + k, :]

            near = tiled(coef_ref[0, top : top + 8, :], 8)
            far = tiled(coef_ref[1, top : top + 8, :], 8)
            ddy = near * (shifted(1) - shifted(-1)) + far * (shifted(2) - shifted(-2))
            moved = (
                pad_ref[0, x, 8 + top : 16 + top, :] * ddx
                + pad_ref[1, x, 8 + top : 16 + top, :] * ddy
                + pad_ref[2, x, 8 + top : 16 + top, :] * ddz
            )
            new_ref[c, x, top : top + 8, :] = (
                SECTION_KEEP * section_ref[c, x, top : top + 8, :] - TIME_STEP * moved
            )

    planes = [(c, x) for c in range(3) for x in range(CX)]
    share = len(planes) // (steps - 1)
    for copy in copies[:4]:
        copy.wait()
    unpack()
    for step in range(steps):
        spread = spread_of(step)
        if step > 0:
            for c, x in planes[share * (step - 1) : share * step]:
                stencil(c, x)
        last = step == steps - 1
        if last:
            stores = [pltpu.make_async_copy(part_ref, part_hbm, sems.at[14])]
            stores[0].start()
        wide = CZ // 4 if last else CZ
        for z in range(0, CZ, wide):
            new = lax.dot_general(
                spread, table_ref[z : z + wide, :], (((1,), (1,)), ((), ())),
                preferred_element_type=F32,
            )
            if step == 0:
                deposit_ref[...] = new
                continue
            if not last:
                deposit_ref[...] += new
                continue
            for c, x in planes:
                base = c * PLANES + x * ROWS
                total = [None] * 4
                for t in range(ROWS // 8):
                    top = 8 * t
                    full = new_ref[c, x, top : top + 8, z : z + wide] + TIME_STEP * (
                        deposit_ref[base + top : base + top + 8, z : z + wide]
                        + new[base + top : base + top + 8]
                    )
                    new_ref[c, x, top : top + 8, z : z + wide] = full
                    scaled = full * tiled(scale_ref[top : top + 8, :], wide // 128)
                    for r in range(4):
                        weighted = scaled * tiled(tip_ref[r, top : top + 8, :], wide // 128)
                        total[r] = weighted if t == 0 else total[r] + weighted
                for r in range(4):
                    summed = jnp.sum(total[r], axis=0, keepdims=True)
                    for k in range(wide // 128):
                        tips_ref[8 * x + z // 128 + k, c, r : r + 1, :] = summed[
                            :, 128 * k : 128 * k + 128
                        ]
            for x in range(CX if last else 0):
                span = pl.ds(8 * x + z // 128, wide // 128)
                stores.append(
                    pltpu.make_async_copy(
                        tips_ref.at[span], tips_hbm.at[span], sems.at[14 + len(stores)]
                    )
                )
                stores[-1].start()
        if step == 0:
            for copy in copies[4:]:
                copy.wait()
            coef_ref[0] = column_of(near_ref[...], ROWS)
            coef_ref[1] = column_of(far_ref[...], ROWS)
    for store in stores:
        store.wait()


def main_part(place, halos, moved, others):
    return pl.pallas_call(
        main_kernel,
        out_shape=(
            far_out(3, TOTAL),
            far_out(SLABS, 3, 4, 128),
            held((3, CX, ROWS, CZ)),
        ),
        in_specs=[SMEM] + [ANY] * 14,
        out_specs=(ANY, ANY, VMEM),
        scratch_shapes=[
            pltpu.VMEM((3, CX, ROWS + 16, CZ), F32),
            pltpu.VMEM((3, 2, ROWS, CZ), F32),
            pltpu.VMEM((3, 2, ROWS, CZ), F32),
            pltpu.VMEM((3, CX, ROWS, CZ), F32),
            pltpu.VMEM((CZ, CHUNK), BF16),
            pltpu.VMEM((8, TOTAL), F32),
            pltpu.VMEM((3 * PLANES, CZ), F32),
            pltpu.VMEM((PEERS, 2, 128), F32),
            pltpu.SMEM((1, PEERS), jnp.int32),
            pltpu.VMEM((1, TOTAL), jnp.int32),
            pltpu.VMEM((1, ROWS), F32),
            pltpu.VMEM((1, ROWS), F32),
            pltpu.VMEM((3, TOTAL), F32),
            pltpu.VMEM((SLABS, 3, 4, 128), F32),
            pltpu.VMEM((2, ROWS, 128), F32),
            pltpu.VMEM((3, TOTAL), F32),
            pltpu.VMEM((ROWS, 128), F32),
            pltpu.VMEM((4, ROWS, 128), F32),
            pltpu.SemaphoreType.DMA((31,)),
        ],
        compiler_params=params(36),
        name="main_part",
    )(place, *halos, moved, *far_in(*others))


WIDTH = 3 * CX * CZ // SLABS


def solve_kernel(tips_ref, green_ref, out_ref, all_ref):
    for s in range(SLABS):
        for c in range(3):
            all_ref[4 * s : 4 * s + 4, 128 * c : 128 * c + 128] = tips_ref[s, c]
    found = jnp.dot(green_ref[...], all_ref[...], precision=HIGH, preferred_element_type=F32)
    for s in range(SLABS):
        for c in range(3):
            out_ref[s, c] = found[4 * s : 4 * s + 4, 128 * c : 128 * c + 128]


def solved(tips, green):
    return pl.pallas_call(
        solve_kernel,
        out_shape=shaped(SLABS, 3, 4, 128),
        in_specs=[VMEM, VMEM],
        out_specs=VMEM,
        scratch_shapes=[pltpu.VMEM((4 * SLABS, WIDTH), F32)],
        compiler_params=params(4),
        name="solve",
    )(tips, green)


def local_kernel(vel_hbm, section_ref, scale_ref, solve_ref, section_hbm, out_ref, sems):
    loads = [pltpu.make_async_copy(vel_hbm.at[c], out_ref.at[c], sems.at[c]) for c in range(3)]
    for load in loads:
        load.start()
    store = pltpu.make_async_copy(section_ref, section_hbm, sems.at[3])
    store.start()
    whole = solve_ref[:, 0:ROWS]
    head = whole.astype(BF16)
    rest = (whole - head.astype(F32)).astype(BF16)
    left = jnp.concatenate([head, rest, head], axis=1)
    scale = jnp.concatenate([scale_ref[...]] * 8, axis=1)
    for c in range(3):
        loads[c].wait()
        for x in range(CX):
            value = section_ref[c, x] * scale
            high = value.astype(BF16)
            low = (value - high.astype(F32)).astype(BF16)
            right = jnp.concatenate([high, high, low], axis=0)
            out_ref[c, x] += jnp.dot(left, right, preferred_element_type=F32)
    store.wait()


def local_solve(velocity, section_new, scale, solve):
    return pl.pallas_call(
        local_kernel,
        out_shape=(far_out(3, CX, ROWS, CZ), held((3, CX, ROWS, CZ))),
        in_specs=[ANY, VMEM, VMEM, VMEM],
        out_specs=(ANY, VMEM),
        scratch_shapes=[pltpu.SemaphoreType.DMA((4,))],
        compiler_params=params(16),
        name="local_solve",
    )(*far_in(velocity), section_new, scale, solve)


def final_kernel(partial_ref, edge_ref, fix_ref, out_hbm, out_ref, sems):
    stores = []
    for c in range(3):
        for x in range(CX):
            for t in range(CZ // 128):
                lanes = slice(128 * t, 128 * t + 128)
                edge = edge_ref[8 * x + t, c]
                value = partial_ref[c, x, :, lanes]
                for r in range(4):
                    value = value - fix_ref[r] * edge[r : r + 1, :]
                out_ref[c, x, :, lanes] = value
            if x % 2 == 1:
                span = pl.ds(x - 1, 2)
                stores.append(
                    pltpu.make_async_copy(
                        out_ref.at[c, span], out_hbm.at[c, span], sems.at[len(stores)]
                    )
                )
                stores[-1].start()
    for copy in stores:
        copy.wait()


def finished(partial, edges, fix):
    return pl.pallas_call(
        final_kernel,
        out_shape=far_out(3, CX, ROWS, CZ),
        in_specs=[VMEM] * 3,
        out_specs=ANY,
        scratch_shapes=[pltpu.VMEM((3, CX, ROWS, CZ), F32), pltpu.SemaphoreType.DMA((6,))],
        compiler_params=params(16),
        name="finish",
    )(partial, edges, fix)


def local(velocity, section, diffusion, rhs_near, rhs_far, part_vel, part_rate, counts, cell_slot):
    n_gx, n_gy = lax.axis_size("gx"), lax.axis_size("gy")
    up_x = [(i, (i + 1) % n_gx) for i in range(n_gx)]
    down_x = [(t, s) for s, t in up_x]
    place = lax.axis_index("gy").astype(jnp.int32).reshape(1)
    high, low, inner, outer, packed, vel_held = prepared(
        place, velocity, part_vel, part_rate.reshape(1, TOTAL)
    )
    before = lax.ppermute(high, "gx", up_x)
    behind = lax.ppermute(low, "gx", down_x)
    inner = lax.ppermute(inner, "gy", [(i, i ^ 1) for i in range(n_gy)])
    outer = lax.ppermute(
        outer, "gy", [pair for i in range(1, n_gy - 1, 2) for pair in ((i, i + 1), (i + 1, i))]
    )
    moved = lax.all_to_all(packed, ("gx", "gy"), split_axis=0, concat_axis=0, tiled=True)
    fluid, scale, tip, fix, solve = find(place, vel_held, cell_slot, diffusion.reshape(8, 128))
    part_new, tips, new_held = main_part(
        place, (inner, outer, before, behind), moved,
        (fluid, scale, tip, velocity, section, counts, cell_slot, rhs_near.reshape(1, ROWS), rhs_far.reshape(1, ROWS)),
    )
    tips, diffusion = lax.optimization_barrier((tips, diffusion))
    all_tips = lax.all_to_all(tips, "gy", split_axis=0, concat_axis=0, tiled=True)
    rate = jnp.pad(
        diffusion.reshape(SLABS, ROWS).T, ((0, 0), (0, 128 - SLABS)), constant_values=1000.0
    )
    reply = solved(all_tips, green_operator(rate))
    reply, solve = lax.optimization_barrier((reply, solve))
    edges = lax.all_to_all(reply, "gy", split_axis=0, concat_axis=0, tiled=True)
    section_new, partial = local_solve(velocity, new_held, scale, solve)
    velocity_new = finished(partial, edges, fix)
    return (velocity_new, section_new, part_new)


def solution(mesh):
    return jax.shard_map(
        local,
        mesh=mesh,
        in_specs=(
            P(None, "gx", "gy", None),
            P(None, "gx", "gy", None),
            P(),
            P("gy"),
            P("gy"),
            P(None, ("gx", "gy")),
            P(("gx", "gy")),
            P(("gx", "gy"), None),
            P(("gx", "gy"), None),
        ),
        out_specs=(P(None, "gx", "gy", None), P(None, "gx", "gy", None), P(None, ("gx", "gy"))),
        check_vma=False,
    )
```

```python
import jax
import jax.numpy as jnp
from jax import lax
from jax.experimental import pallas as pl
from jax.experimental.pallas import tpu as pltpu
from jax.sharding import PartitionSpec as P

TIME_STEP = 0.2
SECTION_KEEP = -5.0 / 9.0
SECTION_GAIN = 15.0 / 16.0
MAIN = 2.5
NEAR = -4.0 / 3.0
FAR = 1.0 / 12.0
SLABS = 32
ROWS = 32
CX = 4
CZ = 1024
PLANES = CX * ROWS
SLOTS = 64
PEERS = 128
TOTAL = PEERS * SLOTS
CHUNK = 2048
HIGH = lax.Precision.HIGHEST
F32 = jnp.float32
BF16 = jnp.bfloat16


def params(mib=60):
    return pltpu.CompilerParams(vmem_limit_bytes=mib * 1024 * 1024)


VMEM = pl.BlockSpec(memory_space=pltpu.MemorySpace.VMEM)
SMEM = pl.BlockSpec(memory_space=pltpu.MemorySpace.SMEM)
ANY = pl.BlockSpec(memory_space=pltpu.MemorySpace.HBM)


def held(shape, dtype=F32):
    return pltpu.MemorySpace.VMEM(shape, dtype)


def shaped(*shape):
    return jax.ShapeDtypeStruct(shape, F32)


def far_out(*shape):
    return pltpu.MemorySpace.HBM(shape, F32)


def far_in(*arrays):
    return [pltpu.with_memory_space_constraint(a, pltpu.MemorySpace.HBM) for a in arrays]


def mm(a, b):
    return tuple(
        tuple(a[i][0] * b[0][j] + a[i][1] * b[1][j] for j in range(2)) for i in range(2)
    )


def add(a, b, sign=1.0):
    return tuple(tuple(a[i][j] + sign * b[i][j] for j in range(2)) for i in range(2))


def neg(a):
    return tuple(tuple(-e for e in row) for row in a)


def each(a, fn):
    return tuple(tuple(fn(e) for e in row) for row in a)


def inverse_of_one_minus(a):
    p, q, r, s = 1.0 - a[0][0], -a[0][1], -a[1][0], 1.0 - a[1][1]
    scale = 1.0 / (p * s - q * r)
    return ((s * scale, -q * scale), (-r * scale, p * scale))


def ldl(main_of, zero):
    recip, low1, low2 = [], [], []
    for k in range(ROWS):
        main = main_of(k)
        if k == 0:
            low1.append(zero)
            low2.append(zero)
            recip.append(1.0 / main)
            continue
        edge = NEAR - FAR * low1[k - 1]
        one = edge * recip[k - 1]
        two = FAR * recip[k - 2] if k > 1 else zero
        low1.append(one)
        low2.append(two)
        recip.append(1.0 / (main - edge * one - FAR * two))
    return recip, low1, low2


def substitute(rows, recip, low1, low2):
    half = []
    for k in range(ROWS):
        value = rows[k]
        if k > 0:
            value = value - low1[k] * half[k - 1]
        if k > 1:
            value = value - low2[k] * half[k - 2]
        half.append(value)
    full = [None] * ROWS
    for k in reversed(range(ROWS)):
        value = half[k] * recip[k]
        if k < ROWS - 1:
            value = value - low1[k + 1] * full[k + 1]
        if k < ROWS - 2:
            value = value - low2[k + 2] * full[k + 2]
        full[k] = value
    return full


ENDS = (0, 1, ROWS - 2, ROWS - 1)


def own_factors(slab, rate_ref, scale_ref, tip_ref, fix_ref, solve_ref, wide_ref):
    lane8 = lax.broadcasted_iota(jnp.int32, (8, 128), 1)
    row = rate_ref[pl.ds(slab // 4, 1), :]
    row = pltpu.roll(jnp.broadcast_to(row, (8, 128)), 128 - ROWS * (slab % 4), 1)
    inv_rate = 1.0 / column_of(row[0:1, 0:ROWS], ROWS)
    scale_ref[...] = SECTION_GAIN * inv_rate
    wide_ref[...] = inv_rate + MAIN
    recip, low1, low2 = ldl(
        lambda k: jnp.broadcast_to(wide_ref[k : k + 1, :], (8, 128)), jnp.zeros((8, 128), F32)
    )
    full = substitute([(lane8 == k).astype(F32) for k in range(ROWS)], recip, low1, low2)
    for k in range(ROWS):
        solve_ref[k : k + 1, :] = full[k][0:1]
    solve = solve_ref[...]
    cols = [jnp.broadcast_to(solve[:, n : n + 1], (ROWS, 128)) for n in ENDS]
    for n in range(4):
        tip_ref[n] = cols[n]
    has_low = jnp.where(slab > 0, 1.0, 0.0)
    has_high = jnp.where(slab < SLABS - 1, 1.0, 0.0)
    fix_ref[0] = FAR * cols[0] * has_low
    fix_ref[1] = (NEAR * cols[0] + FAR * cols[1]) * has_low
    fix_ref[2] = (FAR * cols[2] + NEAR * cols[3]) * has_high
    fix_ref[3] = FAR * cols[3] * has_high


def green_kernel(rate_ref, green_ref, wide_ref, coef_ref):
    lane8 = lax.broadcasted_iota(jnp.int32, (8, 128), 1)
    sub8 = lax.broadcasted_iota(jnp.int32, (8, 128), 0)
    wide_ref[...] = 1.0 / rate_ref[...] + MAIN
    zero = jnp.zeros((8, 128), F32)
    recip, low1, low2 = ldl(lambda k: jnp.broadcast_to(wide_ref[k : k + 1, :], (8, 128)), zero)
    units = [(sub8 == ENDS.index(k)).astype(F32) if k in ENDS else zero for k in range(ROWS)]
    full = substitute(units, recip, low1, low2)

    def entry(k, i):
        return jnp.broadcast_to(full[k][i : i + 1, :], (8, 128))

    not_first = ((lane8 > 0) & (lane8 < SLABS)).astype(F32)
    not_last = (lane8 < SLABS - 1).astype(F32)

    def lower(k):
        s0, s1 = entry(k, 0), entry(k, 1)
        return (FAR * s0 * not_first, (NEAR * s0 + FAR * s1) * not_first)

    def upper(k):
        s2, s3 = entry(k, 2), entry(k, 3)
        return ((FAR * s2 + NEAR * s3) * not_last, FAR * s3 * not_last)

    low_a = (lower(ENDS[0]), lower(ENDS[1]))
    low_c = (lower(ENDS[2]), lower(ENDS[3]))
    up_b = (upper(ENDS[0]), upper(ENDS[1]))
    up_e = (upper(ENDS[2]), upper(ENDS[3]))
    a, b, c, e = low_a, up_b, low_c, up_e
    for hop in (1, 2, 4, 8, 16):
        ax, bx, cx, ex = (each(m, lambda v: pltpu.roll(v, hop, 1)) for m in (a, b, c, e))
        w = inverse_of_one_minus(mm(a, ex))
        wa_c = mm(w, mm(a, cx))
        wb = mm(w, b)
        cy_ex = mm(c, ex)
        new_e = add(e, mm(cy_ex, wb))
        new_c = neg(add(mm(c, cx), mm(cy_ex, wa_c)))
        new_a = add(ax, mm(bx, wa_c))
        new_b = neg(mm(bx, wb))
        joined = lane8 >= hop

        def pick(new, old):
            return tuple(
                tuple(jnp.where(joined, new[i][j], old[i][j]) for j in range(2)) for i in range(2)
            )

        a, b, c, e = pick(new_a, a), pick(new_b, b), pick(new_c, c), pick(new_e, e)
    q = e
    q_prev = each(q, lambda v: jnp.where(lane8 > 0, pltpu.roll(v, 1, 1), 0.0))
    z = inverse_of_one_minus(mm(low_a, q_prev))
    gain = mm(mm(low_c, q_prev), z)
    carry = add(low_c, mm(gain, low_a))
    z_low = mm(z, low_a)
    z_up = mm(z, up_b)
    for group, mats in enumerate(((carry, gain), (z, z_low), (z_up, q))):
        block = jnp.zeros((8, 128), F32)
        for n, m in enumerate(mats):
            for i in range(2):
                for j in range(2):
                    block = jnp.where(sub8 == 4 * n + 2 * i + j, m[i][j], block)
        for s in range(SLABS):
            coef_ref[s, 8 * group : 8 * group + 8, :] = jnp.broadcast_to(block[:, s : s + 1], (8, 128))

    def coef(s, n):
        def one(i, j):
            at = 4 * n + 2 * i + j
            return jnp.broadcast_to(coef_ref[s, at : at + 1, :], (8, 128))

        return tuple(tuple(one(i, j) for j in range(2)) for i in range(2))

    def at_lane(n):
        return lane8 == n

    forward = []
    prev = None
    for s in range(SLABS):
        m, g = coef(s, 0), coef(s, 1)
        now = []
        for i in range(2):
            value = jnp.where(at_lane(4 * s), g[i][0], 0.0)
            value = jnp.where(at_lane(4 * s + 1), g[i][1], value)
            value = jnp.where(at_lane(4 * s + 2 + i), 1.0, value)
            if prev is not None:
                value = value - m[i][0] * prev[0] - m[i][1] * prev[1]
            now.append(value)
        forward.append(now)
        prev = now
    for row in (0, 1, 4 * SLABS - 2, 4 * SLABS - 1):
        green_ref[row : row + 1, :] = jnp.zeros((1, 128), F32)
    after = None
    for s in reversed(range(SLABS)):
        zc, zl, zu, qc = coef(s, 2), coef(s, 3), coef(s, 4), coef(s, 5)
        now = []
        for i in range(2):
            value = jnp.where(at_lane(4 * s), zc[i][0], 0.0)
            value = jnp.where(at_lane(4 * s + 1), zc[i][1], value)
            if s > 0:
                value = value - zl[i][0] * forward[s - 1][0] - zl[i][1] * forward[s - 1][1]
            if after is not None:
                value = value - zu[i][0] * after[0] - zu[i][1] * after[1]
            now.append(value)
        if s < SLABS - 1:
            for i in range(2):
                high = forward[s][i] - qc[i][0] * after[0] - qc[i][1] * after[1]
                green_ref[4 * (s + 1) + i : 4 * (s + 1) + i + 1, :] = high[0:1]
        if s > 0:
            for i in range(2):
                green_ref[4 * (s - 1) + 2 + i : 4 * (s - 1) + 3 + i, :] = now[i][0:1]
        after = now


def green_operator(rate):
    return pl.pallas_call(
        green_kernel,
        out_shape=shaped(128, 128),
        in_specs=[VMEM],
        out_specs=VMEM,
        scratch_shapes=[pltpu.VMEM((ROWS, 128), F32), pltpu.VMEM((SLABS, 24, 128), F32)],
        compiler_params=params(4),
        name="green_operator",
    )(rate)


def pre_kernel(
    place_ref, vel_hbm, part_hbm, rate_hbm, high_hbm, low_hbm, inner_hbm, outer_hbm,
    packed_hbm, bf_ref, vel_ref, part_ref, rate_ref, out_ref, sems,
):
    even = place_ref[0] % 2 == 0
    order = (2, 3, 0, 1)
    into = [
        pltpu.make_async_copy(part_hbm, part_ref, sems.at[0]),
        pltpu.make_async_copy(rate_hbm, rate_ref, sems.at[1]),
    ]
    layers = [
        pltpu.make_async_copy(vel_hbm.at[:, x], vel_ref.at[:, x], sems.at[2 + x]) for x in order
    ]
    for copy in into + layers:
        copy.start()
    for copy in into:
        copy.wait()
    left = lax.broadcasted_iota(jnp.int32, (1, 128), 1) < SLOTS

    def pack(first, last):
        for r in range(first, last):
            part = [part_ref[i : i + 1, 128 * r : 128 * r + 128] for i in range(3)]
            part.append(rate_ref[0:1, 128 * r : 128 * r + 128])
            for n in range(2):
                one, two = part[2 * n], part[2 * n + 1]
                out_ref[2 * r, n : n + 1, :] = jnp.where(left, one, pltpu.roll(two, SLOTS, 1))
                out_ref[2 * r + 1, n : n + 1, :] = jnp.where(left, pltpu.roll(one, SLOTS, 1), two)

    out = []
    for n, x in enumerate(order):
        pack(16 * n, 16 * n + 16)
        layers[n].wait()
        target = high_hbm.at[:, x - 2] if x >= 2 else low_hbm.at[:, x]
        flat = pltpu.make_async_copy(vel_ref.at[:, x], target, sems.at[7 + n])
        flat.start()
        out.append(flat)
        bottom, top = vel_ref.at[:, x, 0:2], vel_ref.at[:, x, ROWS - 2 : ROWS]
        out.append(pltpu.make_async_copy(top, inner_hbm.at[:, x], sems.at[11 + n]))
        out.append(pltpu.make_async_copy(bottom, outer_hbm.at[:, x], sems.at[15 + n]))

        @pl.when(even)
        def _():
            out[-2].start()
            out[-1].start()

        @pl.when(jnp.logical_not(even))
        def _():
            pltpu.make_async_copy(bottom, inner_hbm.at[:, x], sems.at[11 + n]).start()
            pltpu.make_async_copy(top, outer_hbm.at[:, x], sems.at[15 + n]).start()

    out.append(pltpu.make_async_copy(out_ref, packed_hbm, sems.at[19]))
    out[-1].start()
    for c in range(3):
        for x in range(CX):
            span = c * PLANES + x * ROWS
            bf_ref[span : span + ROWS, :] = vel_ref[c, x].astype(BF16)
    for copy in out:
        copy.wait()


def prepared(place, velocity, part_vel, part_rate):
    return pl.pallas_call(
        pre_kernel,
        out_shape=(
            far_out(3, 2, ROWS, CZ),
            far_out(3, 2, ROWS, CZ),
            far_out(3, CX, 2, CZ),
            far_out(3, CX, 2, CZ),
            far_out(PEERS, 2, 128),
            held((3 * PLANES, CZ), BF16),
        ),
        in_specs=[SMEM] + [ANY] * 3,
        out_specs=(ANY,) * 5 + (VMEM,),
        scratch_shapes=[
            pltpu.VMEM((3, CX, ROWS, CZ), F32),
            pltpu.VMEM((3, TOTAL), F32),
            pltpu.VMEM((1, TOTAL), F32),
            pltpu.VMEM((PEERS, 2, 128), F32),
            pltpu.SemaphoreType.DMA((20,)),
        ],
        compiler_params=params(16),
        name="prepare",
    )(place, *far_in(velocity, part_vel, part_rate))


def halves(cells):
    plane = cells >> 10
    span = cells & (CZ - 1)
    return plane, span >> 7, span & 127


def span_table(high, low):
    width = high.shape[1]
    inner = lax.broadcasted_iota(jnp.int32, (128, width), 0) == low
    inner = inner.astype(F32).astype(BF16)
    rows = []
    for t in range(8):
        flag = (high == t).astype(F32).astype(BF16)
        rows.append(inner * flag)
    return jnp.concatenate(rows, axis=0)


def column_of(row, length):
    wide = jnp.broadcast_to(row, (length, length))
    here = lax.broadcasted_iota(jnp.int32, (length, length), 0) == lax.broadcasted_iota(
        jnp.int32, (length, length), 1
    )
    return jnp.broadcast_to(
        jnp.sum(jnp.where(here, wide, 0.0), axis=1, keepdims=True), (length, 128)
    )


def find_kernel(
    place_ref, bf_ref, cell_hbm, rate_hbm, *refs,
):
    outs, held_refs = refs[:5], refs[5:10]
    fluid_ref, scale_ref, tip_ref, fix_ref, solve_ref = held_refs
    table_ref, cell_ref, rate_ref, wide_ref, sems = refs[10:]
    copies = [
        pltpu.make_async_copy(cell_hbm, cell_ref, sems.at[0]),
        pltpu.make_async_copy(rate_hbm, rate_ref, sems.at[1]),
    ]
    for copy in copies:
        copy.start()
    copies[1].wait()
    own_factors(place_ref[0], rate_ref, scale_ref, tip_ref, fix_ref, solve_ref, wide_ref)
    stores = [
        pltpu.make_async_copy(held_refs[n], outs[n], sems.at[1 + n]) for n in range(1, 5)
    ]
    for store in stores:
        store.start()
    copies[0].wait()
    for step in range(TOTAL // CHUNK):
        lanes = slice(step * CHUNK, (step + 1) * CHUNK)
        plane, high, low = halves(cell_ref[:, lanes])
        table_ref[step % 2] = span_table(high, low)
        at = jnp.dot(bf_ref[...], table_ref[step % 2], preferred_element_type=F32)
        mask = lax.broadcasted_iota(jnp.int32, (PLANES, CHUNK), 0) == plane
        for n in range(3):
            fluid_ref[n : n + 1, lanes] = jnp.sum(
                jnp.where(mask, at[n * PLANES : (n + 1) * PLANES], 0.0), axis=0, keepdims=True
            )
        stores.append(
            pltpu.make_async_copy(
                fluid_ref.at[:, lanes], outs[0].at[:, lanes], sems.at[6 + step]
            )
        )
        stores[-1].start()
    for store in stores:
        store.wait()


def find(place, vel_held, cells, rate):
    return pl.pallas_call(
        find_kernel,
        out_shape=(
            far_out(3, TOTAL),
            far_out(ROWS, 128),
            far_out(4, ROWS, 128),
            far_out(4, ROWS, 128),
            far_out(ROWS, 128),
        ),
        in_specs=[SMEM, VMEM, ANY, ANY],
        out_specs=(ANY,) * 5,
        scratch_shapes=[
            pltpu.VMEM((3, TOTAL), F32),
            pltpu.VMEM((ROWS, 128), F32),
            pltpu.VMEM((4, ROWS, 128), F32),
            pltpu.VMEM((4, ROWS, 128), F32),
            pltpu.VMEM((ROWS, 128), F32),
            pltpu.VMEM((2, CZ, CHUNK), BF16),
            pltpu.VMEM((1, TOTAL), jnp.int32),
            pltpu.VMEM((8, 128), F32),
            pltpu.VMEM((ROWS, 128), F32),
            pltpu.SemaphoreType.DMA((6 + TOTAL // CHUNK,)),
        ],
        compiler_params=params(28),
        name="find",
    )(place, vel_held, *far_in(cells, rate))


def main_kernel(
    place_ref, inner_hbm, outer_hbm, before_hbm, behind_hbm, moved_hbm,
    fluid_hbm, scale_hbm, tip_hbm, vel_hbm, section_hbm, count_hbm, cell_hbm, near_hbm, far_hbm,
    part_hbm, tips_hbm, new_ref,
    pad_ref, before_ref, behind_ref, section_ref, table_ref, got_ref, deposit_ref, moved_ref,
    count_ref, cell_ref, near_ref, far_ref, part_ref, tips_ref, coef_ref,
    fluid_ref, scale_ref, tip_ref, sems,
):
    sources = [
        (cell_hbm, cell_ref),
        (moved_hbm, moved_ref),
        (count_hbm, count_ref),
        (fluid_hbm, fluid_ref),
        (scale_hbm, scale_ref),
        (tip_hbm, tip_ref),
        (near_hbm, near_ref),
        (far_hbm, far_ref),
        (vel_hbm, pad_ref.at[:, :, 8 : 8 + ROWS, :]),
        (inner_hbm, pad_ref.at[:, :, 6:8, :]),
        (outer_hbm, pad_ref.at[:, :, 8 + ROWS : 10 + ROWS, :]),
        (before_hbm, before_ref),
        (behind_hbm, behind_ref),
        (section_hbm, section_ref),
    ]
    copies = [pltpu.make_async_copy(a, b, sems.at[n]) for n, (a, b) in enumerate(sources)]
    swaps = [n for n, (a, b) in enumerate(sources) if a is inner_hbm or a is outer_hbm]
    for n, copy in enumerate(copies):
        if n not in swaps:
            copy.start()
    even = place_ref[0] % 2 == 0

    @pl.when(even)
    def _():
        for n, source in zip(swaps, (outer_hbm, inner_hbm)):
            pltpu.make_async_copy(source, sources[n][1], sems.at[n]).start()

    @pl.when(jnp.logical_not(even))
    def _():
        for n in swaps:
            copies[n].start()

    steps = TOTAL // CHUNK

    def lanes_of(step):
        return slice(step * CHUNK, (step + 1) * CHUNK)

    def spread_of(step):
        lanes = lanes_of(step)
        plane, high, low = halves(cell_ref[:, lanes])
        table_ref[step % 2] = span_table(high, low)
        mask = lax.broadcasted_iota(jnp.int32, (PLANES, CHUNK), 0) == plane
        mask = mask.astype(F32).astype(BF16)
        live = got_ref[4:5, lanes] > 0.5
        rate = got_ref[3:4, lanes]
        spread = []
        for n in range(3):
            old = got_ref[n : n + 1, lanes]
            relative = fluid_ref[n : n + 1, lanes] - old
            part_ref[n : n + 1, lanes] = jnp.where(live, old + TIME_STEP * rate * relative, 0.0)
            push = jnp.where(live, -rate * relative, 0.0).astype(BF16)
            spread.append(mask * push)
        return jnp.concatenate(spread, axis=0)

    def unpack():
        left = lax.broadcasted_iota(jnp.int32, (1, 128), 1) < SLOTS
        lane = lax.broadcasted_iota(jnp.int32, (1, 128), 1)
        for r in range(PEERS // 2):
            lanes = slice(128 * r, 128 * r + 128)
            for n in range(2):
                one = moved_ref[2 * r, n : n + 1, :]
                two = moved_ref[2 * r + 1, n : n + 1, :]
                got_ref[2 * n : 2 * n + 1, lanes] = jnp.where(left, one, pltpu.roll(two, SLOTS, 1))
                got_ref[2 * n + 1 : 2 * n + 2, lanes] = jnp.where(
                    left, pltpu.roll(one, SLOTS, 1), two
                )
            limit = jnp.where(left, count_ref[0, 2 * r], count_ref[0, 2 * r + 1])
            got_ref[4:5, lanes] = ((lane & (SLOTS - 1)) < limit).astype(F32)

    def tiled(column, times):
        return jnp.concatenate([column] * times, axis=1)

    def stencil(c, x):
        def layer(i, top):
            if i < 0:
                return before_ref[c, 2 + i, top : top + 8, :]
            if i >= CX:
                return behind_ref[c, i - CX, top : top + 8, :]
            return pad_ref[c, i, 8 + top : 16 + top, :]

        for t in range(ROWS // 8):
            top = 8 * t
            here = layer(x, top)
            ddx = (8.0 / 12.0) * (layer(x + 1, top) - layer(x - 1, top)) - (1.0 / 12.0) * (
                layer(x + 2, top) - layer(x - 2, top)
            )
            rolled = {k: pltpu.roll(here, (-k) % CZ, 1) for k in (1, -1, 2, -2)}
            ddz = (8.0 / 12.0) * (rolled[1] - rolled[-1]) - (1.0 / 12.0) * (rolled[2] - rolled[-2])

            def shifted(k):
                return pad_ref[c, x, 8 + top + k : 16 + top + k, :]

            near = tiled(coef_ref[0, top : top + 8, :], 8)
            far = tiled(coef_ref[1, top : top + 8, :], 8)
            ddy = near * (shifted(1) - shifted(-1)) + far * (shifted(2) - shifted(-2))
            moved = (
                pad_ref[0, x, 8 + top : 16 + top, :] * ddx
                + pad_ref[1, x, 8 + top : 16 + top, :] * ddy
                + pad_ref[2, x, 8 + top : 16 + top, :] * ddz
            )
            new_ref[c, x, top : top + 8, :] = (
                SECTION_KEEP * section_ref[c, x, top : top + 8, :] - TIME_STEP * moved
            )

    planes = [(c, x) for c in range(3) for x in range(CX)]
    share = len(planes) // (steps - 1)
    for copy in copies[:4]:
        copy.wait()
    unpack()
    for step in range(steps):
        spread = spread_of(step)
        if step > 0:
            for c, x in planes[share * (step - 1) : share * step]:
                stencil(c, x)
        last = step == steps - 1
        if last:
            stores = [pltpu.make_async_copy(part_ref, part_hbm, sems.at[14])]
            stores[0].start()
        wide = CZ // 4 if last else CZ
        for z in range(0, CZ, wide):
            new = lax.dot_general(
                spread, table_ref[step % 2, z : z + wide, :], (((1,), (1,)), ((), ())),
                preferred_element_type=F32,
            )
            if step == 0:
                deposit_ref[...] = new
                continue
            if not last:
                deposit_ref[...] += new
                continue
            for c, x in planes:
                base = c * PLANES + x * ROWS
                total = [None] * 4
                for t in range(ROWS // 8):
                    top = 8 * t
                    full = new_ref[c, x, top : top + 8, z : z + wide] + TIME_STEP * (
                        deposit_ref[base + top : base + top + 8, z : z + wide]
                        + new[base + top : base + top + 8]
                    )
                    new_ref[c, x, top : top + 8, z : z + wide] = full
                    scaled = full * tiled(scale_ref[top : top + 8, :], wide // 128)
                    for r in range(4):
                        weighted = scaled * tiled(tip_ref[r, top : top + 8, :], wide // 128)
                        total[r] = weighted if t == 0 else total[r] + weighted
                for r in range(4):
                    summed = jnp.sum(total[r], axis=0, keepdims=True)
                    for k in range(wide // 128):
                        tips_ref[8 * x + z // 128 + k, c, r : r + 1, :] = summed[
                            :, 128 * k : 128 * k + 128
                        ]
            for x in range(CX if last else 0):
                span = pl.ds(8 * x + z // 128, wide // 128)
                stores.append(
                    pltpu.make_async_copy(
                        tips_ref.at[span], tips_hbm.at[span], sems.at[14 + len(stores)]
                    )
                )
                stores[-1].start()
        if step == 0:
            for copy in copies[4:]:
                copy.wait()
            coef_ref[0] = column_of(near_ref[...], ROWS)
            coef_ref[1] = column_of(far_ref[...], ROWS)
    for store in stores:
        store.wait()


def main_part(place, halos, moved, others):
    return pl.pallas_call(
        main_kernel,
        out_shape=(
            far_out(3, TOTAL),
            far_out(SLABS, 3, 4, 128),
            held((3, CX, ROWS, CZ)),
        ),
        in_specs=[SMEM] + [ANY] * 14,
        out_specs=(ANY, ANY, VMEM),
        scratch_shapes=[
            pltpu.VMEM((3, CX, ROWS + 16, CZ), F32),
            pltpu.VMEM((3, 2, ROWS, CZ), F32),
            pltpu.VMEM((3, 2, ROWS, CZ), F32),
            pltpu.VMEM((3, CX, ROWS, CZ), F32),
            pltpu.VMEM((2, CZ, CHUNK), BF16),
            pltpu.VMEM((8, TOTAL), F32),
            pltpu.VMEM((3 * PLANES, CZ), F32),
            pltpu.VMEM((PEERS, 2, 128), F32),
            pltpu.SMEM((1, PEERS), jnp.int32),
            pltpu.VMEM((1, TOTAL), jnp.int32),
            pltpu.VMEM((1, ROWS), F32),
            pltpu.VMEM((1, ROWS), F32),
            pltpu.VMEM((3, TOTAL), F32),
            pltpu.VMEM((SLABS, 3, 4, 128), F32),
            pltpu.VMEM((2, ROWS, 128), F32),
            pltpu.VMEM((3, TOTAL), F32),
            pltpu.VMEM((ROWS, 128), F32),
            pltpu.VMEM((4, ROWS, 128), F32),
            pltpu.SemaphoreType.DMA((31,)),
        ],
        compiler_params=params(36),
        name="main_part",
    )(place, *halos, moved, *far_in(*others))


WIDTH = 3 * CX * CZ // SLABS


def solve_kernel(tips_ref, green_ref, out_ref, all_ref):
    for s in range(SLABS):
        for c in range(3):
            all_ref[4 * s : 4 * s + 4, 128 * c : 128 * c + 128] = tips_ref[s, c]
    found = jnp.dot(green_ref[...], all_ref[...], precision=HIGH, preferred_element_type=F32)
    for s in range(SLABS):
        for c in range(3):
            out_ref[s, c] = found[4 * s : 4 * s + 4, 128 * c : 128 * c + 128]


def solved(tips, green):
    return pl.pallas_call(
        solve_kernel,
        out_shape=shaped(SLABS, 3, 4, 128),
        in_specs=[VMEM, VMEM],
        out_specs=VMEM,
        scratch_shapes=[pltpu.VMEM((4 * SLABS, WIDTH), F32)],
        compiler_params=params(4),
        name="solve",
    )(tips, green)


def local_kernel(vel_hbm, section_ref, scale_ref, solve_ref, section_hbm, out_ref, sems):
    loads = [pltpu.make_async_copy(vel_hbm.at[c], out_ref.at[c], sems.at[c]) for c in range(3)]
    for load in loads:
        load.start()
    store = pltpu.make_async_copy(section_ref, section_hbm, sems.at[3])
    store.start()
    whole = solve_ref[:, 0:ROWS]
    head = whole.astype(BF16)
    rest = (whole - head.astype(F32)).astype(BF16)
    left = jnp.concatenate([head, rest, head], axis=1)
    scale = jnp.concatenate([scale_ref[...]] * 8, axis=1)
    for c in range(3):
        loads[c].wait()
        for x in range(CX):
            value = section_ref[c, x] * scale
            high = value.astype(BF16)
            low = (value - high.astype(F32)).astype(BF16)
            right = jnp.concatenate([high, high, low], axis=0)
            out_ref[c, x] += jnp.dot(left, right, preferred_element_type=F32)
    store.wait()


def local_solve(velocity, section_new, scale, solve):
    return pl.pallas_call(
        local_kernel,
        out_shape=(far_out(3, CX, ROWS, CZ), held((3, CX, ROWS, CZ))),
        in_specs=[ANY, VMEM, VMEM, VMEM],
        out_specs=(ANY, VMEM),
        scratch_shapes=[pltpu.SemaphoreType.DMA((4,))],
        compiler_params=params(16),
        name="local_solve",
    )(*far_in(velocity), section_new, scale, solve)


def final_kernel(partial_ref, edge_ref, fix_ref, out_hbm, out_ref, sems):
    stores = []
    for c in range(3):
        for x in range(CX):
            for t in range(CZ // 128):
                lanes = slice(128 * t, 128 * t + 128)
                edge = edge_ref[8 * x + t, c]
                value = partial_ref[c, x, :, lanes]
                for r in range(4):
                    value = value - fix_ref[r] * edge[r : r + 1, :]
                out_ref[c, x, :, lanes] = value
            if x % 2 == 1:
                span = pl.ds(x - 1, 2)
                stores.append(
                    pltpu.make_async_copy(
                        out_ref.at[c, span], out_hbm.at[c, span], sems.at[len(stores)]
                    )
                )
                stores[-1].start()
    for copy in stores:
        copy.wait()


def finished(partial, edges, fix):
    return pl.pallas_call(
        final_kernel,
        out_shape=far_out(3, CX, ROWS, CZ),
        in_specs=[VMEM] * 3,
        out_specs=ANY,
        scratch_shapes=[pltpu.VMEM((3, CX, ROWS, CZ), F32), pltpu.SemaphoreType.DMA((6,))],
        compiler_params=params(16),
        name="finish",
    )(partial, edges, fix)


def local(velocity, section, diffusion, rhs_near, rhs_far, part_vel, part_rate, counts, cell_slot):
    n_gx, n_gy = lax.axis_size("gx"), lax.axis_size("gy")
    up_x = [(i, (i + 1) % n_gx) for i in range(n_gx)]
    down_x = [(t, s) for s, t in up_x]
    place = lax.axis_index("gy").astype(jnp.int32).reshape(1)
    high, low, inner, outer, packed, vel_held = prepared(
        place, velocity, part_vel, part_rate.reshape(1, TOTAL)
    )
    before = lax.ppermute(high, "gx", up_x)
    behind = lax.ppermute(low, "gx", down_x)
    inner = lax.ppermute(inner, "gy", [(i, i ^ 1) for i in range(n_gy)])
    outer = lax.ppermute(
        outer, "gy", [pair for i in range(1, n_gy - 1, 2) for pair in ((i, i + 1), (i + 1, i))]
    )
    moved = lax.all_to_all(packed, ("gx", "gy"), split_axis=0, concat_axis=0, tiled=True)
    fluid, scale, tip, fix, solve = find(place, vel_held, cell_slot, diffusion.reshape(8, 128))
    part_new, tips, new_held = main_part(
        place, (inner, outer, before, behind), moved,
        (fluid, scale, tip, velocity, section, counts, cell_slot, rhs_near.reshape(1, ROWS), rhs_far.reshape(1, ROWS)),
    )
    tips, diffusion = lax.optimization_barrier((tips, diffusion))
    all_tips = lax.all_to_all(tips, "gy", split_axis=0, concat_axis=0, tiled=True)
    rate = jnp.pad(
        diffusion.reshape(SLABS, ROWS).T, ((0, 0), (0, 128 - SLABS)), constant_values=1000.0
    )
    reply = solved(all_tips, green_operator(rate))
    reply, solve = lax.optimization_barrier((reply, solve))
    edges = lax.all_to_all(reply, "gy", split_axis=0, concat_axis=0, tiled=True)
    section_new, partial = local_solve(velocity, new_held, scale, solve)
    velocity_new = finished(partial, edges, fix)
    return (velocity_new, section_new, part_new)


def solution(mesh):
    return jax.shard_map(
        local,
        mesh=mesh,
        in_specs=(
            P(None, "gx", "gy", None),
            P(None, "gx", "gy", None),
            P(),
            P("gy"),
            P("gy"),
            P(None, ("gx", "gy")),
            P(("gx", "gy")),
            P(("gx", "gy"), None),
            P(("gx", "gy"), None),
        ),
        out_specs=(P(None, "gx", "gy", None), P(None, "gx", "gy", None), P(None, ("gx", "gy"))),
        check_vma=False,
    )
```
